32 devices in a mesh: freq: 4 (over y, core), tcol: 8 (over z, x).
Axes of the slice: x: 2, y: 2, z: 4, core: 2. Of those that a mesh axis runs over, the one named last changes fastest.
Arguments:
- data: bfloat16 [4, 2, 4096, 128], P('freq', None, 'tcol'), may hold values from -6 to 6
- left_factor: bfloat16 [4, 2, 4096, 256], P('freq', None, 'tcol'), may hold values from -0.25 to 0.25
- right_factor: bfloat16 [4, 2, 4096, 256], P('freq', None, 'tcol'), may hold values from -0.1875 to 0.1875
- ranks: int32 [4, 8, 8], P('freq'), may hold values from 1 to 32
- freq_index: int32 [4], P('freq'), may hold values from 0 to 229
Outputs:
- wavefield: float32 [4, 2, 4096, 128], P('freq', None, 'tcol')
- residual: float32 [4, 2, 4096, 128], P('freq', None, 'tcol')
The draws below stay inside these ranges and needn't reach their ends.
Inputs may be any that keep to these rules, and one draw needn't show every extreme that they name: `ranks`: the rank of each tile; factor columns at or beyond it are not part of the kernel.
All inputs are finite; a program needn't handle non-finite values.
Results may differ from the reference program's by a relative error of at most 0.006.
Values may be sent and summed in bfloat16 or wider, within the bound.
No kernel may reach another device: no remote copies, remote signals or barrier semaphores. Data moves between devices by JAX's collectives and lax.ppermute only.
A program may use at most 64 MiB of HBM per device.

```python
import jax
import jax.numpy as jnp

TILE = 512
RANK = 32
SOURCES = 128
ITERS = 3
NTILES = 8
ORDER = 4096
FREQS = 4


def with_ends(drawn, key, low, top_value):
    place = [jax.random.randint(jax.random.fold_in(key, axis), (), 0, length) for axis, length in enumerate(drawn.shape)]
    main_axis = drawn.shape.index(max(drawn.shape))
    beside = place[:main_axis] + [(place[main_axis] + 1) % drawn.shape[main_axis]] + place[main_axis + 1:]
    return drawn.at[tuple(place)].set(low).at[tuple(beside)].set(top_value)


def block_scale(key, dims, cuts, least, largest):
    def one(position, parts):
        draws = jax.random.uniform(jax.random.fold_in(jax.random.fold_in(key, 6), position), (parts,), jnp.float32, least / len(cuts), largest / len(cuts))
        return jnp.repeat(jnp.exp(draws), dims[position] // parts).reshape((-1,) + (1,) * (len(dims) - position - 1))

    gain = one(*cuts[0])
    for cut in cuts[1:]:
        gain = gain * one(*cut)
    return gain


def gaussian(own_key, dims, spread, most, cuts=(), kind=jnp.bfloat16):
    result = jax.random.normal(own_key, dims, jnp.float32) * spread
    if len(cuts) > 0:
        result = block_scale(own_key, dims, cuts, -0.22, 0.18) * result
    return jnp.clip(result, min=-most, max=most).astype(kind)


def setup_inputs(seed: int = 0) -> dict:
    key_of = jax.random.split(jax.random.key(seed), 6)
    data = gaussian(key_of[0], (FREQS, 2, ORDER, SOURCES), 1.0, 6.0, ((0, 4), (2, 8)))
    left_factor = gaussian(key_of[1], (FREQS, 2, ORDER, NTILES * RANK), (2 * RANK * NTILES) ** -0.5, 0.25, ((0, 4), (2, 8)))
    right_factor = gaussian(key_of[2], (FREQS, 2, ORDER, NTILES * RANK), (2 * TILE) ** -0.5, 0.1875, ((0, 4), (2, 8)))
    ranks = with_ends(jax.random.randint(key_of[3], (FREQS, NTILES, NTILES), 1, RANK + 1), jax.random.fold_in(key_of[3], 1), 1, RANK).astype(jnp.int32)
    freq_index = with_ends(jax.random.randint(key_of[4], (FREQS,), 0, 230), jax.random.fold_in(key_of[4], 1), 0, 229).astype(jnp.int32)
    return {"data": data, "left_factor": left_factor, "right_factor": right_factor, "ranks": ranks, "freq_index": freq_index}


def tile_masks(ranks):
    return (jnp.arange(RANK)[None, None, None, :] < ranks[..., None]).astype(jnp.float32)


def apply_forward(left, right, field, masks):
    nfreq = field.shape[0]
    ntile = NTILES
    g = field.astype(jnp.bfloat16).astype(jnp.float32).reshape(nfreq, 2, ntile, TILE, field.shape[3])
    v = right.astype(jnp.float32).reshape(nfreq, 2, ntile, TILE, ntile * RANK)
    real = jnp.einsum('fjbq,fjbs->fjqs', v[:, 0], g[:, 0]) + jnp.einsum('fjbq,fjbs->fjqs', v[:, 1], g[:, 1])
    imag = jnp.einsum('fjbq,fjbs->fjqs', v[:, 0], g[:, 1]) - jnp.einsum('fjbq,fjbs->fjqs', v[:, 1], g[:, 0])
    colmask = jnp.transpose(masks, (0, 2, 1, 3)).reshape(nfreq, ntile, ntile * RANK)
    coeff = jnp.stack([real, imag], 1) * colmask[:, None, :, :, None]
    coeff = coeff.astype(jnp.bfloat16).astype(jnp.float32)
    coeff = coeff.reshape(nfreq, 2, ntile, ntile, RANK, -1)
    coeff = jnp.transpose(coeff, (0, 1, 3, 2, 4, 5)).reshape(nfreq, 2, ntile, ntile * RANK, -1)
    u = left.astype(jnp.float32).reshape(nfreq, 2, ntile, TILE, ntile * RANK)
    wreal = jnp.einsum('fiaq,fiqs->fias', u[:, 0], coeff[:, 0]) - jnp.einsum('fiaq,fiqs->fias', u[:, 1], coeff[:, 1])
    wimag = jnp.einsum('fiaq,fiqs->fias', u[:, 0], coeff[:, 1]) + jnp.einsum('fiaq,fiqs->fias', u[:, 1], coeff[:, 0])
    return jnp.stack([wreal, wimag], 1).reshape(field.shape)


def apply_adjoint(left, right, field, masks):
    nfreq = field.shape[0]
    ntile = NTILES
    r = field.astype(jnp.bfloat16).astype(jnp.float32).reshape(nfreq, 2, ntile, TILE, field.shape[3])
    u = left.astype(jnp.float32).reshape(nfreq, 2, ntile, TILE, ntile * RANK)
    real = jnp.einsum('fiaq,fias->fiqs', u[:, 0], r[:, 0]) + jnp.einsum('fiaq,fias->fiqs', u[:, 1], r[:, 1])
    imag = jnp.einsum('fiaq,fias->fiqs', u[:, 0], r[:, 1]) - jnp.einsum('fiaq,fias->fiqs', u[:, 1], r[:, 0])
    rowmask = masks.reshape(nfreq, ntile, ntile * RANK)
    back = jnp.stack([real, imag], 1) * rowmask[:, None, :, :, None]
    back = back.astype(jnp.bfloat16).astype(jnp.float32)
    back = back.reshape(nfreq, 2, ntile, ntile, RANK, -1)
    back = jnp.transpose(back, (0, 1, 3, 2, 4, 5)).reshape(nfreq, 2, ntile, ntile * RANK, -1)
    v = right.astype(jnp.float32).reshape(nfreq, 2, ntile, TILE, ntile * RANK)
    greal = jnp.einsum('fjbq,fjqs->fjbs', v[:, 0], back[:, 0]) - jnp.einsum('fjbq,fjqs->fjbs', v[:, 1], back[:, 1])
    gimag = jnp.einsum('fjbq,fjqs->fjbs', v[:, 0], back[:, 1]) + jnp.einsum('fjbq,fjqs->fjbs', v[:, 1], back[:, 0])
    return jnp.stack([greal, gimag], 1).reshape(field.shape)


def reference(data, left_factor, right_factor, ranks, freq_index):
    masks = tile_masks(ranks)
    damping = (0.1 + 0.9 * freq_index.astype(jnp.float32) / 229.0)[:, None, None, None]
    residual = data.astype(jnp.float32)
    wavefield = jnp.zeros_like(residual)
    direction = jnp.zeros_like(residual)
    image = jnp.zeros_like(residual)
    for step in range(ITERS):
        gradient = apply_adjoint(left_factor, right_factor, residual, masks) - damping * wavefield
        moved = apply_forward(left_factor, right_factor, gradient, masks)
        a11 = jnp.sum(moved * moved + damping * gradient * gradient, axis=(0, 1, 2))
        b1 = jnp.sum(moved * residual - damping * gradient * wavefield, axis=(0, 1, 2))
        if step == 0:
            alpha = b1 / (1.1 * a11)
            beta = jnp.zeros_like(alpha)
        else:
            a12 = jnp.sum(moved * image + damping * gradient * direction, axis=(0, 1, 2))
            a22 = jnp.sum(image * image + damping * direction * direction, axis=(0, 1, 2))
            b2 = jnp.sum(image * residual - damping * direction * wavefield, axis=(0, 1, 2))
            first = 1.1 * a11
            second = 1.1 * a22
            determinant = first * second - a12 * a12
            alpha = (b1 * second - a12 * b2) / determinant
            beta = (first * b2 - a12 * b1) / determinant
        direction = alpha * gradient + beta * direction
        image = alpha * moved + beta * image
        wavefield = wavefield + direction
        residual = residual - image
    return wavefield, residual
```

```python
import functools

import jax
import jax.numpy as jnp
from jax import lax
from jax.experimental import pallas as pl
from jax.experimental.pallas import tpu as pltpu
from jax.sharding import PartitionSpec as P


RIDE = 16
ROWS = 16
VMEM = pl.BlockSpec(memory_space=pltpu.VMEM)
SMEM = pl.BlockSpec(memory_space=pltpu.SMEM)
F32 = jnp.float32
BF16 = jnp.bfloat16


def dot(a, b):
    return jnp.dot(a, b, preferred_element_type=F32)


def dot_t(a, b):
    return lax.dot_general(a, b, (((0,), (0,)), ((), ())), preferred_element_type=F32)


def side(real, imag):
    return jnp.concatenate([real, imag], axis=1)


def split(value):
    high = value.astype(BF16)
    return high, (value - high.astype(F32)).astype(BF16)


def unpack(ref, rank):
    n = ref.shape[0]
    real = ref[:, 0:rank, :].reshape(n * rank, ref.shape[2])
    imag = ref[:, rank : 2 * rank, :].reshape(n * rank, ref.shape[2])
    return real, imag


def send(out_ref, value, limits, rank):
    s = out_ref.shape[2]
    level = lax.broadcasted_iota(jnp.int32, (rank, s), 0)
    for p in range(out_ref.shape[0]):
        keep = level < limits[p]
        rows = value[p * rank : (p + 1) * rank]
        out_ref[p, 0:rank, :] = jnp.where(keep, rows[:, :s], 0.0).astype(BF16)
        out_ref[p, rank : 2 * rank, :] = jnp.where(keep, rows[:, s:], 0.0).astype(BF16)


def ride(out_ref, first, second, rank):
    s = out_ref.shape[2]
    row = lax.broadcasted_iota(jnp.int32, (RIDE, s), 0)
    block = jnp.where(row == 0, first, second).astype(BF16)
    for p in range(out_ref.shape[0]):
        out_ref[p, 2 * rank : 2 * rank + RIDE, :] = block


def ridden(ref, rank):
    total = ref[0, 2 * rank : 2 * rank + RIDE, :].astype(F32)
    for p in range(1, ref.shape[0]):
        total = total + ref[p, 2 * rank : 2 * rank + RIDE, :].astype(F32)
    return total[0:1], total[1:2]


def inner(a, b):
    both = jnp.sum(a * b, axis=0, keepdims=True)
    s = both.shape[1] // 2
    return both[:, :s] + both[:, s:]


def twice(row):
    return jnp.concatenate([row, row], axis=1)


def ratio(top, bottom):
    safe = bottom > 0
    return jnp.where(safe, top / jnp.where(safe, bottom, 1.0), 0.0)


def apply_gram(hi_ref, lo_ref, real, imag):
    vector = jnp.concatenate([side(real, imag), side(-imag, real)], axis=0)
    return dot(hi_ref[...], vector) + dot(lo_ref[...], vector)


def row_limits(ranks_ref, here, n):
    return [ranks_ref[here, p] for p in range(n)]


def column_limits(ranks_ref, here, n):
    return [ranks_ref[p, here] for p in range(n)]


def start_kernel(rank, here_ref, ranks_ref, data_ref, factor_ref, back_ref, out_ref):
    n = out_ref.shape[0]
    real, imag = data_ref[0], data_ref[1]
    back = dot_t(factor_ref[0], side(real, imag)) + dot_t(factor_ref[1], side(imag, -real))
    back_ref[...] = back
    send(out_ref, back, row_limits(ranks_ref, here_ref[0], n), rank)


def gram_kernel(factor_ref, hi_ref, lo_ref):
    real, imag = factor_ref[0], factor_ref[1]
    width = real.shape[1]
    high, low = split(dot_t(real, real) + dot_t(imag, imag))
    hi_ref[:, :width] = high
    lo_ref[:, :width] = low
    high, low = split(dot_t(real, imag) - dot_t(imag, real))
    hi_ref[:, width:] = high
    lo_ref[:, width:] = low


def column0(rank, here_ref, ranks_ref, b0_ref, hi_ref, lo_ref, g0_ref, sums_ref, out_ref):
    n = out_ref.shape[0]
    real, imag = unpack(b0_ref, rank)
    g0 = apply_gram(hi_ref, lo_ref, real, imag)
    g0_ref[...] = g0
    m00 = inner(side(real, imag).astype(F32), g0)
    sums_ref[0:1, :] = m00
    send(out_ref, g0, column_limits(ranks_ref, here_ref[0], n), rank)
    ride(out_ref, m00, m00, rank)


def row0(rank, here_ref, ranks_ref, c0_ref, hi_ref, lo_ref, back_ref, sums_ref, out_ref):
    n = out_ref.shape[0]
    real, imag = unpack(c0_ref, rank)
    next0 = apply_gram(hi_ref, lo_ref, real, imag)
    c0 = side(real, imag).astype(F32)
    n00 = inner(c0, next0)
    sums_ref[0:1, :] = n00
    sums_ref[1:2, :] = inner(back_ref[...], c0)
    sums_ref[2:3, :] = ridden(c0_ref, rank)[0]
    send(out_ref, next0, row_limits(ranks_ref, here_ref[0], n), rank)
    ride(out_ref, n00, n00, rank)


def column1(
    rank, here_ref, ranks_ref, b1_ref, b0_ref, hi_ref, lo_ref, g0_ref, known_ref,
    g1_ref, b1s_ref, sums_ref, out_ref
):
    n = out_ref.shape[0]
    real, imag = unpack(b1_ref, rank)
    theta0 = ratio(ridden(b1_ref, rank)[0], known_ref[2:3, :])
    wide = twice(theta0)
    g1 = apply_gram(hi_ref, lo_ref, real, imag) - wide * g0_ref[...]
    b0 = side(*unpack(b0_ref, rank)).astype(F32)
    b1 = side(real, imag).astype(F32) - wide * b0
    g1_ref[...] = g1
    b1s_ref[...] = b1
    m11 = inner(b1, g1)
    sums_ref[0:1, :] = m11
    sums_ref[1:2, :] = inner(b0, g1)
    sums_ref[2:3, :] = theta0
    send(out_ref, g1, column_limits(ranks_ref, here_ref[0], n), rank)
    ride(out_ref, m11, m11, rank)


def row1(
    rank, here_ref, ranks_ref, c1_ref, c0_ref, hi_ref, lo_ref, back_ref, sums_ref, out_ref
):
    n = out_ref.shape[0]
    real, imag = unpack(c1_ref, rank)
    next1 = apply_gram(hi_ref, lo_ref, real, imag)
    c1 = side(real, imag).astype(F32)
    c0 = side(*unpack(c0_ref, rank)).astype(F32)
    n11 = inner(c1, next1)
    n01 = inner(c0, next1)
    sums_ref[0:1, :] = n11
    sums_ref[1:2, :] = n01
    sums_ref[2:3, :] = inner(back_ref[...], c1)
    sums_ref[3:4, :] = ridden(c1_ref, rank)[0]
    send(out_ref, next1, row_limits(ranks_ref, here_ref[0], n), rank)
    ride(out_ref, n11, n01, rank)


def column2(
    rank, here_ref, ranks_ref, b2_ref, b0_ref, b1s_ref, hi_ref, lo_ref, g0_ref, g1_ref,
    known0_ref, known1_ref, sums_ref, out_ref
):
    n = out_ref.shape[0]
    real, imag = unpack(b2_ref, rank)
    n11, n01 = ridden(b2_ref, rank)
    theta1 = ratio(n11, known1_ref[3:4, :])
    phi = ratio(n01, known0_ref[2:3, :])
    wide1, wide0 = twice(theta1), twice(phi)
    b0 = side(*unpack(b0_ref, rank)).astype(F32)
    g2 = apply_gram(hi_ref, lo_ref, real, imag) - wide1 * g1_ref[...] - wide0 * g0_ref[...]
    b2 = side(real, imag).astype(F32) - wide1 * b1s_ref[...] - wide0 * b0
    sums_ref[0:1, :] = inner(b2, g2)
    sums_ref[1:2, :] = inner(b0, g2)
    sums_ref[2:3, :] = inner(b1s_ref[...], g2)
    sums_ref[3:4, :] = theta1
    sums_ref[4:5, :] = phi
    send(out_ref, g2, column_limits(ranks_ref, here_ref[0], n), rank)


def row2(
    rank, freq_ref, c2_ref, c0_ref, c1_ref, hi_ref, lo_ref, back_ref,
    m0_ref, n0_ref, m1_ref, n1_ref, m2_ref, out_ref
):
    real, imag = unpack(c2_ref, rank)
    next2 = apply_gram(hi_ref, lo_ref, real, imag)
    c2 = side(real, imag).astype(F32)
    c0 = side(*unpack(c0_ref, rank)).astype(F32)
    c1 = side(*unpack(c1_ref, rank)).astype(F32)
    damping = 0.1 + 0.9 * freq_ref[0].astype(F32) / 229.0
    rows = [
        n0_ref[0:1, :] + damping * m0_ref[0:1, :],
        n1_ref[1:2, :] + damping * m1_ref[1:2, :],
        inner(c0, next2) + damping * m2_ref[1:2, :],
        n1_ref[0:1, :] + damping * m1_ref[0:1, :],
        inner(c1, next2) + damping * m2_ref[2:3, :],
        inner(c2, next2) + damping * m2_ref[0:1, :],
        n0_ref[1:2, :],
        n1_ref[2:3, :],
        inner(back_ref[...], c2),
        m1_ref[2:3, :],
        m2_ref[3:4, :],
        m2_ref[4:5, :],
        jnp.full_like(m0_ref[0:1, :], damping),
    ]
    rows = rows + [jnp.zeros_like(rows[0])] * (ROWS - len(rows))
    block = jnp.concatenate(rows, axis=0)
    for p in range(out_ref.shape[0]):
        out_ref[p] = block


def forms(h, u, g, p, position, size):
    def times(v):
        return [sum(h[a][b] * v[b] for b in range(size)) for a in range(size)]

    def along(a, b):
        return jnp.sum(sum(x * y for x, y in zip(a, b)), axis=0, keepdims=True)

    hg, hp, hx = times(g), times(p), times(position)
    rest = [u[a] - hx[a] for a in range(size)]
    return along(g, hg), along(p, hg), along(p, hp), along(g, rest), along(p, rest)


def finish_kernel(
    rank, nfreq, mine_ref, recv_ref, data_ref, left_ref, right_ref,
    b0_ref, b1_ref, b2_ref, c0_ref, c1_ref, c2_ref, wave_ref, res_ref, table_ref, mix_ref
):
    ntile = recv_ref.shape[0] // nfreq
    for f in range(nfreq):
        total = recv_ref[f * ntile]
        for t in range(1, ntile):
            total = total + recv_ref[f * ntile + t]
        table_ref[0, :, f, :] = total
        table_ref[1, :, f, :] = recv_ref[f * ntile]
    h = [[None] * 3 for _ in range(3)]
    for place, (a, b) in enumerate([(0, 0), (0, 1), (0, 2), (1, 1), (1, 2), (2, 2)]):
        h[a][b] = h[b][a] = table_ref[0, place]
    u = [table_ref[0, 6 + a] for a in range(3)]
    theta0, theta1, phi, damping = [table_ref[1, 9 + a] for a in range(4)]
    one = jnp.ones_like(theta0)
    a11 = jnp.sum(h[0][0], axis=0, keepdims=True)
    b1 = jnp.sum(u[0], axis=0, keepdims=True)
    alpha = b1 / (1.1 * a11)
    p = [alpha * one]
    x = [alpha * one]
    for size in (2, 3):
        zero = jnp.zeros_like(one)
        x = x + [zero]
        p = p + [zero]
        if size == 2:
            g = [one - (theta0 + damping) * x[0], -x[0]]
        else:
            g = [
                one - (theta0 + damping) * x[0] - phi * x[1],
                -x[0] - (theta1 + damping) * x[1],
                -x[1],
            ]
        a11, a12, a22, b1, b2 = forms(h, u, g, p, x, size)
        first, second = 1.1 * a11, 1.1 * a22
        determinant = first * second - a12 * a12
        alpha = (b1 * second - a12 * b2) / determinant
        beta = (first * b2 - a12 * b1) / determinant
        p = [alpha * g[a] + beta * p[a] for a in range(size)]
        x = [x[a] + p[a] for a in range(size)]
    mix_ref[0] = x[0] - theta0 * x[1] + (theta0 * theta1 - phi) * x[2]
    mix_ref[1] = x[1] - theta1 * x[2]
    mix_ref[2] = x[2]
    mix_ref[3] = x[0]
    mix_ref[4] = x[1]
    mix_ref[5] = x[2]
    row = pl.ds(mine_ref[0], 1)

    def combine(refs, offset):
        total = None
        for k, ref in enumerate(refs):
            scale = mix_ref[offset + k, row, :]
            real, imag = unpack(ref, rank)
            term = (scale * real.astype(F32), scale * imag.astype(F32))
            total = term if total is None else (total[0] + term[0], total[1] + term[1])
        return total

    def plain(factor_ref, real, imag):
        (rh, rl), (ih, il) = split(real), split(imag)
        first, second = factor_ref[0], factor_ref[1]
        return (
            dot(first, side(rh, ih)) + dot(second, side(-ih, rh))
            + dot(first, side(rl, il)) + dot(second, side(-il, rl))
        )

    s = wave_ref.shape[2]
    wave = plain(right_ref, *combine([b0_ref, b1_ref, b2_ref], 0))
    wave_ref[0] = wave[:, :s]
    wave_ref[1] = wave[:, s:]
    image = plain(left_ref, *combine([c0_ref, c1_ref, c2_ref], 3))
    res_ref[0] = data_ref[0].astype(F32) - image[:, :s]
    res_ref[1] = data_ref[1].astype(F32) - image[:, s:]


def body(data, left_factor, right_factor, ranks, freq_index):
    ntile = lax.axis_size("tcol")
    nfreq = lax.axis_size("freq")
    here = lax.axis_index("tcol").reshape(1)
    mine = lax.axis_index("freq").reshape(1)
    data, left, right, ranks = data[0], left_factor[0], right_factor[0], ranks[0]
    width = left.shape[2]
    rank = width // ntile
    s = data.shape[2]
    field = jax.ShapeDtypeStruct((width, 2 * s), F32)
    sums = jax.ShapeDtypeStruct((8, s), F32)
    bare = jax.ShapeDtypeStruct((ntile, 2 * rank, s), BF16)
    message = jax.ShapeDtypeStruct((ntile, 2 * rank + RIDE, s), BF16)
    gram = jax.ShapeDtypeStruct((width, 2 * width), BF16)

    def call(kernel, scalars, arrays, outs, scratch=(), *static):
        return pl.pallas_call(
            functools.partial(kernel, *static) if static else kernel,
            out_shape=outs,
            in_specs=[SMEM] * len(scalars) + [VMEM] * len(arrays),
            out_specs=[VMEM] * len(outs),
            scratch_shapes=scratch,
        )(*scalars, *arrays)

    def exchange(value):
        return lax.all_to_all(value, "tcol", 0, 0, tiled=True)

    where = (here, ranks)
    back, out = call(start_kernel, where, (data, left), (field, bare), (), rank)
    b0 = exchange(out)
    vhi, vlo = call(gram_kernel, (), (right,), (gram, gram))
    uhi, ulo = call(gram_kernel, (), (left,), (gram, gram))
    g0, m0, out = call(column0, where, (b0, vhi, vlo), (field, sums, message), (), rank)
    c0 = exchange(out)
    n0, out = call(row0, where, (c0, uhi, ulo, back), (sums, message), (), rank)
    b1 = exchange(out)
    g1, b1s, m1, out = call(
        column1, where, (b1, b0, vhi, vlo, g0, n0), (field, field, sums, message), (), rank
    )
    c1 = exchange(out)
    n1, out = call(row1, where, (c1, c0, uhi, ulo, back), (sums, message), (), rank)
    b2 = exchange(out)
    m2, out = call(
        column2, where, (b2, b0, b1s, vhi, vlo, g0, g1, n0, n1), (sums, bare), (), rank
    )
    c2 = exchange(out)
    (out,) = call(
        row2, (freq_index,), (c2, c0, c1, uhi, ulo, back, m0, n0, m1, n1, m2),
        (jax.ShapeDtypeStruct((nfreq * ntile, ROWS, s), F32),), (), rank
    )
    everyone = lax.all_to_all(out, ("freq", "tcol"), 0, 0, tiled=True)
    shape = jax.ShapeDtypeStruct(data.shape, F32)
    wave, res = call(
        finish_kernel, (mine,), (everyone, data, left, right, b0, b1, b2, c0, c1, c2),
        (shape, shape),
        (pltpu.VMEM((2, ROWS, nfreq, s), F32), pltpu.VMEM((6, nfreq, s), F32)), rank, nfreq
    )
    return wave[None], res[None]


def solution(mesh):
    in_specs = (
        P("freq", None, "tcol", None),
        P("freq", None, "tcol", None),
        P("freq", None, "tcol", None),
        P("freq", None, None),
        P("freq"),
    )
    out_specs = (P("freq", None, "tcol", None), P("freq", None, "tcol", None))
    return jax.shard_map(body, mesh=mesh, in_specs=in_specs, out_specs=out_specs, check_vma=False)
```

```python
import functools

import jax
import jax.numpy as jnp
from jax import lax
from jax.experimental import pallas as pl
from jax.experimental.pallas import tpu as pltpu
from jax.sharding import PartitionSpec as P


RIDE = 16
ROWS = 16
VMEM = pl.BlockSpec(memory_space=pltpu.VMEM)
SMEM = pl.BlockSpec(memory_space=pltpu.SMEM)
F32 = jnp.float32
BF16 = jnp.bfloat16


def dot(a, b):
    return jnp.dot(a, b, preferred_element_type=F32)


def dot_t(a, b):
    return lax.dot_general(a, b, (((0,), (0,)), ((), ())), preferred_element_type=F32)


def side(real, imag):
    return jnp.concatenate([real, imag], axis=1)


def split(value):
    high = value.astype(BF16)
    return high, (value - high.astype(F32)).astype(BF16)


def unpack(ref, rank):
    n = ref.shape[0]
    real = ref[:, 0:rank, :].reshape(n * rank, ref.shape[2])
    imag = ref[:, rank : 2 * rank, :].reshape(n * rank, ref.shape[2])
    return real, imag


def send(out_ref, value, limits, rank):
    s = out_ref.shape[2]
    level = lax.broadcasted_iota(jnp.int32, (rank, s), 0)
    for p in range(out_ref.shape[0]):
        keep = level < limits[p]
        rows = value[p * rank : (p + 1) * rank]
        out_ref[p, 0:rank, :] = jnp.where(keep, rows[:, :s], 0.0).astype(BF16)
        out_ref[p, rank : 2 * rank, :] = jnp.where(keep, rows[:, s:], 0.0).astype(BF16)


def ride(out_ref, first, second, rank):
    s = out_ref.shape[2]
    row = lax.broadcasted_iota(jnp.int32, (RIDE, s), 0)
    block = jnp.where(row == 0, first, second).astype(BF16)
    for p in range(out_ref.shape[0]):
        out_ref[p, 2 * rank : 2 * rank + RIDE, :] = block


def ridden(ref, rank):
    total = ref[0, 2 * rank : 2 * rank + RIDE, :].astype(F32)
    for p in range(1, ref.shape[0]):
        total = total + ref[p, 2 * rank : 2 * rank + RIDE, :].astype(F32)
    return total[0:1], total[1:2]


def inner(a, b):
    both = jnp.sum(a * b, axis=0, keepdims=True)
    s = both.shape[1] // 2
    return both[:, :s] + both[:, s:]


def twice(row):
    return jnp.concatenate([row, row], axis=1)


def ratio(top, bottom):
    safe = bottom > 0
    return jnp.where(safe, top / jnp.where(safe, bottom, 1.0), 0.0)


def apply_gram(hi_ref, lo_ref, real, imag):
    vector = jnp.concatenate([side(real, imag), side(-imag, real)], axis=0)
    return dot(hi_ref[...], vector) + dot(lo_ref[...], vector)


def row_limits(ranks_ref, here, n):
    return [ranks_ref[here, p] for p in range(n)]


def column_limits(ranks_ref, here, n):
    return [ranks_ref[p, here] for p in range(n)]


def start_kernel(rank, here_ref, ranks_ref, data_ref, factor_ref, back_ref, out_ref):
    n = out_ref.shape[0]
    real, imag = data_ref[0], data_ref[1]
    back = dot_t(factor_ref[0], side(real, imag)) + dot_t(factor_ref[1], side(imag, -real))
    back_ref[...] = back
    send(out_ref, back, row_limits(ranks_ref, here_ref[0], n), rank)


def gram_kernel(factor_ref, hi_ref, lo_ref):
    real, imag = factor_ref[0], factor_ref[1]
    width = real.shape[1]
    high, low = split(dot_t(real, real) + dot_t(imag, imag))
    hi_ref[:, :width] = high
    lo_ref[:, :width] = low
    high, low = split(dot_t(real, imag) - dot_t(imag, real))
    hi_ref[:, width:] = high
    lo_ref[:, width:] = low


def column0(rank, here_ref, ranks_ref, b0_ref, hi_ref, lo_ref, g0_ref, sums_ref, out_ref):
    n = out_ref.shape[0]
    real, imag = unpack(b0_ref, rank)
    g0 = apply_gram(hi_ref, lo_ref, real, imag)
    g0_ref[...] = g0
    m00 = inner(side(real, imag).astype(F32), g0)
    sums_ref[0:1, :] = m00
    send(out_ref, g0, column_limits(ranks_ref, here_ref[0], n), rank)
    ride(out_ref, m00, m00, rank)


def row0(rank, here_ref, ranks_ref, c0_ref, hi_ref, lo_ref, back_ref, sums_ref, out_ref):
    n = out_ref.shape[0]
    real, imag = unpack(c0_ref, rank)
    next0 = apply_gram(hi_ref, lo_ref, real, imag)
    c0 = side(real, imag).astype(F32)
    n00 = inner(c0, next0)
    sums_ref[0:1, :] = n00
    sums_ref[1:2, :] = inner(back_ref[...], c0)
    sums_ref[2:3, :] = ridden(c0_ref, rank)[0]
    send(out_ref, next0, row_limits(ranks_ref, here_ref[0], n), rank)
    ride(out_ref, n00, n00, rank)


def column1(
    rank, here_ref, ranks_ref, b1_ref, b0_ref, hi_ref, lo_ref, g0_ref, known_ref,
    g1_ref, b1s_ref, sums_ref, out_ref
):
    n = out_ref.shape[0]
    real, imag = unpack(b1_ref, rank)
    theta0 = ratio(ridden(b1_ref, rank)[0], known_ref[2:3, :])
    wide = twice(theta0)
    g1 = apply_gram(hi_ref, lo_ref, real, imag) - wide * g0_ref[...]
    b0 = side(*unpack(b0_ref, rank)).astype(F32)
    b1 = side(real, imag).astype(F32) - wide * b0
    g1_ref[...] = g1
    b1s_ref[...] = b1
    m11 = inner(b1, g1)
    sums_ref[0:1, :] = m11
    sums_ref[1:2, :] = inner(b0, g1)
    sums_ref[2:3, :] = theta0
    send(out_ref, g1, column_limits(ranks_ref, here_ref[0], n), rank)
    ride(out_ref, m11, m11, rank)


def row1(
    rank, here_ref, ranks_ref, c1_ref, c0_ref, hi_ref, lo_ref, back_ref, sums_ref, out_ref
):
    n = out_ref.shape[0]
    real, imag = unpack(c1_ref, rank)
    next1 = apply_gram(hi_ref, lo_ref, real, imag)
    c1 = side(real, imag).astype(F32)
    c0 = side(*unpack(c0_ref, rank)).astype(F32)
    n11 = inner(c1, next1)
    n01 = inner(c0, next1)
    sums_ref[0:1, :] = n11
    sums_ref[1:2, :] = n01
    sums_ref[2:3, :] = inner(back_ref[...], c1)
    sums_ref[3:4, :] = ridden(c1_ref, rank)[0]
    send(out_ref, next1, row_limits(ranks_ref, here_ref[0], n), rank)
    ride(out_ref, n11, n01, rank)


def column2(
    rank, here_ref, ranks_ref, b2_ref, b0_ref, b1s_ref, hi_ref, lo_ref, g0_ref, g1_ref,
    known0_ref, known1_ref, sums_ref, out_ref
):
    n = out_ref.shape[0]
    real, imag = unpack(b2_ref, rank)
    n11, n01 = ridden(b2_ref, rank)
    theta1 = ratio(n11, known1_ref[3:4, :])
    phi = ratio(n01, known0_ref[2:3, :])
    wide1, wide0 = twice(theta1), twice(phi)
    b0 = side(*unpack(b0_ref, rank)).astype(F32)
    g2 = apply_gram(hi_ref, lo_ref, real, imag) - wide1 * g1_ref[...] - wide0 * g0_ref[...]
    b2 = side(real, imag).astype(F32) - wide1 * b1s_ref[...] - wide0 * b0
    sums_ref[0:1, :] = inner(b2, g2)
    sums_ref[1:2, :] = inner(b0, g2)
    sums_ref[2:3, :] = inner(b1s_ref[...], g2)
    sums_ref[3:4, :] = theta1
    sums_ref[4:5, :] = phi
    send(out_ref, g2, column_limits(ranks_ref, here_ref[0], n), rank)


def row2(
    rank, freq_ref, c2_ref, c0_ref, c1_ref, hi_ref, lo_ref, back_ref,
    m0_ref, n0_ref, m1_ref, n1_ref, m2_ref, out_ref
):
    real, imag = unpack(c2_ref, rank)
    next2 = apply_gram(hi_ref, lo_ref, real, imag)
    c2 = side(real, imag).astype(F32)
    c0 = side(*unpack(c0_ref, rank)).astype(F32)
    c1 = side(*unpack(c1_ref, rank)).astype(F32)
    damping = 0.1 + 0.9 * freq_ref[0].astype(F32) / 229.0
    rows = [
        n0_ref[0:1, :] + damping * m0_ref[0:1, :],
        n1_ref[1:2, :] + damping * m1_ref[1:2, :],
        inner(c0, next2) + damping * m2_ref[1:2, :],
        n1_ref[0:1, :] + damping * m1_ref[0:1, :],
        inner(c1, next2) + damping * m2_ref[2:3, :],
        inner(c2, next2) + damping * m2_ref[0:1, :],
        n0_ref[1:2, :],
        n1_ref[2:3, :],
        inner(back_ref[...], c2),
        m1_ref[2:3, :],
        m2_ref[3:4, :],
        m2_ref[4:5, :],
        jnp.full_like(m0_ref[0:1, :], damping),
    ]
    rows = rows + [jnp.zeros_like(rows[0])] * (ROWS - len(rows))
    block = jnp.concatenate(rows, axis=0)
    for p in range(out_ref.shape[0]):
        out_ref[p] = block


def forms(h, u, g, p, position, size):
    def times(v):
        return [sum(h[a][b] * v[b] for b in range(size)) for a in range(size)]

    def along(a, b):
        return jnp.sum(sum(x * y for x, y in zip(a, b)), axis=0, keepdims=True)

    hg, hp, hx = times(g), times(p), times(position)
    rest = [u[a] - hx[a] for a in range(size)]
    return along(g, hg), along(p, hg), along(p, hp), along(g, rest), along(p, rest)


def finish_kernel(
    rank, nfreq, mine_ref, recv_ref, data_ref, left_ref, right_ref,
    b0_ref, b1_ref, b2_ref, c0_ref, c1_ref, c2_ref, wave_ref, res_ref, table_ref, mix_ref
):
    ntile = recv_ref.shape[0] // nfreq
    for f in range(nfreq):
        total = recv_ref[f * ntile]
        for t in range(1, ntile):
            total = total + recv_ref[f * ntile + t]
        table_ref[0, :, f, :] = total
        table_ref[1, :, f, :] = recv_ref[f * ntile]
    h = [[None] * 3 for _ in range(3)]
    for place, (a, b) in enumerate([(0, 0), (0, 1), (0, 2), (1, 1), (1, 2), (2, 2)]):
        h[a][b] = h[b][a] = table_ref[0, place]
    u = [table_ref[0, 6 + a] for a in range(3)]
    theta0, theta1, phi, damping = [table_ref[1, 9 + a] for a in range(4)]
    one = jnp.ones_like(theta0)
    a11 = jnp.sum(h[0][0], axis=0, keepdims=True)
    b1 = jnp.sum(u[0], axis=0, keepdims=True)
    alpha = b1 / (1.1 * a11)
    p = [alpha * one]
    x = [alpha * one]
    for size in (2, 3):
        zero = jnp.zeros_like(one)
        x = x + [zero]
        p = p + [zero]
        if size == 2:
            g = [one - (theta0 + damping) * x[0], -x[0]]
        else:
            g = [
                one - (theta0 + damping) * x[0] - phi * x[1],
                -x[0] - (theta1 + damping) * x[1],
                -x[1],
            ]
        a11, a12, a22, b1, b2 = forms(h, u, g, p, x, size)
        first, second = 1.1 * a11, 1.1 * a22
        determinant = first * second - a12 * a12
        alpha = (b1 * second - a12 * b2) / determinant
        beta = (first * b2 - a12 * b1) / determinant
        p = [alpha * g[a] + beta * p[a] for a in range(size)]
        x = [x[a] + p[a] for a in range(size)]
    mix_ref[0] = x[0] - theta0 * x[1] + (theta0 * theta1 - phi) * x[2]
    mix_ref[1] = x[1] - theta1 * x[2]
    mix_ref[2] = x[2]
    mix_ref[3] = x[0]
    mix_ref[4] = x[1]
    mix_ref[5] = x[2]
    row = pl.ds(mine_ref[0], 1)

    def combine(refs, offset):
        total = None
        for k, ref in enumerate(refs):
            scale = mix_ref[offset + k, row, :]
            real, imag = unpack(ref, rank)
            term = (scale * real.astype(F32), scale * imag.astype(F32))
            total = term if total is None else (total[0] + term[0], total[1] + term[1])
        return total

    def plain(factor_ref, real, imag):
        (rh, rl), (ih, il) = split(real), split(imag)
        first, second = factor_ref[0], factor_ref[1]
        return (
            dot(first, side(rh, ih)) + dot(second, side(-ih, rh))
            + dot(first, side(rl, il)) + dot(second, side(-il, rl))
        )

    s = wave_ref.shape[2]
    wave = plain(right_ref, *combine([b0_ref, b1_ref, b2_ref], 0))
    wave_ref[0] = wave[:, :s]
    wave_ref[1] = wave[:, s:]
    image = plain(left_ref, *combine([c0_ref, c1_ref, c2_ref], 3))
    res_ref[0] = data_ref[0].astype(F32) - image[:, :s]
    res_ref[1] = data_ref[1].astype(F32) - image[:, s:]


def body(data, left_factor, right_factor, ranks, freq_index):
    ntile = lax.axis_size("tcol")
    nfreq = lax.axis_size("freq")
    here = lax.axis_index("tcol").reshape(1)
    mine = lax.axis_index("freq").reshape(1)
    data, left, right, ranks = data[0], left_factor[0], right_factor[0], ranks[0]
    width = left.shape[2]
    rank = width // ntile
    s = data.shape[2]
    field = jax.ShapeDtypeStruct((width, 2 * s), F32)
    sums = jax.ShapeDtypeStruct((8, s), F32)
    bare = jax.ShapeDtypeStruct((ntile, 2 * rank, s), BF16)
    message = jax.ShapeDtypeStruct((ntile, 2 * rank + RIDE, s), BF16)
    gram = jax.ShapeDtypeStruct((width, 2 * width), BF16)

    room = (8 << 20) + 24 * width * width

    def call(kernel, scalars, arrays, outs, scratch=(), *static):
        return pl.pallas_call(
            functools.partial(kernel, *static) if static else kernel,
            out_shape=outs,
            in_specs=[SMEM] * len(scalars) + [VMEM] * len(arrays),
            out_specs=[VMEM] * len(outs),
            scratch_shapes=scratch,
            compiler_params=pltpu.CompilerParams(vmem_limit_bytes=room),
        )(*scalars, *arrays)

    def exchange(value):
        return lax.all_to_all(value, "tcol", 0, 0, tiled=True)

    where = (here, ranks)
    back, out = call(start_kernel, where, (data, left), (field, bare), (), rank)
    b0 = exchange(out)
    vhi, vlo = call(gram_kernel, (), (right,), (gram, gram))
    uhi, ulo = call(gram_kernel, (), (left,), (gram, gram))
    g0, m0, out = call(column0, where, (b0, vhi, vlo), (field, sums, message), (), rank)
    c0 = exchange(out)
    n0, out = call(row0, where, (c0, uhi, ulo, back), (sums, message), (), rank)
    b1 = exchange(out)
    g1, b1s, m1, out = call(
        column1, where, (b1, b0, vhi, vlo, g0, n0), (field, field, sums, message), (), rank
    )
    c1 = exchange(out)
    n1, out = call(row1, where, (c1, c0, uhi, ulo, back), (sums, message), (), rank)
    b2 = exchange(out)
    m2, out = call(
        column2, where, (b2, b0, b1s, vhi, vlo, g0, g1, n0, n1), (sums, bare), (), rank
    )
    c2 = exchange(out)
    (out,) = call(
        row2, (freq_index,), (c2, c0, c1, uhi, ulo, back, m0, n0, m1, n1, m2),
        (jax.ShapeDtypeStruct((nfreq * ntile, ROWS, s), F32),), (), rank
    )
    everyone = lax.all_to_all(out, ("freq", "tcol"), 0, 0, tiled=True)
    shape = jax.ShapeDtypeStruct(data.shape, F32)
    wave, res = call(
        finish_kernel, (mine,), (everyone, data, left, right, b0, b1, b2, c0, c1, c2),
        (shape, shape),
        (pltpu.VMEM((2, ROWS, nfreq, s), F32), pltpu.VMEM((6, nfreq, s), F32)), rank, nfreq
    )
    return wave[None], res[None]


def solution(mesh):
    in_specs = (
        P("freq", None, "tcol", None),
        P("freq", None, "tcol", None),
        P("freq", None, "tcol", None),
        P("freq", None, None),
        P("freq"),
    )
    out_specs = (P("freq", None, "tcol", None), P("freq", None, "tcol", None))
    return jax.shard_map(body, mesh=mesh, in_specs=in_specs, out_specs=out_specs, check_vma=False)
```

```python
import functools

import jax
import jax.numpy as jnp
from jax import lax
from jax.experimental import pallas as pl
from jax.experimental.pallas import tpu as pltpu
from jax.sharding import PartitionSpec as P


RIDE = 16
LATE = 4
EARLY = 9
VMEM = pl.BlockSpec(memory_space=pltpu.VMEM)
SMEM = pl.BlockSpec(memory_space=pltpu.SMEM)
HBM = pl.BlockSpec(memory_space=pltpu.HBM)
F32 = jnp.float32
BF16 = jnp.bfloat16


def dot(a, b):
    return jnp.dot(a, b, preferred_element_type=F32)


def dot_t(a, b):
    return lax.dot_general(a, b, (((0,), (0,)), ((), ())), preferred_element_type=F32)


def side(real, imag):
    return jnp.concatenate([real, imag], axis=1)


def split(value):
    high = value.astype(BF16)
    return high, (value - high.astype(F32)).astype(BF16)


def unpack(ref, rank):
    n = ref.shape[0]
    real = ref[:, 0:rank, :].reshape(n * rank, ref.shape[2])
    imag = ref[:, rank : 2 * rank, :].reshape(n * rank, ref.shape[2])
    return real, imag


def fields(ref, rank):
    return side(*unpack(ref, rank)).astype(F32)


def send(out_ref, value, rank):
    s = out_ref.shape[2]
    for p in range(out_ref.shape[0]):
        rows = value[p * rank : (p + 1) * rank].astype(BF16)
        out_ref[p, 0:rank, :] = rows[:, :s]
        out_ref[p, rank : 2 * rank, :] = rows[:, s:]


def ride(out_ref, rows, rank):
    rows = rows + [jnp.zeros_like(rows[0])] * (RIDE - len(rows))
    block = jnp.concatenate(rows, axis=0).astype(BF16)
    for p in range(out_ref.shape[0]):
        out_ref[p, 2 * rank : 2 * rank + RIDE, :] = block


def ridden(ref, rank):
    total = ref[0, 2 * rank : 2 * rank + RIDE, :].astype(F32)
    for p in range(1, ref.shape[0]):
        total = total + ref[p, 2 * rank : 2 * rank + RIDE, :].astype(F32)
    return total


def inner(a, b):
    both = jnp.sum(a * b, axis=0, keepdims=True)
    s = both.shape[1] // 2
    return both[:, :s] + both[:, s:]


def twice(row):
    return jnp.concatenate([row, row], axis=1)


def ratio(top, bottom):
    safe = bottom > 0
    return jnp.where(safe, top / jnp.where(safe, bottom, 1.0), 0.0)


def apply_gram(hi_ref, lo_ref, real, imag):
    vector = jnp.concatenate([side(real, imag), side(-imag, real)], axis=0)
    return dot(hi_ref[...], vector) + dot(lo_ref[...], vector)


def make_gram(factor_ref, hi_ref, lo_ref, limits):
    real, imag = factor_ref[0], factor_ref[1]
    width = real.shape[1]
    rank = width // len(limits)
    level = lax.broadcasted_iota(jnp.int32, (rank, width), 0)

    def put(value, place):
        for p, limit in enumerate(limits):
            rows = slice(p * rank, (p + 1) * rank)
            high, low = split(jnp.where(level < limit, value[rows], 0.0))
            hi_ref[rows, place : place + width] = high
            lo_ref[rows, place : place + width] = low

    put(dot_t(real, real) + dot_t(imag, imag), 0)
    put(dot_t(real, imag) - dot_t(imag, real), width)


def start_kernel(
    rank, here_ref, mine_ref, ranks_hbm, freq_hbm, data_hbm, left_hbm, right_hbm,
    right_ref, back_ref, sums_ref, out_ref, uhi_ref, ulo_ref, vhi_ref, vlo_ref,
    ranks_ref, freq_ref, data_ref, left_ref, sem
):
    n = out_ref.shape[0]
    s = out_ref.shape[2]
    pairs = [
        (left_hbm, left_ref), (data_hbm, data_ref), (ranks_hbm, ranks_ref),
        (freq_hbm, freq_ref), (right_hbm, right_ref),
    ]
    copies = [
        pltpu.make_async_copy(source, target, sem.at[k])
        for k, (source, target) in enumerate(pairs)
    ]
    for copy in copies:
        copy.start()
    for copy in copies[:4]:
        copy.wait()
    here = here_ref[0]
    row_limits = [ranks_ref[here, p] for p in range(n)]
    column_limits = [ranks_ref[p, here] for p in range(n)]
    damping = 0.1 + 0.9 * freq_ref[0].astype(F32) / 229.0
    sums_ref[...] = jnp.full(sums_ref.shape, damping)
    real, imag = data_ref[0], data_ref[1]
    back = dot_t(left_ref[0], side(real, imag)) + dot_t(left_ref[1], side(imag, -real))
    level = lax.broadcasted_iota(jnp.int32, (rank, 2 * s), 0)
    back = jnp.concatenate(
        [
            jnp.where(level < limit, back[p * rank : (p + 1) * rank], 0.0)
            for p, limit in enumerate(row_limits)
        ],
        axis=0,
    )
    back_ref[...] = back
    send(out_ref, back, rank)
    make_gram(left_ref, uhi_ref, ulo_ref, row_limits)
    copies[4].wait()
    make_gram(right_ref, vhi_ref, vlo_ref, column_limits)


def column0(rank, b0_ref, hi_ref, lo_ref, g0_ref, sums_ref, out_ref):
    real, imag = unpack(b0_ref, rank)
    g0 = apply_gram(hi_ref, lo_ref, real, imag)
    g0_ref[...] = g0
    m00 = inner(side(real, imag).astype(F32), g0)
    sums_ref[0:1, :] = m00
    send(out_ref, g0, rank)
    ride(out_ref, [m00], rank)


def row0(rank, c0_ref, hi_ref, lo_ref, back_ref, sums_ref, out_ref):
    real, imag = unpack(c0_ref, rank)
    next0 = apply_gram(hi_ref, lo_ref, real, imag)
    c0 = side(real, imag).astype(F32)
    n00 = inner(c0, next0)
    sums_ref[0:1, :] = n00
    sums_ref[1:2, :] = inner(back_ref[...], c0)
    sums_ref[2:3, :] = ridden(c0_ref, rank)[0:1]
    send(out_ref, next0, rank)
    ride(out_ref, [n00], rank)


def column1(
    rank, b1_ref, b0_ref, hi_ref, lo_ref, g0_ref, n0_ref, g1_ref, sums_ref, out_ref
):
    real, imag = unpack(b1_ref, rank)
    theta0 = ratio(ridden(b1_ref, rank)[0:1], n0_ref[2:3, :])
    wide = twice(theta0)
    g1 = apply_gram(hi_ref, lo_ref, real, imag) - wide * g0_ref[...]
    b0 = fields(b0_ref, rank)
    b1 = side(real, imag).astype(F32) - wide * b0
    g1_ref[...] = g1
    m11 = inner(b1, g1)
    sums_ref[0:1, :] = m11
    sums_ref[1:2, :] = inner(b0, g1)
    sums_ref[2:3, :] = theta0
    send(out_ref, g1, rank)
    ride(out_ref, [m11], rank)


def row1(rank, c1_ref, c0_ref, hi_ref, lo_ref, back_ref, sums_ref, out_ref):
    real, imag = unpack(c1_ref, rank)
    next1 = apply_gram(hi_ref, lo_ref, real, imag)
    c1 = side(real, imag).astype(F32)
    n11 = inner(c1, next1)
    n01 = inner(fields(c0_ref, rank), next1)
    sums_ref[0:1, :] = n11
    sums_ref[1:2, :] = n01
    sums_ref[2:3, :] = inner(back_ref[...], c1)
    sums_ref[3:4, :] = ridden(c1_ref, rank)[0:1]
    send(out_ref, next1, rank)
    ride(out_ref, [n11, n01], rank)


def column2(
    rank, b2_ref, b0_ref, b1_ref, hi_ref, lo_ref, g0_ref, g1_ref,
    damp_ref, m0_ref, n0_ref, m1_ref, n1_ref, sums_ref, out_ref
):
    real, imag = unpack(b2_ref, rank)
    came = ridden(b2_ref, rank)
    theta1 = ratio(came[0:1], n1_ref[3:4, :])
    phi = ratio(came[1:2], n0_ref[2:3, :])
    wide1, wide0 = twice(theta1), twice(phi)
    g2 = apply_gram(hi_ref, lo_ref, real, imag) - wide1 * g1_ref[...] - wide0 * g0_ref[...]
    send(out_ref, g2, rank)
    b0 = fields(b0_ref, rank)
    b1 = fields(b1_ref, rank) - twice(m1_ref[2:3, :]) * b0
    b2 = side(real, imag).astype(F32) - wide1 * b1 - wide0 * b0
    sums_ref[0:1, :] = inner(b0, g2)
    sums_ref[1:2, :] = inner(b1, g2)
    sums_ref[2:3, :] = inner(b2, g2)
    sums_ref[3:4, :] = theta1
    sums_ref[4:5, :] = phi
    damping = damp_ref[0:1, :]
    known = [
        n0_ref[0:1, :] + damping * m0_ref[0:1, :],
        n1_ref[1:2, :] + damping * m1_ref[1:2, :],
        n1_ref[0:1, :] + damping * m1_ref[0:1, :],
        n0_ref[1:2, :],
        n1_ref[2:3, :],
    ]
    rest = [row - row.astype(BF16).astype(F32) for row in known]
    ride(out_ref, known + rest, rank)


def row2(
    rank, share, here_ref, c2_ref, c0_ref, c1_ref, hi_ref, lo_ref, back_ref,
    damp_ref, m1_ref, m2_ref, out_ref, table_ref
):
    real, imag = unpack(c2_ref, rank)
    next2 = apply_gram(hi_ref, lo_ref, real, imag)
    damping = damp_ref[0:1, :]
    came = ridden(c2_ref, rank)
    table_ref[0:5, :] = came[0:5] + came[5:10]
    table_ref[5:6, :] = m1_ref[2:3, :]
    table_ref[6:8, :] = m2_ref[3:5, :]
    table_ref[8:9, :] = damping
    rows = [
        inner(fields(c0_ref, rank), next2) + damping * m2_ref[0:1, :],
        inner(fields(c1_ref, rank), next2) + damping * m2_ref[1:2, :],
        inner(side(real, imag).astype(F32), next2) + damping * m2_ref[2:3, :],
        inner(back_ref[...], side(real, imag).astype(F32)),
        table_ref[pl.ds(here_ref[0] * share, share), :],
    ]
    more = out_ref.shape[1] - LATE - share
    if more:
        rows.append(jnp.zeros((more, real.shape[1]), F32))
    block = jnp.concatenate(rows, axis=0)
    for p in range(out_ref.shape[0]):
        out_ref[p] = block


def forms(h, u, g, p, position, size):
    def times(v):
        return [sum(h[a][b] * v[b] for b in range(size)) for a in range(size)]

    def along(a, b):
        return jnp.sum(sum(x * y for x, y in zip(a, b)), axis=0, keepdims=True)

    hg, hp, hx = times(g), times(p), times(position)
    rest = [u[a] - hx[a] for a in range(size)]
    return along(g, hg), along(p, hg), along(p, hp), along(g, rest), along(p, rest)


def finish_kernel(
    rank, nfreq, share, mine_ref, data_hbm, left_hbm, recv_ref, right_ref,
    b0_ref, b1_ref, b2_ref, c0_ref, c1_ref, c2_ref, wave_hbm, res_hbm,
    table_ref, mix_ref, wave_ref, res_ref, data_ref, left_ref, sem
):
    left_copy = pltpu.make_async_copy(left_hbm, left_ref, sem.at[2])
    data_copy = pltpu.make_async_copy(data_hbm, data_ref, sem.at[3])
    left_copy.start()
    data_copy.start()
    ntile = recv_ref.shape[0] // nfreq
    for f in range(nfreq):
        total = recv_ref[f * ntile]
        for t in range(1, ntile):
            total = total + recv_ref[f * ntile + t]
        table_ref[0:LATE, f, :] = total[0:LATE]
        for q in range(EARLY):
            place = LATE + q % share
            table_ref[LATE + q, f : f + 1, :] = recv_ref[f * ntile + q // share, place : place + 1]
    h = [[None] * 3 for _ in range(3)]
    places = [(0, 0, 2), (1, 1, 2), (2, 2, 2), (4, 0, 0), (5, 0, 1), (6, 1, 1)]
    for place, a, b in places:
        h[a][b] = h[b][a] = table_ref[place]
    u = [table_ref[7], table_ref[8], table_ref[3]]
    theta0, theta1, phi, damping = [table_ref[9 + a] for a in range(4)]
    one = jnp.ones_like(theta0)
    a11 = jnp.sum(h[0][0], axis=0, keepdims=True)
    b1 = jnp.sum(u[0], axis=0, keepdims=True)
    alpha = b1 / (1.1 * a11)
    p = [alpha * one]
    x = [alpha * one]
    for size in (2, 3):
        zero = jnp.zeros_like(one)
        x = x + [zero]
        p = p + [zero]
        if size == 2:
            g = [one - (theta0 + damping) * x[0], -x[0]]
        else:
            g = [
                one - (theta0 + damping) * x[0] - phi * x[1],
                -x[0] - (theta1 + damping) * x[1],
                -x[1],
            ]
        a11, a12, a22, b1, b2 = forms(h, u, g, p, x, size)
        first, second = 1.1 * a11, 1.1 * a22
        determinant = first * second - a12 * a12
        alpha = (b1 * second - a12 * b2) / determinant
        beta = (first * b2 - a12 * b1) / determinant
        p = [alpha * g[a] + beta * p[a] for a in range(size)]
        x = [x[a] + p[a] for a in range(size)]
    mix_ref[0] = x[0] - theta0 * x[1] + (theta0 * theta1 - phi) * x[2]
    mix_ref[1] = x[1] - theta1 * x[2]
    mix_ref[2] = x[2]
    mix_ref[3] = x[0]
    mix_ref[4] = x[1]
    mix_ref[5] = x[2]
    row = pl.ds(mine_ref[0], 1)

    def combine(refs, offset):
        total = None
        for k, ref in enumerate(refs):
            scale = mix_ref[offset + k, row, :]
            real, imag = unpack(ref, rank)
            term = (scale * real.astype(F32), scale * imag.astype(F32))
            total = term if total is None else (total[0] + term[0], total[1] + term[1])
        return total

    def plain(factor_ref, real, imag):
        (rh, rl), (ih, il) = split(real), split(imag)
        first, second = factor_ref[0], factor_ref[1]
        return (
            dot(first, side(rh, ih)) + dot(second, side(-ih, rh))
            + dot(first, side(rl, il)) + dot(second, side(-il, rl))
        )

    s = wave_ref.shape[2]
    wave = plain(right_ref, *combine([b0_ref, b1_ref, b2_ref], 0))
    wave_ref[0] = wave[:, :s]
    wave_ref[1] = wave[:, s:]
    wave_copy = pltpu.make_async_copy(wave_ref, wave_hbm, sem.at[0])
    wave_copy.start()
    mixed = combine([c0_ref, c1_ref, c2_ref], 3)
    left_copy.wait()
    data_copy.wait()
    image = plain(left_ref, *mixed)
    res_ref[0] = data_ref[0].astype(F32) - image[:, :s]
    res_ref[1] = data_ref[1].astype(F32) - image[:, s:]
    res_copy = pltpu.make_async_copy(res_ref, res_hbm, sem.at[1])
    res_copy.start()
    wave_copy.wait()
    res_copy.wait()


def body(data, left_factor, right_factor, ranks, freq_index):
    ntile = lax.axis_size("tcol")
    nfreq = lax.axis_size("freq")
    here = lax.axis_index("tcol").reshape(1)
    mine = lax.axis_index("freq").reshape(1)
    data, left, right, ranks = data[0], left_factor[0], right_factor[0], ranks[0]
    data, left, right, ranks = [
        pltpu.with_memory_space_constraint(value, pltpu.HBM)
        for value in (data, left, right, ranks)
    ]
    width = left.shape[2]
    rank = width // ntile
    s = data.shape[2]
    share = -(-EARLY // ntile)
    height = -(-(LATE + share) // 8) * 8
    field = jax.ShapeDtypeStruct((width, 2 * s), F32)
    sums = jax.ShapeDtypeStruct((8, s), F32)
    bare = jax.ShapeDtypeStruct((ntile, 2 * rank, s), BF16)
    message = jax.ShapeDtypeStruct((ntile, 2 * rank + RIDE, s), BF16)
    gram = jax.ShapeDtypeStruct((width, 2 * width), BF16)
    room = (8 << 20) + 24 * width * width

    def like(value):
        return jax.ShapeDtypeStruct(value.shape, value.dtype)

    def call(kernel, specs, args, outs, scratch=(), target=VMEM):
        return pl.pallas_call(
            functools.partial(kernel, rank),
            out_shape=outs,
            in_specs=specs,
            out_specs=[target] * len(outs),
            scratch_shapes=scratch,
            compiler_params=pltpu.CompilerParams(vmem_limit_bytes=room),
        )(*args)

    def step(kernel, args, outs):
        return call(kernel, [VMEM] * len(args), args, outs)

    def exchange(value):
        return lax.all_to_all(value, "tcol", 0, 0, tiled=True)

    vright, back, damp, out, uhi, ulo, vhi, vlo = call(
        start_kernel, [SMEM] * 2 + [HBM] * 5, (here, mine, ranks, freq_index, data, left, right),
        (like(right), field, sums, bare, gram, gram, gram, gram),
        [
            pltpu.SMEM(ranks.shape, jnp.int32),
            pltpu.SMEM(freq_index.shape, jnp.int32),
            pltpu.VMEM(data.shape, BF16),
            pltpu.VMEM(left.shape, BF16),
            pltpu.SemaphoreType.DMA((5,)),
        ],
    )
    b0 = exchange(out)
    g0, m0, out = step(column0, (b0, vhi, vlo), (field, sums, message))
    c0 = exchange(out)
    n0, out = step(row0, (c0, uhi, ulo, back), (sums, message))
    b1 = exchange(out)
    g1, m1, out = step(column1, (b1, b0, vhi, vlo, g0, n0), (field, sums, message))
    c1 = exchange(out)
    n1, out = step(row1, (c1, c0, uhi, ulo, back), (sums, message))
    b2 = exchange(out)
    m2, out = step(
        column2, (b2, b0, b1, vhi, vlo, g0, g1, damp, m0, n0, m1, n1), (sums, message)
    )
    c2 = exchange(out)
    args = (here, c2, c0, c1, uhi, ulo, back, damp, m1, m2)
    (out,) = call(
        lambda rank, *refs: row2(rank, share, *refs), [SMEM] + [VMEM] * 9, args,
        (jax.ShapeDtypeStruct((nfreq * ntile, height, s), F32),),
        [pltpu.VMEM((max(16, ntile * share), s), F32)],
    )
    everyone = lax.all_to_all(out, ("freq", "tcol"), 0, 0, tiled=True)
    shape = jax.ShapeDtypeStruct(data.shape, F32)
    wave, res = call(
        lambda rank, *refs: finish_kernel(rank, nfreq, share, *refs),
        [SMEM, HBM, HBM] + [VMEM] * 8,
        (mine, data, left, everyone, vright, b0, b1, b2, c0, c1, c2), (shape, shape),
        [
            pltpu.VMEM((LATE + EARLY, nfreq, s), F32),
            pltpu.VMEM((6, nfreq, s), F32),
            pltpu.VMEM(shape.shape, F32),
            pltpu.VMEM(shape.shape, F32),
            pltpu.VMEM(data.shape, BF16),
            pltpu.VMEM(left.shape, BF16),
            pltpu.SemaphoreType.DMA((4,)),
        ],
        HBM,
    )
    return wave[None], res[None]


def solution(mesh):
    in_specs = (
        P("freq", None, "tcol", None),
        P("freq", None, "tcol", None),
        P("freq", None, "tcol", None),
        P("freq", None, None),
        P("freq"),
    )
    out_specs = (P("freq", None, "tcol", None), P("freq", None, "tcol", None))
    return jax.shard_map(body, mesh=mesh, in_specs=in_specs, out_specs=out_specs, check_vma=False)
```

```python
import functools

import jax
import jax.numpy as jnp
from jax import lax
from jax.experimental import pallas as pl
from jax.experimental.pallas import tpu as pltpu
from jax.sharding import PartitionSpec as P


RIDE = 16
LATE = 4
EARLY = 9
VMEM = pl.BlockSpec(memory_space=pltpu.VMEM)
SMEM = pl.BlockSpec(memory_space=pltpu.SMEM)
HBM = pl.BlockSpec(memory_space=pltpu.HBM)
F32 = jnp.float32
BF16 = jnp.bfloat16


def dot(a, b):
    return jnp.dot(a, b, preferred_element_type=F32)


def dot_t(a, b):
    return lax.dot_general(a, b, (((0,), (0,)), ((), ())), preferred_element_type=F32)


def side(real, imag):
    return jnp.concatenate([real, imag], axis=1)


def split(value):
    high = value.astype(BF16)
    return high, (value - high.astype(F32)).astype(BF16)


def unpack(ref, rank):
    n = ref.shape[0]
    real = ref[:, 0:rank, :].reshape(n * rank, ref.shape[2])
    imag = ref[:, rank : 2 * rank, :].reshape(n * rank, ref.shape[2])
    return real, imag


def fields(ref, rank):
    return side(*unpack(ref, rank)).astype(F32)


def send(out_ref, value, rank):
    s = out_ref.shape[2]
    for p in range(out_ref.shape[0]):
        rows = value[p * rank : (p + 1) * rank].astype(BF16)
        out_ref[p, 0:rank, :] = rows[:, :s]
        out_ref[p, rank : 2 * rank, :] = rows[:, s:]


def ride(out_ref, rows, rank):
    rows = rows + [jnp.zeros_like(rows[0])] * (RIDE - len(rows))
    block = jnp.concatenate(rows, axis=0).astype(BF16)
    for p in range(out_ref.shape[0]):
        out_ref[p, 2 * rank : 2 * rank + RIDE, :] = block


def ridden(ref, rank):
    total = ref[0, 2 * rank : 2 * rank + RIDE, :].astype(F32)
    for p in range(1, ref.shape[0]):
        total = total + ref[p, 2 * rank : 2 * rank + RIDE, :].astype(F32)
    return total


def inner(a, b):
    both = jnp.sum(a * b, axis=0, keepdims=True)
    s = both.shape[1] // 2
    return both[:, :s] + both[:, s:]


def twice(row):
    return jnp.concatenate([row, row], axis=1)


def ratio(top, bottom):
    safe = bottom > 0
    return jnp.where(safe, top / jnp.where(safe, bottom, 1.0), 0.0)


def apply_gram(hi_ref, lo_ref, real, imag):
    vector = jnp.concatenate([side(real, imag), side(-imag, real)], axis=0)
    return dot(hi_ref[...], vector) + dot(lo_ref[...], vector)


def make_gram(factor_ref, hi_ref, lo_ref, limits):
    real, imag = factor_ref[0], factor_ref[1]
    width = real.shape[1]
    rank = width // len(limits)
    level = lax.broadcasted_iota(jnp.int32, (rank, width), 0)

    def put(value, place):
        for p, limit in enumerate(limits):
            rows = slice(p * rank, (p + 1) * rank)
            high, low = split(jnp.where(level < limit, value[rows], 0.0))
            hi_ref[rows, place : place + width] = high
            lo_ref[rows, place : place + width] = low

    put(dot_t(real, real) + dot_t(imag, imag), 0)
    put(dot_t(real, imag) - dot_t(imag, real), width)


def start_kernel(
    rank, here_ref, mine_ref, ranks_hbm, freq_hbm, data_hbm, left_hbm, right_hbm,
    right_ref, back_ref, sums_ref, out_ref, uhi_ref, ulo_ref, vhi_ref, vlo_ref,
    ranks_ref, freq_ref, data_ref, left_ref, sem
):
    n = out_ref.shape[0]
    s = out_ref.shape[2]
    pairs = [
        (left_hbm, left_ref), (data_hbm, data_ref), (ranks_hbm, ranks_ref),
        (freq_hbm, freq_ref), (right_hbm, right_ref),
    ]
    copies = [
        pltpu.make_async_copy(source, target, sem.at[k])
        for k, (source, target) in enumerate(pairs)
    ]
    for copy in copies:
        copy.start()
    for copy in copies[:4]:
        copy.wait()
    here = here_ref[0]
    row_limits = [ranks_ref[here, p] for p in range(n)]
    column_limits = [ranks_ref[p, here] for p in range(n)]
    damping = 0.1 + 0.9 * freq_ref[0].astype(F32) / 229.0
    sums_ref[...] = jnp.full(sums_ref.shape, damping)
    real, imag = data_ref[0], data_ref[1]
    back = dot_t(left_ref[0], side(real, imag)) + dot_t(left_ref[1], side(imag, -real))
    level = lax.broadcasted_iota(jnp.int32, (rank, 2 * s), 0)
    back = jnp.concatenate(
        [
            jnp.where(level < limit, back[p * rank : (p + 1) * rank], 0.0)
            for p, limit in enumerate(row_limits)
        ],
        axis=0,
    )
    back_ref[...] = back
    send(out_ref, back, rank)
    make_gram(left_ref, uhi_ref, ulo_ref, row_limits)
    copies[4].wait()
    make_gram(right_ref, vhi_ref, vlo_ref, column_limits)


def column0(rank, b0_ref, hi_ref, lo_ref, g0_ref, sums_ref, out_ref):
    real, imag = unpack(b0_ref, rank)
    g0 = apply_gram(hi_ref, lo_ref, real, imag)
    g0_ref[...] = g0
    m00 = inner(side(real, imag).astype(F32), g0)
    sums_ref[0:1, :] = m00
    send(out_ref, g0, rank)
    ride(out_ref, [m00], rank)


def row0(rank, c0_ref, hi_ref, lo_ref, back_ref, sums_ref, out_ref):
    real, imag = unpack(c0_ref, rank)
    next0 = apply_gram(hi_ref, lo_ref, real, imag)
    c0 = side(real, imag).astype(F32)
    n00 = inner(c0, next0)
    sums_ref[0:1, :] = n00
    sums_ref[1:2, :] = inner(back_ref[...], c0)
    sums_ref[2:3, :] = ridden(c0_ref, rank)[0:1]
    send(out_ref, next0, rank)
    ride(out_ref, [n00], rank)


def column1(
    rank, b1_ref, b0_ref, hi_ref, lo_ref, g0_ref, n0_ref, g1_ref, sums_ref, out_ref
):
    real, imag = unpack(b1_ref, rank)
    theta0 = ratio(ridden(b1_ref, rank)[0:1], n0_ref[2:3, :])
    wide = twice(theta0)
    g1 = apply_gram(hi_ref, lo_ref, real, imag) - wide * g0_ref[...]
    b0 = fields(b0_ref, rank)
    b1 = side(real, imag).astype(F32) - wide * b0
    g1_ref[...] = g1
    m11 = inner(b1, g1)
    sums_ref[0:1, :] = m11
    sums_ref[1:2, :] = inner(b0, g1)
    sums_ref[2:3, :] = theta0
    send(out_ref, g1, rank)
    ride(out_ref, [m11], rank)


def row1(rank, c1_ref, c0_ref, hi_ref, lo_ref, back_ref, sums_ref, out_ref):
    real, imag = unpack(c1_ref, rank)
    next1 = apply_gram(hi_ref, lo_ref, real, imag)
    c1 = side(real, imag).astype(F32)
    n11 = inner(c1, next1)
    n01 = inner(fields(c0_ref, rank), next1)
    sums_ref[0:1, :] = n11
    sums_ref[1:2, :] = n01
    sums_ref[2:3, :] = inner(back_ref[...], c1)
    sums_ref[3:4, :] = ridden(c1_ref, rank)[0:1]
    send(out_ref, next1, rank)
    ride(out_ref, [n11, n01], rank)


def column2(
    rank, b2_ref, b0_ref, b1_ref, hi_ref, lo_ref, g0_ref, g1_ref,
    damp_ref, m0_ref, n0_ref, m1_ref, n1_ref, sums_ref, out_ref
):
    real, imag = unpack(b2_ref, rank)
    came = ridden(b2_ref, rank)
    theta1 = ratio(came[0:1], n1_ref[3:4, :])
    phi = ratio(came[1:2], n0_ref[2:3, :])
    wide1, wide0 = twice(theta1), twice(phi)
    g2 = apply_gram(hi_ref, lo_ref, real, imag) - wide1 * g1_ref[...] - wide0 * g0_ref[...]
    send(out_ref, g2, rank)
    b0 = fields(b0_ref, rank)
    b1 = fields(b1_ref, rank) - twice(m1_ref[2:3, :]) * b0
    b2 = side(real, imag).astype(F32) - wide1 * b1 - wide0 * b0
    sums_ref[0:1, :] = inner(b0, g2)
    sums_ref[1:2, :] = inner(b1, g2)
    sums_ref[2:3, :] = inner(b2, g2)
    sums_ref[3:4, :] = theta1
    sums_ref[4:5, :] = phi
    damping = damp_ref[0:1, :]
    known = [
        n0_ref[0:1, :] + damping * m0_ref[0:1, :],
        n1_ref[1:2, :] + damping * m1_ref[1:2, :],
        n1_ref[0:1, :] + damping * m1_ref[0:1, :],
        n0_ref[1:2, :],
        n1_ref[2:3, :],
    ]
    rest = [row - row.astype(BF16).astype(F32) for row in known]
    ride(out_ref, known + rest, rank)


def row2(
    rank, share, here_ref, c2_ref, c0_ref, c1_ref, hi_ref, lo_ref, back_ref,
    damp_ref, m1_ref, m2_ref, out_ref, table_ref
):
    real, imag = unpack(c2_ref, rank)
    next2 = apply_gram(hi_ref, lo_ref, real, imag)
    damping = damp_ref[0:1, :]
    came = ridden(c2_ref, rank)
    table_ref[0:5, :] = came[0:5] + came[5:10]
    table_ref[5:6, :] = m1_ref[2:3, :]
    table_ref[6:8, :] = m2_ref[3:5, :]
    table_ref[8:9, :] = damping
    rows = [
        inner(fields(c0_ref, rank), next2) + damping * m2_ref[0:1, :],
        inner(fields(c1_ref, rank), next2) + damping * m2_ref[1:2, :],
        inner(side(real, imag).astype(F32), next2) + damping * m2_ref[2:3, :],
        inner(back_ref[...], side(real, imag).astype(F32)),
        table_ref[pl.ds(here_ref[0] * share, share), :],
    ]
    more = out_ref.shape[1] - LATE - share
    if more:
        rows.append(jnp.zeros((more, real.shape[1]), F32))
    block = jnp.concatenate(rows, axis=0)
    for p in range(out_ref.shape[0]):
        out_ref[p] = block


def forms(h, u, g, p, position, size, axis):
    def times(v):
        return [sum(h[a][b] * v[b] for b in range(size)) for a in range(size)]

    def along(a, b):
        return jnp.sum(sum(x * y for x, y in zip(a, b)), axis=axis, keepdims=True)

    hg, hp, hx = times(g), times(p), times(position)
    rest = [u[a] - hx[a] for a in range(size)]
    return along(g, hg), along(p, hg), along(p, hp), along(g, rest), along(p, rest)


def descend(h, u, theta0, theta1, phi, damping, axis):
    one = jnp.ones_like(theta0)
    a11 = jnp.sum(h[0][0], axis=axis, keepdims=True)
    b1 = jnp.sum(u[0], axis=axis, keepdims=True)
    alpha = b1 / (1.1 * a11)
    p = [alpha * one]
    x = [alpha * one]
    for size in (2, 3):
        zero = jnp.zeros_like(one)
        x = x + [zero]
        p = p + [zero]
        if size == 2:
            g = [one - (theta0 + damping) * x[0], -x[0]]
        else:
            g = [
                one - (theta0 + damping) * x[0] - phi * x[1],
                -x[0] - (theta1 + damping) * x[1],
                -x[1],
            ]
        a11, a12, a22, b1, b2 = forms(h, u, g, p, x, size, axis)
        first, second = 1.1 * a11, 1.1 * a22
        determinant = first * second - a12 * a12
        alpha = (b1 * second - a12 * b2) / determinant
        beta = (first * b2 - a12 * b1) / determinant
        p = [alpha * g[a] + beta * p[a] for a in range(size)]
        x = [x[a] + p[a] for a in range(size)]
    return x


def finish_kernel(
    rank, nfreq, share, mine_ref, data_hbm, left_hbm, recv_ref, right_ref,
    b0_ref, b1_ref, b2_ref, c0_ref, c1_ref, c2_ref, wave_hbm, res_hbm,
    table_ref, mix_ref, wave_ref, res_ref, data_ref, left_ref, sem
):
    left_copy = pltpu.make_async_copy(left_hbm, left_ref, sem.at[2])
    data_copy = pltpu.make_async_copy(data_hbm, data_ref, sem.at[3])
    left_copy.start()
    data_copy.start()
    ntile = recv_ref.shape[0] // nfreq
    for f in range(nfreq):
        total = recv_ref[f * ntile]
        for t in range(1, ntile):
            total = total + recv_ref[f * ntile + t]
        table_ref[0:LATE, f, :] = total[0:LATE]
        for q in range(EARLY):
            place = LATE + q % share
            table_ref[LATE + q, f : f + 1, :] = recv_ref[f * ntile + q // share, place : place + 1]
    h = [[None] * 3 for _ in range(3)]
    places = [(0, 0, 2), (1, 1, 2), (2, 2, 2), (4, 0, 0), (5, 0, 1), (6, 1, 1)]
    for place, a, b in places:
        h[a][b] = h[b][a] = table_ref[place]
    u = [table_ref[7], table_ref[8], table_ref[3]]
    theta0, theta1, phi, damping = [table_ref[9 + a] for a in range(4)]
    x = descend(h, u, theta0, theta1, phi, damping, 0)
    mix_ref[0] = x[0] - theta0 * x[1] + (theta0 * theta1 - phi) * x[2]
    mix_ref[1] = x[1] - theta1 * x[2]
    mix_ref[2] = x[2]
    mix_ref[3] = x[0]
    mix_ref[4] = x[1]
    mix_ref[5] = x[2]
    row = pl.ds(mine_ref[0], 1)

    def combine(refs, offset):
        total = None
        for k, ref in enumerate(refs):
            scale = mix_ref[offset + k, row, :]
            real, imag = unpack(ref, rank)
            term = (scale * real.astype(F32), scale * imag.astype(F32))
            total = term if total is None else (total[0] + term[0], total[1] + term[1])
        return total

    def plain(factor_ref, real, imag):
        (rh, rl), (ih, il) = split(real), split(imag)
        first, second = factor_ref[0], factor_ref[1]
        return (
            dot(first, side(rh, ih)) + dot(second, side(-ih, rh))
            + dot(first, side(rl, il)) + dot(second, side(-il, rl))
        )

    s = wave_ref.shape[2]
    wave = plain(right_ref, *combine([b0_ref, b1_ref, b2_ref], 0))
    wave_ref[0] = wave[:, :s]
    wave_ref[1] = wave[:, s:]
    wave_copy = pltpu.make_async_copy(wave_ref, wave_hbm, sem.at[0])
    wave_copy.start()
    mixed = combine([c0_ref, c1_ref, c2_ref], 3)
    left_copy.wait()
    data_copy.wait()
    image = plain(left_ref, *mixed)
    res_ref[0] = data_ref[0].astype(F32) - image[:, :s]
    res_ref[1] = data_ref[1].astype(F32) - image[:, s:]
    res_copy = pltpu.make_async_copy(res_ref, res_hbm, sem.at[1])
    res_copy.start()
    wave_copy.wait()
    res_copy.wait()


def lane_limits(limits, rank, width):
    lane = lax.broadcasted_iota(jnp.int32, (1, width), 1)
    limit = jnp.zeros((1, width), jnp.int32)
    for p, value in enumerate(limits):
        limit = jnp.where(lane >= p * rank, value, limit)
    return (lax.rem(lane, rank) < limit).astype(F32)


def packed_gram(real, imag):
    width = real.shape[1]
    both = jnp.concatenate([real, imag], axis=0)
    upper = dot_t(both, both)
    lower = dot_t(real, imag) - dot_t(imag, real)
    row = lax.broadcasted_iota(jnp.int32, (width, width), 0)
    column = lax.broadcasted_iota(jnp.int32, (width, width), 1)
    return jnp.where(row <= column, upper, lower).astype(BF16)


def unpacked_gram(packed):
    width = packed.shape[1]
    here = packed.astype(F32)
    there = here.T
    row = lax.broadcasted_iota(jnp.int32, (width, width), 0)
    column = lax.broadcasted_iota(jnp.int32, (width, width), 1)
    real = jnp.where(row <= column, here, there)
    imag = jnp.where(row > column, here, jnp.where(row < column, -there, 0.0))
    return real.astype(BF16), imag.astype(BF16)


def gather_start(
    rank, n, here_ref, mine_ref, ranks_hbm, data_hbm, left_hbm, right_hbm, *refs
):
    outs, (ranks_ref, data_ref, left_ref, right_ref, back_ref, sem) = refs[:-6], refs[-6:]
    pairs = [
        (left_hbm, left_ref), (data_hbm, data_ref), (ranks_hbm, ranks_ref),
        (right_hbm, right_ref),
    ]
    copies = [
        pltpu.make_async_copy(source, target, sem.at[k])
        for k, (source, target) in enumerate(pairs)
    ]
    for copy in copies:
        copy.start()
    for copy in copies[:3]:
        copy.wait()
    width = left_ref.shape[2]
    s = data_ref.shape[2]
    q = s // n
    here = here_ref[0]
    keep = lane_limits([ranks_ref[here, p] for p in range(n)], rank, width).astype(BF16)
    real, imag = left_ref[0] * keep, left_ref[1] * keep
    both = side(data_ref[0], data_ref[1])
    first, second = dot_t(both, real), dot_t(both, imag)
    back_ref[0] = (first[:s] + second[s:]).astype(BF16)
    back_ref[1] = (first[s:] - second[:s]).astype(BF16)
    gram = packed_gram(real, imag)
    for out in outs:
        out[0:width, :] = gram
    copies[3].wait()
    keep = lane_limits([ranks_ref[p, here] for p in range(n)], rank, width).astype(BF16)
    gram = packed_gram(right_ref[0] * keep, right_ref[1] * keep)
    z, x = lax.div(here, 2), lax.rem(here, 2)
    for k, out in enumerate(outs):
        out[width : 2 * width, :] = gram
        base = 2 * lax.rem(z + k, n // 2)
        for block, target in enumerate([base + 1 - x, base + x]):
            rows = pl.ds(pl.multiple_of(target * q, q), q)
            place = 2 * width + 2 * q * block
            out[place : place + q, :] = back_ref[0, rows, :]
            out[place + q : place + 2 * q, :] = back_ref[1, rows, :]


def swap_tiles(rank, source, target):
    n, rows, width = source.shape
    per = 128 // rank
    lane = lax.div(lax.broadcasted_iota(jnp.int32, (rows, 128), 1), rank)
    for g in range(n // per):
        for h in range(width // 128):
            ins = [source[per * g + a, :, 128 * h : 128 * h + 128] for a in range(per)]
            for b in range(per):
                out = None
                for a in range(per):
                    shift = (a - b) * rank % 128
                    piece = pltpu.roll(ins[a], shift, 1) if shift else ins[a]
                    out = piece if out is None else jnp.where(lane == a, piece, out)
                target[per * h + b, :, 128 * g : 128 * g + 128] = out


def apply_tiles(gram_ref, source, target):
    n, rows, _ = source.shape
    q = rows // 2
    for j in range(n):
        high, low = split(source[j])
        vector = jnp.concatenate([high, low], axis=0)
        real, imag = dot(vector, gram_ref[0, j]), dot(vector, gram_ref[1, j])
        real = real[:rows] + real[rows:]
        imag = imag[:rows] + imag[rows:]
        target[j, 0:q, :] = real[:q] + imag[q:]
        target[j, q:rows, :] = real[q:] - imag[:q]


def inner_tiles(first, second):
    n, rows, _ = first.shape
    total = first[0] * second[0]
    for j in range(1, n):
        total = total + first[j] * second[j]
    total = jnp.sum(total, axis=1, keepdims=True)
    return total[: rows // 2] + total[rows // 2 :]


def take_off(target, terms):
    scales = [jnp.concatenate([scale, scale], axis=0) for scale, _ in terms]
    for j in range(target.shape[0]):
        value = target[j]
        for scale, (_, other) in zip(scales, terms):
            value = value - scale * other[j]
        target[j] = value


def chain_kernel(
    rank, n, here_ref, freq_ref, *refs
):
    tiles = refs[:n]
    b_ref, c_ref, stats_ref, left_ref, right_ref, one_ref, two_ref = refs[n:]
    width = tiles[0].shape[1]
    q = stats_ref.shape[0]
    here = here_ref[0]
    z, x = lax.div(here, 2), lax.rem(here, 2)
    half = n // 2
    for k in range(half):
        base = 2 * lax.rem(z + half - k, half)
        for other in range(2):
            ref = tiles[k + half * other]
            at = pl.ds(base + (1 - x if other else x), 1)
            for place, gram_ref in enumerate((left_ref, right_ref)):
                real, imag = unpacked_gram(ref[place * width : (place + 1) * width, :])
                gram_ref[0, at] = real[None]
                gram_ref[1, at] = imag[None]
            start = 2 * width + (0 if other else 2 * q)
            one_ref[at] = ref[start : start + 2 * q, :].astype(F32)[None]
    b0, b1, b2 = b_ref.at[0], b_ref.at[1], b_ref.at[2]
    c0, c1, c2 = c_ref.at[0], c_ref.at[1], c_ref.at[2]
    swap_tiles(rank, one_ref, b0)
    apply_tiles(right_ref, b0, two_ref)
    m00 = inner_tiles(b0, two_ref)
    swap_tiles(rank, two_ref, c0)
    apply_tiles(left_ref, c0, one_ref)
    n00 = inner_tiles(c0, one_ref)
    theta0 = ratio(n00, m00)
    swap_tiles(rank, one_ref, b1)
    take_off(b1, [(theta0, b0)])
    apply_tiles(right_ref, b1, two_ref)
    m11 = inner_tiles(b1, two_ref)
    m01 = inner_tiles(b0, two_ref)
    swap_tiles(rank, two_ref, c1)
    apply_tiles(left_ref, c1, one_ref)
    n11 = inner_tiles(c1, one_ref)
    n01 = inner_tiles(c0, one_ref)
    theta1 = ratio(n11, m11)
    phi = ratio(n01, m00)
    swap_tiles(rank, one_ref, b2)
    take_off(b2, [(theta1, b1), (phi, b0)])
    apply_tiles(right_ref, b2, two_ref)
    m02 = inner_tiles(b0, two_ref)
    m12 = inner_tiles(b1, two_ref)
    m22 = inner_tiles(b2, two_ref)
    swap_tiles(rank, two_ref, c2)
    apply_tiles(left_ref, c2, one_ref)
    n02 = inner_tiles(c0, one_ref)
    n12 = inner_tiles(c1, one_ref)
    n22 = inner_tiles(c2, one_ref)
    damping = 0.1 + 0.9 * freq_ref[0].astype(F32) / 229.0
    values = [
        n00 + damping * m00, n01 + damping * m01, n02 + damping * m02,
        n11 + damping * m11, n12 + damping * m12, n22 + damping * m22,
        m00, m01, m02, theta0, theta1, phi,
    ]
    lane = lax.broadcasted_iota(jnp.int32, stats_ref.shape, 1)
    block = jnp.full(stats_ref.shape, damping)
    for place, value in enumerate(values):
        block = jnp.where(lane == place, value, block)
    stats_ref[...] = block


def mix_kernel(rank, stats_refs, b_ref, c_ref, out_ref):
    blocks = [ref[...] for ref in stats_refs]
    lane = lax.broadcasted_iota(jnp.int32, blocks[0].shape, 1)
    where_f = [lane == f for f in range(len(blocks))]

    def pick(place):
        value = jnp.zeros_like(blocks[0])
        for f, block in enumerate(blocks):
            shift = (f - place) % 128
            value = jnp.where(where_f[f], pltpu.roll(block, shift, 1) if shift else block, value)
        return value

    h = [[None] * 3 for _ in range(3)]
    for place, (a, b) in enumerate([(0, 0), (0, 1), (0, 2), (1, 1), (1, 2), (2, 2)]):
        h[a][b] = h[b][a] = pick(place)
    u = [pick(6), pick(7), pick(8)]
    theta0, theta1, phi, damping = pick(9), pick(10), pick(11), pick(12)
    x = descend(h, u, theta0, theta1, phi, damping, 1)
    n, rows, _ = b_ref.shape[1:]
    scales = []
    for value in x:
        own = jnp.sum(jnp.where(lane == 0, value, 0.0), axis=1, keepdims=True)
        scales.append(jnp.concatenate([own, own], axis=0))
    for j in range(n):
        for place, ref in enumerate((b_ref, c_ref)):
            value = scales[0] * ref[0, j] + scales[1] * ref[1, j] + scales[2] * ref[2, j]
            out_ref[j, place * rows : (place + 1) * rows, :] = value.astype(BF16)


def home_mix(rank, nfreq, data_hbm, left_hbm, right_hbm, *refs):
    stats_refs = refs[:nfreq]
    b_ref, c_ref, out_ref, data_ref, left_ref, right_ref, sem = refs[nfreq:]
    pairs = [(right_hbm, right_ref), (left_hbm, left_ref), (data_hbm, data_ref)]
    copies = [
        pltpu.make_async_copy(source, target, sem.at[k])
        for k, (source, target) in enumerate(pairs)
    ]
    for copy in copies:
        copy.start()
    mix_kernel(rank, stats_refs, b_ref, c_ref, out_ref)
    for copy in copies:
        copy.wait()


def dot_nt(a, b):
    return lax.dot_general(a, b, (((1,), (1,)), ((), ())), preferred_element_type=F32)


def home_kernel(
    rank, recv_ref, data_ref, left_ref, right_ref, wave_hbm, res_hbm, wave_ref, res_ref, sem
):
    n, rows, width = recv_ref.shape
    q = rows // 4
    s = n * q

    def plain(factor_ref, place):
        real = recv_ref[:, place * q : (place + 1) * q, :].reshape(s, width)
        imag = recv_ref[:, (place + 1) * q : (place + 2) * q, :].reshape(s, width)
        both = jnp.concatenate([real, imag], axis=0)
        first, second = dot_nt(factor_ref[0], both), dot_nt(factor_ref[1], both)
        return first[:, :s] - second[:, s:], first[:, s:] + second[:, :s]

    wave_ref[0], wave_ref[1] = plain(right_ref, 0)
    wave_copy = pltpu.make_async_copy(wave_ref, wave_hbm, sem.at[0])
    wave_copy.start()
    real, imag = plain(left_ref, 2)
    res_ref[0] = data_ref[0].astype(F32) - real
    res_ref[1] = data_ref[1].astype(F32) - imag
    res_copy = pltpu.make_async_copy(res_ref, res_hbm, sem.at[1])
    res_copy.start()
    wave_copy.wait()
    res_copy.wait()


def by_source(data, left, right, ranks, freq_index, ntile, nfreq, here, mine):
    width = left.shape[2]
    rank = width // ntile
    s = data.shape[2]
    q = s // ntile
    half = ntile // 2
    room = (16 << 20) + 64 * width * width

    def like(value):
        return jax.ShapeDtypeStruct(value.shape, value.dtype)

    def call(kernel, specs, args, outs, scratch=(), target=VMEM):
        return pl.pallas_call(
            kernel,
            out_shape=outs,
            in_specs=specs,
            out_specs=[target] * len(outs),
            scratch_shapes=scratch,
            compiler_params=pltpu.CompilerParams(vmem_limit_bytes=room),
        )(*args)

    def along(shift):
        return [
            (2 * z + x, 2 * ((z + shift) % half) + x) for z in range(half) for x in range(2)
        ]

    across = [(t, t ^ 1) for t in range(ntile)]
    packet = jax.ShapeDtypeStruct((2 * width + 4 * q, width), BF16)
    packets = call(
        functools.partial(gather_start, rank, ntile), [SMEM] * 2 + [HBM] * 4,
        (here, mine, ranks, data, left, right), (packet,) * half,
        [
            pltpu.SMEM(ranks.shape, jnp.int32),
            pltpu.VMEM(data.shape, BF16),
            pltpu.VMEM(left.shape, BF16),
            pltpu.VMEM(right.shape, BF16),
            pltpu.VMEM((2, s, width), BF16),
            pltpu.SemaphoreType.DMA((4,)),
        ],
    )
    same = [packets[0]] + [
        lax.ppermute(packets[k], "tcol", along(k)) for k in range(1, half)
    ]
    other = [lax.ppermute(value, "tcol", across) for value in same]
    vectors = jax.ShapeDtypeStruct((3, ntile, 2 * q, width), F32)
    grams = pltpu.VMEM((2, ntile, width, width), BF16)
    vector = pltpu.VMEM((ntile, 2 * q, width), F32)
    b, c, stats = call(
        functools.partial(chain_kernel, rank, ntile), [SMEM] * 2 + [VMEM] * ntile,
        (here, freq_index, *same, *other),
        (vectors, vectors, jax.ShapeDtypeStruct((q, 128), F32)),
        [grams, grams, vector, vector],
    )
    gathered = stats[None]
    step = 1
    while step < nfreq:
        pairs = [(f, f ^ step) for f in range(nfreq)]
        gathered = jnp.concatenate([gathered, lax.ppermute(gathered, "freq", pairs)], axis=0)
        step *= 2
    out, data_in, left_in, right_in = call(
        functools.partial(home_mix, rank, nfreq), [HBM] * 3 + [VMEM] * (nfreq + 2),
        (data, left, right, *[gathered[f] for f in range(nfreq)], b, c),
        (
            jax.ShapeDtypeStruct((ntile, 4 * q, width), BF16),
            like(data), like(left), like(right),
        ),
        [pltpu.SemaphoreType.DMA((3,))],
    )
    back = lax.all_to_all(out, "tcol", 0, 0, tiled=True)
    shape = jax.ShapeDtypeStruct(data.shape, F32)
    return call(
        functools.partial(home_kernel, rank), [VMEM] * 4, (back, data_in, left_in, right_in),
        (shape, shape),
        [
            pltpu.VMEM(shape.shape, F32),
            pltpu.VMEM(shape.shape, F32),
            pltpu.SemaphoreType.DMA((2,)),
        ],
        HBM,
    )


def body(data, left_factor, right_factor, ranks, freq_index):
    ntile = lax.axis_size("tcol")
    nfreq = lax.axis_size("freq")
    here = lax.axis_index("tcol").reshape(1)
    mine = lax.axis_index("freq").reshape(1)
    data, left, right, ranks = data[0], left_factor[0], right_factor[0], ranks[0]
    data, left, right, ranks = [
        pltpu.with_memory_space_constraint(value, pltpu.HBM)
        for value in (data, left, right, ranks)
    ]
    width = left.shape[2]
    rank = width // ntile
    s = data.shape[2]
    fits = s % (16 * ntile) == 0 and width % 128 == 0 and 128 % rank == 0
    if fits and nfreq & (nfreq - 1) == 0 and ntile * width * width <= 1 << 20:
        wave, res = by_source(data, left, right, ranks, freq_index, ntile, nfreq, here, mine)
        return wave[None], res[None]
    share = -(-EARLY // ntile)
    height = -(-(LATE + share) // 8) * 8
    field = jax.ShapeDtypeStruct((width, 2 * s), F32)
    sums = jax.ShapeDtypeStruct((8, s), F32)
    bare = jax.ShapeDtypeStruct((ntile, 2 * rank, s), BF16)
    message = jax.ShapeDtypeStruct((ntile, 2 * rank + RIDE, s), BF16)
    gram = jax.ShapeDtypeStruct((width, 2 * width), BF16)
    room = (8 << 20) + 24 * width * width

    def like(value):
        return jax.ShapeDtypeStruct(value.shape, value.dtype)

    def call(kernel, specs, args, outs, scratch=(), target=VMEM):
        return pl.pallas_call(
            functools.partial(kernel, rank),
            out_shape=outs,
            in_specs=specs,
            out_specs=[target] * len(outs),
            scratch_shapes=scratch,
            compiler_params=pltpu.CompilerParams(vmem_limit_bytes=room),
        )(*args)

    def step(kernel, args, outs):
        return call(kernel, [VMEM] * len(args), args, outs)

    def exchange(value):
        return lax.all_to_all(value, "tcol", 0, 0, tiled=True)

    vright, back, damp, out, uhi, ulo, vhi, vlo = call(
        start_kernel, [SMEM] * 2 + [HBM] * 5, (here, mine, ranks, freq_index, data, left, right),
        (like(right), field, sums, bare, gram, gram, gram, gram),
        [
            pltpu.SMEM(ranks.shape, jnp.int32),
            pltpu.SMEM(freq_index.shape, jnp.int32),
            pltpu.VMEM(data.shape, BF16),
            pltpu.VMEM(left.shape, BF16),
            pltpu.SemaphoreType.DMA((5,)),
        ],
    )
    b0 = exchange(out)
    g0, m0, out = step(column0, (b0, vhi, vlo), (field, sums, message))
    c0 = exchange(out)
    n0, out = step(row0, (c0, uhi, ulo, back), (sums, message))
    b1 = exchange(out)
    g1, m1, out = step(column1, (b1, b0, vhi, vlo, g0, n0), (field, sums, message))
    c1 = exchange(out)
    n1, out = step(row1, (c1, c0, uhi, ulo, back), (sums, message))
    b2 = exchange(out)
    m2, out = step(
        column2, (b2, b0, b1, vhi, vlo, g0, g1, damp, m0, n0, m1, n1), (sums, message)
    )
    c2 = exchange(out)
    args = (here, c2, c0, c1, uhi, ulo, back, damp, m1, m2)
    (out,) = call(
        lambda rank, *refs: row2(rank, share, *refs), [SMEM] + [VMEM] * 9, args,
        (jax.ShapeDtypeStruct((nfreq * ntile, height, s), F32),),
        [pltpu.VMEM((max(16, ntile * share), s), F32)],
    )
    everyone = lax.all_to_all(out, ("freq", "tcol"), 0, 0, tiled=True)
    shape = jax.ShapeDtypeStruct(data.shape, F32)
    wave, res = call(
        lambda rank, *refs: finish_kernel(rank, nfreq, share, *refs),
        [SMEM, HBM, HBM] + [VMEM] * 8,
        (mine, data, left, everyone, vright, b0, b1, b2, c0, c1, c2), (shape, shape),
        [
            pltpu.VMEM((LATE + EARLY, nfreq, s), F32),
            pltpu.VMEM((6, nfreq, s), F32),
            pltpu.VMEM(shape.shape, F32),
            pltpu.VMEM(shape.shape, F32),
            pltpu.VMEM(data.shape, BF16),
            pltpu.VMEM(left.shape, BF16),
            pltpu.SemaphoreType.DMA((4,)),
        ],
        HBM,
    )
    return wave[None], res[None]


def solution(mesh):
    in_specs = (
        P("freq", None, "tcol", None),
        P("freq", None, "tcol", None),
        P("freq", None, "tcol", None),
        P("freq", None, None),
        P("freq"),
    )
    out_specs = (P("freq", None, "tcol", None), P("freq", None, "tcol", None))
    return jax.shard_map(body, mesh=mesh, in_specs=in_specs, out_specs=out_specs, check_vma=False)
```

```python
import functools

import jax
import jax.numpy as jnp
from jax import lax
from jax.experimental import pallas as pl
from jax.experimental.pallas import tpu as pltpu
from jax.sharding import PartitionSpec as P


RIDE = 16
LATE = 4
EARLY = 9
VMEM = pl.BlockSpec(memory_space=pltpu.VMEM)
SMEM = pl.BlockSpec(memory_space=pltpu.SMEM)
HBM = pl.BlockSpec(memory_space=pltpu.HBM)
F32 = jnp.float32
BF16 = jnp.bfloat16


def dot(a, b):
    return jnp.dot(a, b, preferred_element_type=F32)


def dot_t(a, b):
    return lax.dot_general(a, b, (((0,), (0,)), ((), ())), preferred_element_type=F32)


def side(real, imag):
    return jnp.concatenate([real, imag], axis=1)


def split(value):
    high = value.astype(BF16)
    return high, (value - high.astype(F32)).astype(BF16)


def unpack(ref, rank):
    n = ref.shape[0]
    real = ref[:, 0:rank, :].reshape(n * rank, ref.shape[2])
    imag = ref[:, rank : 2 * rank, :].reshape(n * rank, ref.shape[2])
    return real, imag


def fields(ref, rank):
    return side(*unpack(ref, rank)).astype(F32)


def send(out_ref, value, rank):
    s = out_ref.shape[2]
    for p in range(out_ref.shape[0]):
        rows = value[p * rank : (p + 1) * rank].astype(BF16)
        out_ref[p, 0:rank, :] = rows[:, :s]
        out_ref[p, rank : 2 * rank, :] = rows[:, s:]


def ride(out_ref, rows, rank):
    rows = rows + [jnp.zeros_like(rows[0])] * (RIDE - len(rows))
    block = jnp.concatenate(rows, axis=0).astype(BF16)
    for p in range(out_ref.shape[0]):
        out_ref[p, 2 * rank : 2 * rank + RIDE, :] = block


def ridden(ref, rank):
    total = ref[0, 2 * rank : 2 * rank + RIDE, :].astype(F32)
    for p in range(1, ref.shape[0]):
        total = total + ref[p, 2 * rank : 2 * rank + RIDE, :].astype(F32)
    return total


def inner(a, b):
    both = jnp.sum(a * b, axis=0, keepdims=True)
    s = both.shape[1] // 2
    return both[:, :s] + both[:, s:]


def twice(row):
    return jnp.concatenate([row, row], axis=1)


def ratio(top, bottom):
    safe = bottom > 0
    return jnp.where(safe, top / jnp.where(safe, bottom, 1.0), 0.0)


def apply_gram(hi_ref, lo_ref, real, imag):
    vector = jnp.concatenate([side(real, imag), side(-imag, real)], axis=0)
    return dot(hi_ref[...], vector) + dot(lo_ref[...], vector)


def make_gram(factor_ref, hi_ref, lo_ref, limits):
    real, imag = factor_ref[0], factor_ref[1]
    width = real.shape[1]
    rank = width // len(limits)
    level = lax.broadcasted_iota(jnp.int32, (rank, width), 0)

    def put(value, place):
        for p, limit in enumerate(limits):
            rows = slice(p * rank, (p + 1) * rank)
            high, low = split(jnp.where(level < limit, value[rows], 0.0))
            hi_ref[rows, place : place + width] = high
            lo_ref[rows, place : place + width] = low

    put(dot_t(real, real) + dot_t(imag, imag), 0)
    put(dot_t(real, imag) - dot_t(imag, real), width)


def start_kernel(
    rank, here_ref, mine_ref, ranks_hbm, freq_hbm, data_hbm, left_hbm, right_hbm,
    right_ref, back_ref, sums_ref, out_ref, uhi_ref, ulo_ref, vhi_ref, vlo_ref,
    ranks_ref, freq_ref, data_ref, left_ref, sem
):
    n = out_ref.shape[0]
    s = out_ref.shape[2]
    pairs = [
        (left_hbm, left_ref), (data_hbm, data_ref), (ranks_hbm, ranks_ref),
        (freq_hbm, freq_ref), (right_hbm, right_ref),
    ]
    copies = [
        pltpu.make_async_copy(source, target, sem.at[k])
        for k, (source, target) in enumerate(pairs)
    ]
    for copy in copies:
        copy.start()
    for copy in copies[:4]:
        copy.wait()
    here = here_ref[0]
    row_limits = [ranks_ref[here, p] for p in range(n)]
    column_limits = [ranks_ref[p, here] for p in range(n)]
    damping = 0.1 + 0.9 * freq_ref[0].astype(F32) / 229.0
    sums_ref[...] = jnp.full(sums_ref.shape, damping)
    real, imag = data_ref[0], data_ref[1]
    back = dot_t(left_ref[0], side(real, imag)) + dot_t(left_ref[1], side(imag, -real))
    level = lax.broadcasted_iota(jnp.int32, (rank, 2 * s), 0)
    back = jnp.concatenate(
        [
            jnp.where(level < limit, back[p * rank : (p + 1) * rank], 0.0)
            for p, limit in enumerate(row_limits)
        ],
        axis=0,
    )
    back_ref[...] = back
    send(out_ref, back, rank)
    make_gram(left_ref, uhi_ref, ulo_ref, row_limits)
    copies[4].wait()
    make_gram(right_ref, vhi_ref, vlo_ref, column_limits)


def column0(rank, b0_ref, hi_ref, lo_ref, g0_ref, sums_ref, out_ref):
    real, imag = unpack(b0_ref, rank)
    g0 = apply_gram(hi_ref, lo_ref, real, imag)
    g0_ref[...] = g0
    m00 = inner(side(real, imag).astype(F32), g0)
    sums_ref[0:1, :] = m00
    send(out_ref, g0, rank)
    ride(out_ref, [m00], rank)


def row0(rank, c0_ref, hi_ref, lo_ref, back_ref, sums_ref, out_ref):
    real, imag = unpack(c0_ref, rank)
    next0 = apply_gram(hi_ref, lo_ref, real, imag)
    c0 = side(real, imag).astype(F32)
    n00 = inner(c0, next0)
    sums_ref[0:1, :] = n00
    sums_ref[1:2, :] = inner(back_ref[...], c0)
    sums_ref[2:3, :] = ridden(c0_ref, rank)[0:1]
    send(out_ref, next0, rank)
    ride(out_ref, [n00], rank)


def column1(
    rank, b1_ref, b0_ref, hi_ref, lo_ref, g0_ref, n0_ref, g1_ref, sums_ref, out_ref
):
    real, imag = unpack(b1_ref, rank)
    theta0 = ratio(ridden(b1_ref, rank)[0:1], n0_ref[2:3, :])
    wide = twice(theta0)
    g1 = apply_gram(hi_ref, lo_ref, real, imag) - wide * g0_ref[...]
    b0 = fields(b0_ref, rank)
    b1 = side(real, imag).astype(F32) - wide * b0
    g1_ref[...] = g1
    m11 = inner(b1, g1)
    sums_ref[0:1, :] = m11
    sums_ref[1:2, :] = inner(b0, g1)
    sums_ref[2:3, :] = theta0
    send(out_ref, g1, rank)
    ride(out_ref, [m11], rank)


def row1(rank, c1_ref, c0_ref, hi_ref, lo_ref, back_ref, sums_ref, out_ref):
    real, imag = unpack(c1_ref, rank)
    next1 = apply_gram(hi_ref, lo_ref, real, imag)
    c1 = side(real, imag).astype(F32)
    n11 = inner(c1, next1)
    n01 = inner(fields(c0_ref, rank), next1)
    sums_ref[0:1, :] = n11
    sums_ref[1:2, :] = n01
    sums_ref[2:3, :] = inner(back_ref[...], c1)
    sums_ref[3:4, :] = ridden(c1_ref, rank)[0:1]
    send(out_ref, next1, rank)
    ride(out_ref, [n11, n01], rank)


def column2(
    rank, b2_ref, b0_ref, b1_ref, hi_ref, lo_ref, g0_ref, g1_ref,
    damp_ref, m0_ref, n0_ref, m1_ref, n1_ref, sums_ref, out_ref
):
    real, imag = unpack(b2_ref, rank)
    came = ridden(b2_ref, rank)
    theta1 = ratio(came[0:1], n1_ref[3:4, :])
    phi = ratio(came[1:2], n0_ref[2:3, :])
    wide1, wide0 = twice(theta1), twice(phi)
    g2 = apply_gram(hi_ref, lo_ref, real, imag) - wide1 * g1_ref[...] - wide0 * g0_ref[...]
    send(out_ref, g2, rank)
    b0 = fields(b0_ref, rank)
    b1 = fields(b1_ref, rank) - twice(m1_ref[2:3, :]) * b0
    b2 = side(real, imag).astype(F32) - wide1 * b1 - wide0 * b0
    sums_ref[0:1, :] = inner(b0, g2)
    sums_ref[1:2, :] = inner(b1, g2)
    sums_ref[2:3, :] = inner(b2, g2)
    sums_ref[3:4, :] = theta1
    sums_ref[4:5, :] = phi
    damping = damp_ref[0:1, :]
    known = [
        n0_ref[0:1, :] + damping * m0_ref[0:1, :],
        n1_ref[1:2, :] + damping * m1_ref[1:2, :],
        n1_ref[0:1, :] + damping * m1_ref[0:1, :],
        n0_ref[1:2, :],
        n1_ref[2:3, :],
    ]
    rest = [row - row.astype(BF16).astype(F32) for row in known]
    ride(out_ref, known + rest, rank)


def row2(
    rank, share, here_ref, c2_ref, c0_ref, c1_ref, hi_ref, lo_ref, back_ref,
    damp_ref, m1_ref, m2_ref, out_ref, table_ref
):
    real, imag = unpack(c2_ref, rank)
    next2 = apply_gram(hi_ref, lo_ref, real, imag)
    damping = damp_ref[0:1, :]
    came = ridden(c2_ref, rank)
    table_ref[0:5, :] = came[0:5] + came[5:10]
    table_ref[5:6, :] = m1_ref[2:3, :]
    table_ref[6:8, :] = m2_ref[3:5, :]
    table_ref[8:9, :] = damping
    rows = [
        inner(fields(c0_ref, rank), next2) + damping * m2_ref[0:1, :],
        inner(fields(c1_ref, rank), next2) + damping * m2_ref[1:2, :],
        inner(side(real, imag).astype(F32), next2) + damping * m2_ref[2:3, :],
        inner(back_ref[...], side(real, imag).astype(F32)),
        table_ref[pl.ds(here_ref[0] * share, share), :],
    ]
    more = out_ref.shape[1] - LATE - share
    if more:
        rows.append(jnp.zeros((more, real.shape[1]), F32))
    block = jnp.concatenate(rows, axis=0)
    for p in range(out_ref.shape[0]):
        out_ref[p] = block


def forms(h, u, g, p, position, size, axis):
    def times(v):
        return [sum(h[a][b] * v[b] for b in range(size)) for a in range(size)]

    def along(a, b):
        return jnp.sum(sum(x * y for x, y in zip(a, b)), axis=axis, keepdims=True)

    hg, hp, hx = times(g), times(p), times(position)
    rest = [u[a] - hx[a] for a in range(size)]
    return along(g, hg), along(p, hg), along(p, hp), along(g, rest), along(p, rest)


def descend(h, u, theta0, theta1, phi, damping, axis):
    one = jnp.ones_like(theta0)
    a11 = jnp.sum(h[0][0], axis=axis, keepdims=True)
    b1 = jnp.sum(u[0], axis=axis, keepdims=True)
    alpha = b1 / (1.1 * a11)
    p = [alpha * one]
    x = [alpha * one]
    for size in (2, 3):
        zero = jnp.zeros_like(one)
        x = x + [zero]
        p = p + [zero]
        if size == 2:
            g = [one - (theta0 + damping) * x[0], -x[0]]
        else:
            g = [
                one - (theta0 + damping) * x[0] - phi * x[1],
                -x[0] - (theta1 + damping) * x[1],
                -x[1],
            ]
        a11, a12, a22, b1, b2 = forms(h, u, g, p, x, size, axis)
        first, second = 1.1 * a11, 1.1 * a22
        determinant = first * second - a12 * a12
        alpha = (b1 * second - a12 * b2) / determinant
        beta = (first * b2 - a12 * b1) / determinant
        p = [alpha * g[a] + beta * p[a] for a in range(size)]
        x = [x[a] + p[a] for a in range(size)]
    return x


def finish_kernel(
    rank, nfreq, share, mine_ref, data_hbm, left_hbm, recv_ref, right_ref,
    b0_ref, b1_ref, b2_ref, c0_ref, c1_ref, c2_ref, wave_hbm, res_hbm,
    table_ref, mix_ref, wave_ref, res_ref, data_ref, left_ref, sem
):
    left_copy = pltpu.make_async_copy(left_hbm, left_ref, sem.at[2])
    data_copy = pltpu.make_async_copy(data_hbm, data_ref, sem.at[3])
    left_copy.start()
    data_copy.start()
    ntile = recv_ref.shape[0] // nfreq
    for f in range(nfreq):
        total = recv_ref[f * ntile]
        for t in range(1, ntile):
            total = total + recv_ref[f * ntile + t]
        table_ref[0:LATE, f, :] = total[0:LATE]
        for q in range(EARLY):
            place = LATE + q % share
            table_ref[LATE + q, f : f + 1, :] = recv_ref[f * ntile + q // share, place : place + 1]
    h = [[None] * 3 for _ in range(3)]
    places = [(0, 0, 2), (1, 1, 2), (2, 2, 2), (4, 0, 0), (5, 0, 1), (6, 1, 1)]
    for place, a, b in places:
        h[a][b] = h[b][a] = table_ref[place]
    u = [table_ref[7], table_ref[8], table_ref[3]]
    theta0, theta1, phi, damping = [table_ref[9 + a] for a in range(4)]
    x = descend(h, u, theta0, theta1, phi, damping, 0)
    mix_ref[0] = x[0] - theta0 * x[1] + (theta0 * theta1 - phi) * x[2]
    mix_ref[1] = x[1] - theta1 * x[2]
    mix_ref[2] = x[2]
    mix_ref[3] = x[0]
    mix_ref[4] = x[1]
    mix_ref[5] = x[2]
    row = pl.ds(mine_ref[0], 1)

    def combine(refs, offset):
        total = None
        for k, ref in enumerate(refs):
            scale = mix_ref[offset + k, row, :]
            real, imag = unpack(ref, rank)
            term = (scale * real.astype(F32), scale * imag.astype(F32))
            total = term if total is None else (total[0] + term[0], total[1] + term[1])
        return total

    def plain(factor_ref, real, imag):
        (rh, rl), (ih, il) = split(real), split(imag)
        first, second = factor_ref[0], factor_ref[1]
        return (
            dot(first, side(rh, ih)) + dot(second, side(-ih, rh))
            + dot(first, side(rl, il)) + dot(second, side(-il, rl))
        )

    s = wave_ref.shape[2]
    wave = plain(right_ref, *combine([b0_ref, b1_ref, b2_ref], 0))
    wave_ref[0] = wave[:, :s]
    wave_ref[1] = wave[:, s:]
    wave_copy = pltpu.make_async_copy(wave_ref, wave_hbm, sem.at[0])
    wave_copy.start()
    mixed = combine([c0_ref, c1_ref, c2_ref], 3)
    left_copy.wait()
    data_copy.wait()
    image = plain(left_ref, *mixed)
    res_ref[0] = data_ref[0].astype(F32) - image[:, :s]
    res_ref[1] = data_ref[1].astype(F32) - image[:, s:]
    res_copy = pltpu.make_async_copy(res_ref, res_hbm, sem.at[1])
    res_copy.start()
    wave_copy.wait()
    res_copy.wait()


def lane_limits(limits, rank, width):
    lane = lax.broadcasted_iota(jnp.int32, (1, width), 1)
    limit = jnp.zeros((1, width), jnp.int32)
    for p, value in enumerate(limits):
        limit = jnp.where(lane >= p * rank, value, limit)
    return (lax.rem(lane, rank) < limit).astype(F32)


def packed_gram(real, imag):
    width = real.shape[1]
    both = jnp.concatenate([real, imag], axis=0)
    upper = dot_t(both, both)
    lower = dot_t(real, imag) - dot_t(imag, real)
    row = lax.broadcasted_iota(jnp.int32, (width, width), 0)
    column = lax.broadcasted_iota(jnp.int32, (width, width), 1)
    return jnp.where(row <= column, upper, lower).astype(BF16)


def unpacked_gram(packed):
    width = packed.shape[1]
    here = packed.astype(F32)
    there = here.T
    row = lax.broadcasted_iota(jnp.int32, (width, width), 0)
    column = lax.broadcasted_iota(jnp.int32, (width, width), 1)
    real = jnp.where(row <= column, here, there)
    imag = jnp.where(row > column, here, jnp.where(row < column, -there, 0.0))
    return real.astype(BF16), imag.astype(BF16)


def offsets(half):
    return sorted(range(1, half), key=lambda k: (min(k, half - k), k))


def tile_parts(refs, half):
    whole = refs[0].shape[0] - refs[0].shape[1]
    parts = {0: (refs[0], refs[0], whole)}
    order = offsets(half)
    for place, k in enumerate(order[:-1]):
        parts[k] = (refs[1 + place], refs[1 + place], whole)
    parts[order[-1]] = (refs[-2], refs[-1], 0)
    return [parts[k] for k in range(half)]


def gather_start(
    rank, n, here_ref, mine_ref, ranks_hbm, data_hbm, left_hbm, right_hbm, *refs
):
    ranks_ref, data_ref, left_ref, right_ref, back_ref, sem = refs[-6:]
    half = n // 2
    packets = tile_parts(refs[: half + 1], half)
    pairs = [
        (left_hbm, left_ref), (data_hbm, data_ref), (ranks_hbm, ranks_ref),
        (right_hbm, right_ref),
    ]
    copies = [
        pltpu.make_async_copy(source, target, sem.at[k])
        for k, (source, target) in enumerate(pairs)
    ]
    for copy in copies:
        copy.start()
    for copy in copies[:3]:
        copy.wait()
    width = left_ref.shape[2]
    s = data_ref.shape[2]
    q = s // n
    here = here_ref[0]
    keep = lane_limits([ranks_ref[here, p] for p in range(n)], rank, width).astype(BF16)
    real, imag = left_ref[0] * keep, left_ref[1] * keep
    both = side(data_ref[0], data_ref[1])
    first, second = dot_t(both, real), dot_t(both, imag)
    back_ref[0] = (first[:s] + second[s:]).astype(BF16)
    back_ref[1] = (first[s:] - second[:s]).astype(BF16)
    gram = packed_gram(real, imag)
    for first, _, _ in packets:
        first[0:width, :] = gram
    copies[3].wait()
    keep = lane_limits([ranks_ref[p, here] for p in range(n)], rank, width).astype(BF16)
    gram = packed_gram(right_ref[0] * keep, right_ref[1] * keep)
    z, x = lax.div(here, 2), lax.rem(here, 2)
    for k, (first, second, place) in enumerate(packets):
        second[place : place + width, :] = gram
        base = 2 * lax.rem(z + k, half)
        for block, target in enumerate([base + 1 - x, base + x]):
            rows = pl.ds(pl.multiple_of(target * q, q), q)
            place = width + 2 * q * block
            first[place : place + q, :] = back_ref[0, rows, :]
            first[place + q : place + 2 * q, :] = back_ref[1, rows, :]


def swap_tiles(rank, source, target):
    n, rows, width = source.shape
    per = 128 // rank
    lane = lax.div(lax.broadcasted_iota(jnp.int32, (rows, 128), 1), rank)
    for g in range(n // per):
        for h in range(width // 128):
            ins = [source[per * g + a, :, 128 * h : 128 * h + 128] for a in range(per)]
            for b in range(per):
                out = None
                for a in range(per):
                    shift = (a - b) * rank % 128
                    piece = pltpu.roll(ins[a], shift, 1) if shift else ins[a]
                    out = piece if out is None else jnp.where(lane == a, piece, out)
                target[per * h + b, :, 128 * g : 128 * g + 128] = out


def apply_tiles(gram_ref, source, target):
    n, rows, _ = source.shape
    q = rows // 2
    for j in range(n):
        high, low = split(source[j])
        vector = jnp.concatenate([high, low], axis=0)
        real, imag = dot(vector, gram_ref[0, j]), dot(vector, gram_ref[1, j])
        real = real[:rows] + real[rows:]
        imag = imag[:rows] + imag[rows:]
        target[j, 0:q, :] = real[:q] + imag[q:]
        target[j, q:rows, :] = real[q:] - imag[:q]


def inner_tiles(first, second):
    n, rows, _ = first.shape
    total = first[0] * second[0]
    for j in range(1, n):
        total = total + first[j] * second[j]
    total = jnp.sum(total, axis=1, keepdims=True)
    return total[: rows // 2] + total[rows // 2 :]


def take_off(target, terms):
    scales = [jnp.concatenate([scale, scale], axis=0) for scale, _ in terms]
    for j in range(target.shape[0]):
        value = target[j]
        for scale, (_, other) in zip(scales, terms):
            value = value - scale * other[j]
        target[j] = value


def chain_kernel(
    rank, n, here_ref, freq_ref, *refs
):
    half = n // 2
    tiles = [tile_parts(refs[: half + 1], half), tile_parts(refs[half + 1 : n + 2], half)]
    b_ref, c_ref, stats_ref, left_ref, right_ref, one_ref, two_ref = refs[n + 2 :]
    width = refs[0].shape[1]
    q = stats_ref.shape[0]
    here = here_ref[0]
    z, x = lax.div(here, 2), lax.rem(here, 2)
    for k in range(half):
        base = 2 * lax.rem(z + half - k, half)
        for other in range(2):
            first, second, place = tiles[other][k]
            at = pl.ds(base + (1 - x if other else x), 1)
            grams = (first[0:width, :], second[place : place + width, :])
            for packed, gram_ref in zip(grams, (left_ref, right_ref)):
                real, imag = unpacked_gram(packed)
                gram_ref[0, at] = real[None]
                gram_ref[1, at] = imag[None]
            start = width + (0 if other else 2 * q)
            one_ref[at] = first[start : start + 2 * q, :].astype(F32)[None]
    b0, b1, b2 = b_ref.at[0], b_ref.at[1], b_ref.at[2]
    c0, c1, c2 = c_ref.at[0], c_ref.at[1], c_ref.at[2]
    swap_tiles(rank, one_ref, b0)
    apply_tiles(right_ref, b0, two_ref)
    m00 = inner_tiles(b0, two_ref)
    swap_tiles(rank, two_ref, c0)
    apply_tiles(left_ref, c0, one_ref)
    n00 = inner_tiles(c0, one_ref)
    theta0 = ratio(n00, m00)
    swap_tiles(rank, one_ref, b1)
    take_off(b1, [(theta0, b0)])
    apply_tiles(right_ref, b1, two_ref)
    m11 = inner_tiles(b1, two_ref)
    m01 = inner_tiles(b0, two_ref)
    swap_tiles(rank, two_ref, c1)
    apply_tiles(left_ref, c1, one_ref)
    n11 = inner_tiles(c1, one_ref)
    n01 = inner_tiles(c0, one_ref)
    theta1 = ratio(n11, m11)
    phi = ratio(n01, m00)
    swap_tiles(rank, one_ref, b2)
    take_off(b2, [(theta1, b1), (phi, b0)])
    apply_tiles(right_ref, b2, two_ref)
    m02 = inner_tiles(b0, two_ref)
    m12 = inner_tiles(b1, two_ref)
    m22 = inner_tiles(b2, two_ref)
    swap_tiles(rank, two_ref, c2)
    apply_tiles(left_ref, c2, one_ref)
    n02 = inner_tiles(c0, one_ref)
    n12 = inner_tiles(c1, one_ref)
    n22 = inner_tiles(c2, one_ref)
    damping = 0.1 + 0.9 * freq_ref[0].astype(F32) / 229.0
    values = [
        n00 + damping * m00, n01 + damping * m01, n02 + damping * m02,
        n11 + damping * m11, n12 + damping * m12, n22 + damping * m22,
        m00, m01, m02, theta0, theta1, phi,
    ]
    lane = lax.broadcasted_iota(jnp.int32, stats_ref.shape, 1)
    block = jnp.full(stats_ref.shape, damping)
    for place, value in enumerate(values):
        block = jnp.where(lane == place, value, block)
    stats_ref[...] = block


def mix_kernel(rank, stats_refs, b_ref, c_ref, out_ref):
    blocks = [ref[...] for ref in stats_refs]
    lane = lax.broadcasted_iota(jnp.int32, blocks[0].shape, 1)
    where_f = [lane == f for f in range(len(blocks))]

    def pick(place):
        value = jnp.zeros_like(blocks[0])
        for f, block in enumerate(blocks):
            shift = (f - place) % 128
            value = jnp.where(where_f[f], pltpu.roll(block, shift, 1) if shift else block, value)
        return value

    h = [[None] * 3 for _ in range(3)]
    for place, (a, b) in enumerate([(0, 0), (0, 1), (0, 2), (1, 1), (1, 2), (2, 2)]):
        h[a][b] = h[b][a] = pick(place)
    u = [pick(6), pick(7), pick(8)]
    theta0, theta1, phi, damping = pick(9), pick(10), pick(11), pick(12)
    x = descend(h, u, theta0, theta1, phi, damping, 1)
    n, rows, _ = b_ref.shape[1:]
    scales = []
    for value in x:
        own = jnp.sum(jnp.where(lane == 0, value, 0.0), axis=1, keepdims=True)
        scales.append(jnp.concatenate([own, own], axis=0))
    for j in range(n):
        for place, ref in enumerate((b_ref, c_ref)):
            value = scales[0] * ref[0, j] + scales[1] * ref[1, j] + scales[2] * ref[2, j]
            out_ref[j, place * rows : (place + 1) * rows, :] = value.astype(BF16)


def home_mix(rank, nfreq, data_hbm, left_hbm, right_hbm, *refs):
    stats_refs = refs[:nfreq]
    b_ref, c_ref, out_ref, data_ref, left_ref, right_ref, sem = refs[nfreq:]
    pairs = [(right_hbm, right_ref), (left_hbm, left_ref), (data_hbm, data_ref)]
    copies = [
        pltpu.make_async_copy(source, target, sem.at[k])
        for k, (source, target) in enumerate(pairs)
    ]
    for copy in copies:
        copy.start()
    mix_kernel(rank, stats_refs, b_ref, c_ref, out_ref)
    for copy in copies:
        copy.wait()


def dot_nt(a, b):
    return lax.dot_general(a, b, (((1,), (1,)), ((), ())), preferred_element_type=F32)


def home_kernel(
    rank, recv_ref, data_ref, left_ref, right_ref, wave_hbm, res_hbm, wave_ref, res_ref, sem
):
    n, rows, width = recv_ref.shape
    q = rows // 4
    s = n * q

    def plain(factor_ref, place):
        real = recv_ref[:, place * q : (place + 1) * q, :].reshape(s, width)
        imag = recv_ref[:, (place + 1) * q : (place + 2) * q, :].reshape(s, width)
        both = jnp.concatenate([real, imag], axis=0)
        first, second = dot_nt(factor_ref[0], both), dot_nt(factor_ref[1], both)
        return first[:, :s] - second[:, s:], first[:, s:] + second[:, :s]

    wave_ref[0], wave_ref[1] = plain(right_ref, 0)
    wave_copy = pltpu.make_async_copy(wave_ref, wave_hbm, sem.at[0])
    wave_copy.start()
    real, imag = plain(left_ref, 2)
    res_ref[0] = data_ref[0].astype(F32) - real
    res_ref[1] = data_ref[1].astype(F32) - imag
    res_copy = pltpu.make_async_copy(res_ref, res_hbm, sem.at[1])
    res_copy.start()
    wave_copy.wait()
    res_copy.wait()


def by_source(data, left, right, ranks, freq_index, ntile, nfreq, here, mine):
    width = left.shape[2]
    rank = width // ntile
    s = data.shape[2]
    q = s // ntile
    half = ntile // 2
    room = (16 << 20) + 64 * width * width

    def like(value):
        return jax.ShapeDtypeStruct(value.shape, value.dtype)

    def call(kernel, specs, args, outs, scratch=(), target=VMEM):
        return pl.pallas_call(
            kernel,
            out_shape=outs,
            in_specs=specs,
            out_specs=[target] * len(outs),
            scratch_shapes=scratch,
            compiler_params=pltpu.CompilerParams(vmem_limit_bytes=room),
        )(*args)

    def along(shift):
        return [
            (2 * z + x, 2 * ((z + shift) % half) + x) for z in range(half) for x in range(2)
        ]

    across = [(t, t ^ 1) for t in range(ntile)]
    sizes = [2 * width + 4 * q] * (half - 1) + [width + 4 * q, width]
    shifts = [0] + offsets(half)
    shifts = shifts + shifts[-1:]
    packets = call(
        functools.partial(gather_start, rank, ntile), [SMEM] * 2 + [HBM] * 4,
        (here, mine, ranks, data, left, right),
        [jax.ShapeDtypeStruct((size, width), BF16) for size in sizes],
        [
            pltpu.SMEM(ranks.shape, jnp.int32),
            pltpu.VMEM(data.shape, BF16),
            pltpu.VMEM(left.shape, BF16),
            pltpu.VMEM(right.shape, BF16),
            pltpu.VMEM((2, s, width), BF16),
            pltpu.SemaphoreType.DMA((4,)),
        ],
    )
    same = [packets[0]] + [
        lax.ppermute(packet, "tcol", along(k)) for packet, k in zip(packets[1:], shifts[1:])
    ]
    other = [lax.ppermute(value, "tcol", across) for value in same]
    vectors = jax.ShapeDtypeStruct((3, ntile, 2 * q, width), F32)
    grams = pltpu.VMEM((2, ntile, width, width), BF16)
    vector = pltpu.VMEM((ntile, 2 * q, width), F32)
    b, c, stats = call(
        functools.partial(chain_kernel, rank, ntile), [SMEM] * 2 + [VMEM] * (ntile + 2),
        (here, freq_index, *same, *other),
        (vectors, vectors, jax.ShapeDtypeStruct((q, 128), F32)),
        [grams, grams, vector, vector],
    )
    gathered = stats[None]
    step = 1
    while step < nfreq:
        pairs = [(f, f ^ step) for f in range(nfreq)]
        gathered = jnp.concatenate([gathered, lax.ppermute(gathered, "freq", pairs)], axis=0)
        step *= 2
    out, data_in, left_in, right_in = call(
        functools.partial(home_mix, rank, nfreq), [HBM] * 3 + [VMEM] * (nfreq + 2),
        (data, left, right, *[gathered[f] for f in range(nfreq)], b, c),
        (
            jax.ShapeDtypeStruct((ntile, 4 * q, width), BF16),
            like(data), like(left), like(right),
        ),
        [pltpu.SemaphoreType.DMA((3,))],
    )
    back = lax.all_to_all(out, "tcol", 0, 0, tiled=True)
    shape = jax.ShapeDtypeStruct(data.shape, F32)
    return call(
        functools.partial(home_kernel, rank), [VMEM] * 4, (back, data_in, left_in, right_in),
        (shape, shape),
        [
            pltpu.VMEM(shape.shape, F32),
            pltpu.VMEM(shape.shape, F32),
            pltpu.SemaphoreType.DMA((2,)),
        ],
        HBM,
    )


def body(data, left_factor, right_factor, ranks, freq_index):
    ntile = lax.axis_size("tcol")
    nfreq = lax.axis_size("freq")
    here = lax.axis_index("tcol").reshape(1)
    mine = lax.axis_index("freq").reshape(1)
    data, left, right, ranks = data[0], left_factor[0], right_factor[0], ranks[0]
    data, left, right, ranks = [
        pltpu.with_memory_space_constraint(value, pltpu.HBM)
        for value in (data, left, right, ranks)
    ]
    width = left.shape[2]
    rank = width // ntile
    s = data.shape[2]
    fits = ntile % 4 == 0 and s % (16 * ntile) == 0 and width % 128 == 0 and 128 % rank == 0
    if fits and nfreq & (nfreq - 1) == 0 and ntile * width * width <= 1 << 20:
        wave, res = by_source(data, left, right, ranks, freq_index, ntile, nfreq, here, mine)
        return wave[None], res[None]
    share = -(-EARLY // ntile)
    height = -(-(LATE + share) // 8) * 8
    field = jax.ShapeDtypeStruct((width, 2 * s), F32)
    sums = jax.ShapeDtypeStruct((8, s), F32)
    bare = jax.ShapeDtypeStruct((ntile, 2 * rank, s), BF16)
    message = jax.ShapeDtypeStruct((ntile, 2 * rank + RIDE, s), BF16)
    gram = jax.ShapeDtypeStruct((width, 2 * width), BF16)
    room = (8 << 20) + 24 * width * width

    def like(value):
        return jax.ShapeDtypeStruct(value.shape, value.dtype)

    def call(kernel, specs, args, outs, scratch=(), target=VMEM):
        return pl.pallas_call(
            functools.partial(kernel, rank),
            out_shape=outs,
            in_specs=specs,
            out_specs=[target] * len(outs),
            scratch_shapes=scratch,
            compiler_params=pltpu.CompilerParams(vmem_limit_bytes=room),
        )(*args)

    def step(kernel, args, outs):
        return call(kernel, [VMEM] * len(args), args, outs)

    def exchange(value):
        return lax.all_to_all(value, "tcol", 0, 0, tiled=True)

    vright, back, damp, out, uhi, ulo, vhi, vlo = call(
        start_kernel, [SMEM] * 2 + [HBM] * 5, (here, mine, ranks, freq_index, data, left, right),
        (like(right), field, sums, bare, gram, gram, gram, gram),
        [
            pltpu.SMEM(ranks.shape, jnp.int32),
            pltpu.SMEM(freq_index.shape, jnp.int32),
            pltpu.VMEM(data.shape, BF16),
            pltpu.VMEM(left.shape, BF16),
            pltpu.SemaphoreType.DMA((5,)),
        ],
    )
    b0 = exchange(out)
    g0, m0, out = step(column0, (b0, vhi, vlo), (field, sums, message))
    c0 = exchange(out)
    n0, out = step(row0, (c0, uhi, ulo, back), (sums, message))
    b1 = exchange(out)
    g1, m1, out = step(column1, (b1, b0, vhi, vlo, g0, n0), (field, sums, message))
    c1 = exchange(out)
    n1, out = step(row1, (c1, c0, uhi, ulo, back), (sums, message))
    b2 = exchange(out)
    m2, out = step(
        column2, (b2, b0, b1, vhi, vlo, g0, g1, damp, m0, n0, m1, n1), (sums, message)
    )
    c2 = exchange(out)
    args = (here, c2, c0, c1, uhi, ulo, back, damp, m1, m2)
    (out,) = call(
        lambda rank, *refs: row2(rank, share, *refs), [SMEM] + [VMEM] * 9, args,
        (jax.ShapeDtypeStruct((nfreq * ntile, height, s), F32),),
        [pltpu.VMEM((max(16, ntile * share), s), F32)],
    )
    everyone = lax.all_to_all(out, ("freq", "tcol"), 0, 0, tiled=True)
    shape = jax.ShapeDtypeStruct(data.shape, F32)
    wave, res = call(
        lambda rank, *refs: finish_kernel(rank, nfreq, share, *refs),
        [SMEM, HBM, HBM] + [VMEM] * 8,
        (mine, data, left, everyone, vright, b0, b1, b2, c0, c1, c2), (shape, shape),
        [
            pltpu.VMEM((LATE + EARLY, nfreq, s), F32),
            pltpu.VMEM((6, nfreq, s), F32),
            pltpu.VMEM(shape.shape, F32),
            pltpu.VMEM(shape.shape, F32),
            pltpu.VMEM(data.shape, BF16),
            pltpu.VMEM(left.shape, BF16),
            pltpu.SemaphoreType.DMA((4,)),
        ],
        HBM,
    )
    return wave[None], res[None]


def solution(mesh):
    in_specs = (
        P("freq", None, "tcol", None),
        P("freq", None, "tcol", None),
        P("freq", None, "tcol", None),
        P("freq", None, None),
        P("freq"),
    )
    out_specs = (P("freq", None, "tcol", None), P("freq", None, "tcol", None))
    return jax.shard_map(body, mesh=mesh, in_specs=in_specs, out_specs=out_specs, check_vma=False)
```

```python
import functools

import jax
import jax.numpy as jnp
from jax import lax
from jax.experimental import pallas as pl
from jax.experimental.pallas import tpu as pltpu
from jax.sharding import PartitionSpec as P


RIDE = 16
LATE = 4
EARLY = 9
VMEM = pl.BlockSpec(memory_space=pltpu.VMEM)
SMEM = pl.BlockSpec(memory_space=pltpu.SMEM)
HBM = pl.BlockSpec(memory_space=pltpu.HBM)
F32 = jnp.float32
BF16 = jnp.bfloat16


def dot(a, b):
    return jnp.dot(a, b, preferred_element_type=F32)


def dot_t(a, b):
    return lax.dot_general(a, b, (((0,), (0,)), ((), ())), preferred_element_type=F32)


def side(real, imag):
    return jnp.concatenate([real, imag], axis=1)


def split(value):
    high = value.astype(BF16)
    return high, (value - high.astype(F32)).astype(BF16)


def unpack(ref, rank):
    n = ref.shape[0]
    real = ref[:, 0:rank, :].reshape(n * rank, ref.shape[2])
    imag = ref[:, rank : 2 * rank, :].reshape(n * rank, ref.shape[2])
    return real, imag


def fields(ref, rank):
    return side(*unpack(ref, rank)).astype(F32)


def send(out_ref, value, rank):
    s = out_ref.shape[2]
    for p in range(out_ref.shape[0]):
        rows = value[p * rank : (p + 1) * rank].astype(BF16)
        out_ref[p, 0:rank, :] = rows[:, :s]
        out_ref[p, rank : 2 * rank, :] = rows[:, s:]


def ride(out_ref, rows, rank):
    rows = rows + [jnp.zeros_like(rows[0])] * (RIDE - len(rows))
    block = jnp.concatenate(rows, axis=0).astype(BF16)
    for p in range(out_ref.shape[0]):
        out_ref[p, 2 * rank : 2 * rank + RIDE, :] = block


def ridden(ref, rank):
    total = ref[0, 2 * rank : 2 * rank + RIDE, :].astype(F32)
    for p in range(1, ref.shape[0]):
        total = total + ref[p, 2 * rank : 2 * rank + RIDE, :].astype(F32)
    return total


def inner(a, b):
    both = jnp.sum(a * b, axis=0, keepdims=True)
    s = both.shape[1] // 2
    return both[:, :s] + both[:, s:]


def twice(row):
    return jnp.concatenate([row, row], axis=1)


def ratio(top, bottom):
    safe = bottom > 0
    return jnp.where(safe, top / jnp.where(safe, bottom, 1.0), 0.0)


def apply_gram(hi_ref, lo_ref, real, imag):
    vector = jnp.concatenate([side(real, imag), side(-imag, real)], axis=0)
    return dot(hi_ref[...], vector) + dot(lo_ref[...], vector)


def make_gram(factor_ref, hi_ref, lo_ref, limits):
    real, imag = factor_ref[0], factor_ref[1]
    width = real.shape[1]
    rank = width // len(limits)
    level = lax.broadcasted_iota(jnp.int32, (rank, width), 0)

    def put(value, place):
        for p, limit in enumerate(limits):
            rows = slice(p * rank, (p + 1) * rank)
            high, low = split(jnp.where(level < limit, value[rows], 0.0))
            hi_ref[rows, place : place + width] = high
            lo_ref[rows, place : place + width] = low

    put(dot_t(real, real) + dot_t(imag, imag), 0)
    put(dot_t(real, imag) - dot_t(imag, real), width)


def start_kernel(
    rank, here_ref, mine_ref, ranks_hbm, freq_hbm, data_hbm, left_hbm, right_hbm,
    right_ref, back_ref, sums_ref, out_ref, uhi_ref, ulo_ref, vhi_ref, vlo_ref,
    ranks_ref, freq_ref, data_ref, left_ref, sem
):
    n = out_ref.shape[0]
    s = out_ref.shape[2]
    pairs = [
        (left_hbm, left_ref), (data_hbm, data_ref), (ranks_hbm, ranks_ref),
        (freq_hbm, freq_ref), (right_hbm, right_ref),
    ]
    copies = [
        pltpu.make_async_copy(source, target, sem.at[k])
        for k, (source, target) in enumerate(pairs)
    ]
    for copy in copies:
        copy.start()
    for copy in copies[:4]:
        copy.wait()
    here = here_ref[0]
    row_limits = [ranks_ref[here, p] for p in range(n)]
    column_limits = [ranks_ref[p, here] for p in range(n)]
    damping = 0.1 + 0.9 * freq_ref[0].astype(F32) / 229.0
    sums_ref[...] = jnp.full(sums_ref.shape, damping)
    real, imag = data_ref[0], data_ref[1]
    back = dot_t(left_ref[0], side(real, imag)) + dot_t(left_ref[1], side(imag, -real))
    level = lax.broadcasted_iota(jnp.int32, (rank, 2 * s), 0)
    back = jnp.concatenate(
        [
            jnp.where(level < limit, back[p * rank : (p + 1) * rank], 0.0)
            for p, limit in enumerate(row_limits)
        ],
        axis=0,
    )
    back_ref[...] = back
    send(out_ref, back, rank)
    make_gram(left_ref, uhi_ref, ulo_ref, row_limits)
    copies[4].wait()
    make_gram(right_ref, vhi_ref, vlo_ref, column_limits)


def column0(rank, b0_ref, hi_ref, lo_ref, g0_ref, sums_ref, out_ref):
    real, imag = unpack(b0_ref, rank)
    g0 = apply_gram(hi_ref, lo_ref, real, imag)
    g0_ref[...] = g0
    m00 = inner(side(real, imag).astype(F32), g0)
    sums_ref[0:1, :] = m00
    send(out_ref, g0, rank)
    ride(out_ref, [m00], rank)


def row0(rank, c0_ref, hi_ref, lo_ref, back_ref, sums_ref, out_ref):
    real, imag = unpack(c0_ref, rank)
    next0 = apply_gram(hi_ref, lo_ref, real, imag)
    c0 = side(real, imag).astype(F32)
    n00 = inner(c0, next0)
    sums_ref[0:1, :] = n00
    sums_ref[1:2, :] = inner(back_ref[...], c0)
    sums_ref[2:3, :] = ridden(c0_ref, rank)[0:1]
    send(out_ref, next0, rank)
    ride(out_ref, [n00], rank)


def column1(
    rank, b1_ref, b0_ref, hi_ref, lo_ref, g0_ref, n0_ref, g1_ref, sums_ref, out_ref
):
    real, imag = unpack(b1_ref, rank)
    theta0 = ratio(ridden(b1_ref, rank)[0:1], n0_ref[2:3, :])
    wide = twice(theta0)
    g1 = apply_gram(hi_ref, lo_ref, real, imag) - wide * g0_ref[...]
    b0 = fields(b0_ref, rank)
    b1 = side(real, imag).astype(F32) - wide * b0
    g1_ref[...] = g1
    m11 = inner(b1, g1)
    sums_ref[0:1, :] = m11
    sums_ref[1:2, :] = inner(b0, g1)
    sums_ref[2:3, :] = theta0
    send(out_ref, g1, rank)
    ride(out_ref, [m11], rank)


def row1(rank, c1_ref, c0_ref, hi_ref, lo_ref, back_ref, sums_ref, out_ref):
    real, imag = unpack(c1_ref, rank)
    next1 = apply_gram(hi_ref, lo_ref, real, imag)
    c1 = side(real, imag).astype(F32)
    n11 = inner(c1, next1)
    n01 = inner(fields(c0_ref, rank), next1)
    sums_ref[0:1, :] = n11
    sums_ref[1:2, :] = n01
    sums_ref[2:3, :] = inner(back_ref[...], c1)
    sums_ref[3:4, :] = ridden(c1_ref, rank)[0:1]
    send(out_ref, next1, rank)
    ride(out_ref, [n11, n01], rank)


def column2(
    rank, b2_ref, b0_ref, b1_ref, hi_ref, lo_ref, g0_ref, g1_ref,
    damp_ref, m0_ref, n0_ref, m1_ref, n1_ref, sums_ref, out_ref
):
    real, imag = unpack(b2_ref, rank)
    came = ridden(b2_ref, rank)
    theta1 = ratio(came[0:1], n1_ref[3:4, :])
    phi = ratio(came[1:2], n0_ref[2:3, :])
    wide1, wide0 = twice(theta1), twice(phi)
    g2 = apply_gram(hi_ref, lo_ref, real, imag) - wide1 * g1_ref[...] - wide0 * g0_ref[...]
    send(out_ref, g2, rank)
    b0 = fields(b0_ref, rank)
    b1 = fields(b1_ref, rank) - twice(m1_ref[2:3, :]) * b0
    b2 = side(real, imag).astype(F32) - wide1 * b1 - wide0 * b0
    sums_ref[0:1, :] = inner(b0, g2)
    sums_ref[1:2, :] = inner(b1, g2)
    sums_ref[2:3, :] = inner(b2, g2)
    sums_ref[3:4, :] = theta1
    sums_ref[4:5, :] = phi
    damping = damp_ref[0:1, :]
    known = [
        n0_ref[0:1, :] + damping * m0_ref[0:1, :],
        n1_ref[1:2, :] + damping * m1_ref[1:2, :],
        n1_ref[0:1, :] + damping * m1_ref[0:1, :],
        n0_ref[1:2, :],
        n1_ref[2:3, :],
    ]
    rest = [row - row.astype(BF16).astype(F32) for row in known]
    ride(out_ref, known + rest, rank)


def row2(
    rank, share, here_ref, c2_ref, c0_ref, c1_ref, hi_ref, lo_ref, back_ref,
    damp_ref, m1_ref, m2_ref, out_ref, table_ref
):
    real, imag = unpack(c2_ref, rank)
    next2 = apply_gram(hi_ref, lo_ref, real, imag)
    damping = damp_ref[0:1, :]
    came = ridden(c2_ref, rank)
    table_ref[0:5, :] = came[0:5] + came[5:10]
    table_ref[5:6, :] = m1_ref[2:3, :]
    table_ref[6:8, :] = m2_ref[3:5, :]
    table_ref[8:9, :] = damping
    rows = [
        inner(fields(c0_ref, rank), next2) + damping * m2_ref[0:1, :],
        inner(fields(c1_ref, rank), next2) + damping * m2_ref[1:2, :],
        inner(side(real, imag).astype(F32), next2) + damping * m2_ref[2:3, :],
        inner(back_ref[...], side(real, imag).astype(F32)),
        table_ref[pl.ds(here_ref[0] * share, share), :],
    ]
    more = out_ref.shape[1] - LATE - share
    if more:
        rows.append(jnp.zeros((more, real.shape[1]), F32))
    block = jnp.concatenate(rows, axis=0)
    for p in range(out_ref.shape[0]):
        out_ref[p] = block


def forms(h, u, g, p, position, size, axis):
    def times(v):
        return [sum(h[a][b] * v[b] for b in range(size)) for a in range(size)]

    def along(a, b):
        return jnp.sum(sum(x * y for x, y in zip(a, b)), axis=axis, keepdims=True)

    hg, hp, hx = times(g), times(p), times(position)
    rest = [u[a] - hx[a] for a in range(size)]
    return along(g, hg), along(p, hg), along(p, hp), along(g, rest), along(p, rest)


def descend(h, u, theta0, theta1, phi, damping, axis):
    one = jnp.ones_like(theta0)
    a11 = jnp.sum(h[0][0], axis=axis, keepdims=True)
    b1 = jnp.sum(u[0], axis=axis, keepdims=True)
    alpha = b1 / (1.1 * a11)
    p = [alpha * one]
    x = [alpha * one]
    for size in (2, 3):
        zero = jnp.zeros_like(one)
        x = x + [zero]
        p = p + [zero]
        if size == 2:
            g = [one - (theta0 + damping) * x[0], -x[0]]
        else:
            g = [
                one - (theta0 + damping) * x[0] - phi * x[1],
                -x[0] - (theta1 + damping) * x[1],
                -x[1],
            ]
        a11, a12, a22, b1, b2 = forms(h, u, g, p, x, size, axis)
        first, second = 1.1 * a11, 1.1 * a22
        determinant = first * second - a12 * a12
        alpha = (b1 * second - a12 * b2) / determinant
        beta = (first * b2 - a12 * b1) / determinant
        p = [alpha * g[a] + beta * p[a] for a in range(size)]
        x = [x[a] + p[a] for a in range(size)]
    return x


def finish_kernel(
    rank, nfreq, share, mine_ref, data_hbm, left_hbm, recv_ref, right_ref,
    b0_ref, b1_ref, b2_ref, c0_ref, c1_ref, c2_ref, wave_hbm, res_hbm,
    table_ref, mix_ref, wave_ref, res_ref, data_ref, left_ref, sem
):
    left_copy = pltpu.make_async_copy(left_hbm, left_ref, sem.at[2])
    data_copy = pltpu.make_async_copy(data_hbm, data_ref, sem.at[3])
    left_copy.start()
    data_copy.start()
    ntile = recv_ref.shape[0] // nfreq
    for f in range(nfreq):
        total = recv_ref[f * ntile]
        for t in range(1, ntile):
            total = total + recv_ref[f * ntile + t]
        table_ref[0:LATE, f, :] = total[0:LATE]
        for q in range(EARLY):
            place = LATE + q % share
            table_ref[LATE + q, f : f + 1, :] = recv_ref[f * ntile + q // share, place : place + 1]
    h = [[None] * 3 for _ in range(3)]
    places = [(0, 0, 2), (1, 1, 2), (2, 2, 2), (4, 0, 0), (5, 0, 1), (6, 1, 1)]
    for place, a, b in places:
        h[a][b] = h[b][a] = table_ref[place]
    u = [table_ref[7], table_ref[8], table_ref[3]]
    theta0, theta1, phi, damping = [table_ref[9 + a] for a in range(4)]
    x = descend(h, u, theta0, theta1, phi, damping, 0)
    mix_ref[0] = x[0] - theta0 * x[1] + (theta0 * theta1 - phi) * x[2]
    mix_ref[1] = x[1] - theta1 * x[2]
    mix_ref[2] = x[2]
    mix_ref[3] = x[0]
    mix_ref[4] = x[1]
    mix_ref[5] = x[2]
    row = pl.ds(mine_ref[0], 1)

    def combine(refs, offset):
        total = None
        for k, ref in enumerate(refs):
            scale = mix_ref[offset + k, row, :]
            real, imag = unpack(ref, rank)
            term = (scale * real.astype(F32), scale * imag.astype(F32))
            total = term if total is None else (total[0] + term[0], total[1] + term[1])
        return total

    def plain(factor_ref, real, imag):
        (rh, rl), (ih, il) = split(real), split(imag)
        first, second = factor_ref[0], factor_ref[1]
        return (
            dot(first, side(rh, ih)) + dot(second, side(-ih, rh))
            + dot(first, side(rl, il)) + dot(second, side(-il, rl))
        )

    s = wave_ref.shape[2]
    wave = plain(right_ref, *combine([b0_ref, b1_ref, b2_ref], 0))
    wave_ref[0] = wave[:, :s]
    wave_ref[1] = wave[:, s:]
    wave_copy = pltpu.make_async_copy(wave_ref, wave_hbm, sem.at[0])
    wave_copy.start()
    mixed = combine([c0_ref, c1_ref, c2_ref], 3)
    left_copy.wait()
    data_copy.wait()
    image = plain(left_ref, *mixed)
    res_ref[0] = data_ref[0].astype(F32) - image[:, :s]
    res_ref[1] = data_ref[1].astype(F32) - image[:, s:]
    res_copy = pltpu.make_async_copy(res_ref, res_hbm, sem.at[1])
    res_copy.start()
    wave_copy.wait()
    res_copy.wait()


def lane_limits(limits, rank, width):
    lane = lax.broadcasted_iota(jnp.int32, (1, width), 1)
    limit = jnp.zeros((1, width), jnp.int32)
    for p, value in enumerate(limits):
        limit = jnp.where(lane >= p * rank, value, limit)
    return (lax.rem(lane, rank) < limit).astype(F32)


def packed_gram(real, imag):
    width = real.shape[1]
    both = jnp.concatenate([real, imag], axis=0)
    upper = dot_t(both, both)
    lower = dot_t(real, imag) - dot_t(imag, real)
    row = lax.broadcasted_iota(jnp.int32, (width, width), 0)
    column = lax.broadcasted_iota(jnp.int32, (width, width), 1)
    return jnp.where(row <= column, upper, lower).astype(BF16)


def unpacked_gram(packed):
    width = packed.shape[1]
    here = packed.astype(F32)
    there = here.T
    row = lax.broadcasted_iota(jnp.int32, (width, width), 0)
    column = lax.broadcasted_iota(jnp.int32, (width, width), 1)
    real = jnp.where(row <= column, here, there)
    imag = jnp.where(row > column, here, jnp.where(row < column, -there, 0.0))
    return real.astype(BF16), imag.astype(BF16)


def offsets(half):
    return sorted(range(1, half), key=lambda k: (min(k, half - k), k))


def tile_parts(refs, half):
    whole = refs[0].shape[0] - refs[0].shape[1]
    parts = {0: (refs[0], refs[0], whole)}
    order = offsets(half)
    for place, k in enumerate(order[:-1]):
        parts[k] = (refs[1 + place], refs[1 + place], whole)
    parts[order[-1]] = (refs[-2], refs[-1], 0)
    return [parts[k] for k in range(half)]


def gather_start(
    rank, n, here_ref, mine_ref, ranks_hbm, data_hbm, left_hbm, right_hbm, *refs
):
    ranks_ref, data_ref, left_ref, right_ref, back_ref, sem = refs[-6:]
    half = n // 2
    packets = tile_parts(refs[: half + 1], half)
    pairs = [
        (left_hbm, left_ref), (data_hbm, data_ref), (ranks_hbm, ranks_ref),
        (right_hbm, right_ref),
    ]
    copies = [
        pltpu.make_async_copy(source, target, sem.at[k])
        for k, (source, target) in enumerate(pairs)
    ]
    for copy in copies:
        copy.start()
    for copy in copies[:3]:
        copy.wait()
    width = left_ref.shape[2]
    s = data_ref.shape[2]
    q = s // n
    here = here_ref[0]
    keep = lane_limits([ranks_ref[here, p] for p in range(n)], rank, width).astype(BF16)
    real, imag = left_ref[0] * keep, left_ref[1] * keep
    both = side(data_ref[0], data_ref[1])
    first, second = dot_t(both, real), dot_t(both, imag)
    back_ref[0] = (first[:s] + second[s:]).astype(BF16)
    back_ref[1] = (first[s:] - second[:s]).astype(BF16)
    gram = packed_gram(real, imag)
    for first, _, _ in packets:
        first[0:width, :] = gram
    copies[3].wait()
    keep = lane_limits([ranks_ref[p, here] for p in range(n)], rank, width).astype(BF16)
    gram = packed_gram(right_ref[0] * keep, right_ref[1] * keep)
    z, x = lax.div(here, 2), lax.rem(here, 2)
    for k, (first, second, place) in enumerate(packets):
        second[place : place + width, :] = gram
        base = 2 * lax.rem(z + k, half)
        for block, target in enumerate([base + 1 - x, base + x]):
            rows = pl.ds(pl.multiple_of(target * q, q), q)
            place = width + 2 * q * block
            first[place : place + q, :] = back_ref[0, rows, :]
            first[place + q : place + 2 * q, :] = back_ref[1, rows, :]


def swap_tiles(rank, source, target):
    n, rows, width = source.shape
    per = 128 // rank
    lane = lax.div(lax.broadcasted_iota(jnp.int32, (rows, 128), 1), rank)
    for g in range(n // per):
        for h in range(width // 128):
            ins = [source[per * g + a, :, 128 * h : 128 * h + 128] for a in range(per)]
            for b in range(per):
                out = None
                for a in range(per):
                    shift = (a - b) * rank % 128
                    piece = pltpu.roll(ins[a], shift, 1) if shift else ins[a]
                    out = piece if out is None else jnp.where(lane == a, piece, out)
                target[per * h + b, :, 128 * g : 128 * g + 128] = out


def apply_tiles(gram_ref, source, target):
    n, rows, _ = source.shape
    q = rows // 2
    for j in range(n):
        high, low = split(source[j])
        vector = jnp.concatenate([high, low], axis=0)
        real, imag = dot(vector, gram_ref[0, j]), dot(vector, gram_ref[1, j])
        real = real[:rows] + real[rows:]
        imag = imag[:rows] + imag[rows:]
        target[j, 0:q, :] = real[:q] + imag[q:]
        target[j, q:rows, :] = real[q:] - imag[:q]


def inner_tiles(first, second):
    n, rows, _ = first.shape
    total = first[0] * second[0]
    for j in range(1, n):
        total = total + first[j] * second[j]
    total = jnp.sum(total, axis=1, keepdims=True)
    return total[: rows // 2] + total[rows // 2 :]


def take_off(target, terms):
    scales = [jnp.concatenate([scale, scale], axis=0) for scale, _ in terms]
    for j in range(target.shape[0]):
        value = target[j]
        for scale, (_, other) in zip(scales, terms):
            value = value - scale * other[j]
        target[j] = value


def chain_kernel(
    rank, n, here_ref, freq_ref, data_hbm, left_hbm, right_hbm, *refs
):
    half = n // 2
    *refs, data_ref, home_left, home_right, gram_left, gram_right, one_ref, two_ref, sem = refs
    pairs = [(right_hbm, home_right), (left_hbm, home_left), (data_hbm, data_ref)]
    copies = [
        pltpu.make_async_copy(source, target, sem.at[k])
        for k, (source, target) in enumerate(pairs)
    ]
    for copy in copies:
        copy.start()
    tiles = [tile_parts(refs[: half + 1], half), tile_parts(refs[half + 1 : n + 2], half)]
    b_ref, c_ref, stats_ref = refs[n + 2 :]
    left_ref, right_ref = gram_left, gram_right
    width = refs[0].shape[1]
    q = stats_ref.shape[0]
    here = here_ref[0]
    z, x = lax.div(here, 2), lax.rem(here, 2)
    for k in range(half):
        base = 2 * lax.rem(z + half - k, half)
        for other in range(2):
            first, second, place = tiles[other][k]
            at = pl.ds(base + (1 - x if other else x), 1)
            grams = (first[0:width, :], second[place : place + width, :])
            for packed, gram_ref in zip(grams, (left_ref, right_ref)):
                real, imag = unpacked_gram(packed)
                gram_ref[0, at] = real[None]
                gram_ref[1, at] = imag[None]
            start = width + (0 if other else 2 * q)
            one_ref[at] = first[start : start + 2 * q, :].astype(F32)[None]
    b0, b1, b2 = b_ref.at[0], b_ref.at[1], b_ref.at[2]
    c0, c1, c2 = c_ref.at[0], c_ref.at[1], c_ref.at[2]
    swap_tiles(rank, one_ref, b0)
    apply_tiles(right_ref, b0, two_ref)
    m00 = inner_tiles(b0, two_ref)
    swap_tiles(rank, two_ref, c0)
    apply_tiles(left_ref, c0, one_ref)
    n00 = inner_tiles(c0, one_ref)
    theta0 = ratio(n00, m00)
    swap_tiles(rank, one_ref, b1)
    take_off(b1, [(theta0, b0)])
    apply_tiles(right_ref, b1, two_ref)
    m11 = inner_tiles(b1, two_ref)
    m01 = inner_tiles(b0, two_ref)
    swap_tiles(rank, two_ref, c1)
    apply_tiles(left_ref, c1, one_ref)
    n11 = inner_tiles(c1, one_ref)
    n01 = inner_tiles(c0, one_ref)
    theta1 = ratio(n11, m11)
    phi = ratio(n01, m00)
    swap_tiles(rank, one_ref, b2)
    take_off(b2, [(theta1, b1), (phi, b0)])
    apply_tiles(right_ref, b2, two_ref)
    m02 = inner_tiles(b0, two_ref)
    m12 = inner_tiles(b1, two_ref)
    m22 = inner_tiles(b2, two_ref)
    swap_tiles(rank, two_ref, c2)
    apply_tiles(left_ref, c2, one_ref)
    n02 = inner_tiles(c0, one_ref)
    n12 = inner_tiles(c1, one_ref)
    n22 = inner_tiles(c2, one_ref)
    damping = 0.1 + 0.9 * freq_ref[0].astype(F32) / 229.0
    values = [
        n00 + damping * m00, n01 + damping * m01, n02 + damping * m02,
        n11 + damping * m11, n12 + damping * m12, n22 + damping * m22,
        m00, m01, m02, theta0, theta1, phi,
    ]
    lane = lax.broadcasted_iota(jnp.int32, stats_ref.shape, 1)
    block = jnp.full(stats_ref.shape, damping)
    for place, value in enumerate(values):
        block = jnp.where(lane == place, value, block)
    stats_ref[...] = block
    for copy in copies:
        copy.wait()


def mix_kernel(nfreq, *refs):
    stats_refs, (b_ref, c_ref, out_ref) = refs[:nfreq], refs[nfreq:]
    blocks = [ref[...] for ref in stats_refs]
    lane = lax.broadcasted_iota(jnp.int32, blocks[0].shape, 1)
    where_f = [lane == f for f in range(len(blocks))]

    def pick(place):
        value = jnp.zeros_like(blocks[0])
        for f, block in enumerate(blocks):
            shift = (f - place) % 128
            value = jnp.where(where_f[f], pltpu.roll(block, shift, 1) if shift else block, value)
        return value

    h = [[None] * 3 for _ in range(3)]
    for place, (a, b) in enumerate([(0, 0), (0, 1), (0, 2), (1, 1), (1, 2), (2, 2)]):
        h[a][b] = h[b][a] = pick(place)
    u = [pick(6), pick(7), pick(8)]
    theta0, theta1, phi, damping = pick(9), pick(10), pick(11), pick(12)
    x = descend(h, u, theta0, theta1, phi, damping, 1)
    n, rows, _ = b_ref.shape[1:]
    scales = []
    for value in x:
        own = jnp.sum(jnp.where(lane == 0, value, 0.0), axis=1, keepdims=True)
        scales.append(jnp.concatenate([own, own], axis=0))
    for j in range(n):
        for place, ref in enumerate((b_ref, c_ref)):
            value = scales[0] * ref[0, j] + scales[1] * ref[1, j] + scales[2] * ref[2, j]
            out_ref[j, place * rows : (place + 1) * rows, :] = value.astype(BF16)


def dot_nt(a, b):
    return lax.dot_general(a, b, (((1,), (1,)), ((), ())), preferred_element_type=F32)


def home_kernel(
    rank, recv_ref, data_ref, left_ref, right_ref, wave_hbm, res_hbm, wave_ref, res_ref, sem
):
    n, rows, width = recv_ref.shape
    q = rows // 4
    s = n * q

    def plain(factor_ref, place):
        real = recv_ref[:, place * q : (place + 1) * q, :].reshape(s, width)
        imag = recv_ref[:, (place + 1) * q : (place + 2) * q, :].reshape(s, width)
        both = jnp.concatenate([real, imag], axis=0)
        first, second = dot_nt(factor_ref[0], both), dot_nt(factor_ref[1], both)
        return first[:, :s] - second[:, s:], first[:, s:] + second[:, :s]

    wave_ref[0], wave_ref[1] = plain(right_ref, 0)
    wave_copy = pltpu.make_async_copy(wave_ref, wave_hbm, sem.at[0])
    wave_copy.start()
    real, imag = plain(left_ref, 2)
    res_ref[0] = data_ref[0].astype(F32) - real
    res_ref[1] = data_ref[1].astype(F32) - imag
    res_copy = pltpu.make_async_copy(res_ref, res_hbm, sem.at[1])
    res_copy.start()
    wave_copy.wait()
    res_copy.wait()


def by_source(data, left, right, ranks, freq_index, ntile, nfreq, here, mine):
    width = left.shape[2]
    rank = width // ntile
    s = data.shape[2]
    q = s // ntile
    half = ntile // 2
    room = (16 << 20) + 64 * width * width

    def like(value):
        return jax.ShapeDtypeStruct(value.shape, value.dtype)

    def call(kernel, specs, args, outs, scratch=(), target=VMEM):
        return pl.pallas_call(
            kernel,
            out_shape=outs,
            in_specs=specs,
            out_specs=[target] * len(outs),
            scratch_shapes=scratch,
            compiler_params=pltpu.CompilerParams(vmem_limit_bytes=room),
        )(*args)

    def along(shift):
        return [
            (2 * z + x, 2 * ((z + shift) % half) + x) for z in range(half) for x in range(2)
        ]

    across = [(t, t ^ 1) for t in range(ntile)]
    sizes = [2 * width + 4 * q] * (half - 1) + [width + 4 * q, width]
    shifts = [0] + offsets(half)
    shifts = shifts + shifts[-1:]
    packets = call(
        functools.partial(gather_start, rank, ntile), [SMEM] * 2 + [HBM] * 4,
        (here, mine, ranks, data, left, right),
        [jax.ShapeDtypeStruct((size, width), BF16) for size in sizes],
        [
            pltpu.SMEM(ranks.shape, jnp.int32),
            pltpu.VMEM(data.shape, BF16),
            pltpu.VMEM(left.shape, BF16),
            pltpu.VMEM(right.shape, BF16),
            pltpu.VMEM((2, s, width), BF16),
            pltpu.SemaphoreType.DMA((4,)),
        ],
    )
    same = [packets[0], lax.ppermute(packets[1], "tcol", along(shifts[1]))]
    other = [lax.ppermute(packets[0], "tcol", across)]
    for packet, k in zip(packets[2:], shifts[2:]):
        if k == shifts[-1]:
            packet, same[1] = lax.optimization_barrier((packet, same[1]))
        else:
            packet, other[0] = lax.optimization_barrier((packet, other[0]))
        same.append(lax.ppermute(packet, "tcol", along(k)))
    other = other + [lax.ppermute(value, "tcol", across) for value in same[1:]]
    vectors = jax.ShapeDtypeStruct((3, ntile, 2 * q, width), F32)
    grams = pltpu.VMEM((2, ntile, width, width), BF16)
    vector = pltpu.VMEM((ntile, 2 * q, width), F32)
    b, c, stats, data_in, left_in, right_in = call(
        functools.partial(chain_kernel, rank, ntile),
        [SMEM] * 2 + [HBM] * 3 + [VMEM] * (ntile + 2),
        (here, freq_index, data, left, right, *same, *other),
        (
            vectors, vectors, jax.ShapeDtypeStruct((q, 128), F32),
            like(data), like(left), like(right),
        ),
        [grams, grams, vector, vector, pltpu.SemaphoreType.DMA((3,))],
    )
    gathered = stats[None]
    step = 1
    while step < nfreq:
        pairs = [(f, f ^ step) for f in range(nfreq)]
        gathered = jnp.concatenate([gathered, lax.ppermute(gathered, "freq", pairs)], axis=0)
        step *= 2
    (out,) = call(
        functools.partial(mix_kernel, nfreq), [VMEM] * (nfreq + 2),
        (*[gathered[f] for f in range(nfreq)], b, c),
        (jax.ShapeDtypeStruct((ntile, 4 * q, width), BF16),),
    )
    back = lax.all_to_all(out, "tcol", 0, 0, tiled=True)
    shape = jax.ShapeDtypeStruct(data.shape, F32)
    return call(
        functools.partial(home_kernel, rank), [VMEM] * 4, (back, data_in, left_in, right_in),
        (shape, shape),
        [
            pltpu.VMEM(shape.shape, F32),
            pltpu.VMEM(shape.shape, F32),
            pltpu.SemaphoreType.DMA((2,)),
        ],
        HBM,
    )


def body(data, left_factor, right_factor, ranks, freq_index):
    ntile = lax.axis_size("tcol")
    nfreq = lax.axis_size("freq")
    here = lax.axis_index("tcol").reshape(1)
    mine = lax.axis_index("freq").reshape(1)
    data, left, right, ranks = data[0], left_factor[0], right_factor[0], ranks[0]
    data, left, right, ranks = [
        pltpu.with_memory_space_constraint(value, pltpu.HBM)
        for value in (data, left, right, ranks)
    ]
    width = left.shape[2]
    rank = width // ntile
    s = data.shape[2]
    fits = ntile % 4 == 0 and s % (16 * ntile) == 0 and width % 128 == 0 and 128 % rank == 0
    if fits and nfreq & (nfreq - 1) == 0 and ntile * width * width <= 1 << 20:
        wave, res = by_source(data, left, right, ranks, freq_index, ntile, nfreq, here, mine)
        return wave[None], res[None]
    share = -(-EARLY // ntile)
    height = -(-(LATE + share) // 8) * 8
    field = jax.ShapeDtypeStruct((width, 2 * s), F32)
    sums = jax.ShapeDtypeStruct((8, s), F32)
    bare = jax.ShapeDtypeStruct((ntile, 2 * rank, s), BF16)
    message = jax.ShapeDtypeStruct((ntile, 2 * rank + RIDE, s), BF16)
    gram = jax.ShapeDtypeStruct((width, 2 * width), BF16)
    room = (8 << 20) + 24 * width * width

    def like(value):
        return jax.ShapeDtypeStruct(value.shape, value.dtype)

    def call(kernel, specs, args, outs, scratch=(), target=VMEM):
        return pl.pallas_call(
            functools.partial(kernel, rank),
            out_shape=outs,
            in_specs=specs,
            out_specs=[target] * len(outs),
            scratch_shapes=scratch,
            compiler_params=pltpu.CompilerParams(vmem_limit_bytes=room),
        )(*args)

    def step(kernel, args, outs):
        return call(kernel, [VMEM] * len(args), args, outs)

    def exchange(value):
        return lax.all_to_all(value, "tcol", 0, 0, tiled=True)

    vright, back, damp, out, uhi, ulo, vhi, vlo = call(
        start_kernel, [SMEM] * 2 + [HBM] * 5, (here, mine, ranks, freq_index, data, left, right),
        (like(right), field, sums, bare, gram, gram, gram, gram),
        [
            pltpu.SMEM(ranks.shape, jnp.int32),
            pltpu.SMEM(freq_index.shape, jnp.int32),
            pltpu.VMEM(data.shape, BF16),
            pltpu.VMEM(left.shape, BF16),
            pltpu.SemaphoreType.DMA((5,)),
        ],
    )
    b0 = exchange(out)
    g0, m0, out = step(column0, (b0, vhi, vlo), (field, sums, message))
    c0 = exchange(out)
    n0, out = step(row0, (c0, uhi, ulo, back), (sums, message))
    b1 = exchange(out)
    g1, m1, out = step(column1, (b1, b0, vhi, vlo, g0, n0), (field, sums, message))
    c1 = exchange(out)
    n1, out = step(row1, (c1, c0, uhi, ulo, back), (sums, message))
    b2 = exchange(out)
    m2, out = step(
        column2, (b2, b0, b1, vhi, vlo, g0, g1, damp, m0, n0, m1, n1), (sums, message)
    )
    c2 = exchange(out)
    args = (here, c2, c0, c1, uhi, ulo, back, damp, m1, m2)
    (out,) = call(
        lambda rank, *refs: row2(rank, share, *refs), [SMEM] + [VMEM] * 9, args,
        (jax.ShapeDtypeStruct((nfreq * ntile, height, s), F32),),
        [pltpu.VMEM((max(16, ntile * share), s), F32)],
    )
    everyone = lax.all_to_all(out, ("freq", "tcol"), 0, 0, tiled=True)
    shape = jax.ShapeDtypeStruct(data.shape, F32)
    wave, res = call(
        lambda rank, *refs: finish_kernel(rank, nfreq, share, *refs),
        [SMEM, HBM, HBM] + [VMEM] * 8,
        (mine, data, left, everyone, vright, b0, b1, b2, c0, c1, c2), (shape, shape),
        [
            pltpu.VMEM((LATE + EARLY, nfreq, s), F32),
            pltpu.VMEM((6, nfreq, s), F32),
            pltpu.VMEM(shape.shape, F32),
            pltpu.VMEM(shape.shape, F32),
            pltpu.VMEM(data.shape, BF16),
            pltpu.VMEM(left.shape, BF16),
            pltpu.SemaphoreType.DMA((4,)),
        ],
        HBM,
    )
    return wave[None], res[None]


def solution(mesh):
    in_specs = (
        P("freq", None, "tcol", None),
        P("freq", None, "tcol", None),
        P("freq", None, "tcol", None),
        P("freq", None, None),
        P("freq"),
    )
    out_specs = (P("freq", None, "tcol", None), P("freq", None, "tcol", None))
    return jax.shard_map(body, mesh=mesh, in_specs=in_specs, out_specs=out_specs, check_vma=False)
```

```python
import functools

import jax
import jax.numpy as jnp
from jax import lax
from jax.experimental import pallas as pl
from jax.experimental.pallas import tpu as pltpu
from jax.sharding import PartitionSpec as P


RIDE = 16
LATE = 4
EARLY = 9
VMEM = pl.BlockSpec(memory_space=pltpu.VMEM)
SMEM = pl.BlockSpec(memory_space=pltpu.SMEM)
HBM = pl.BlockSpec(memory_space=pltpu.HBM)
F32 = jnp.float32
BF16 = jnp.bfloat16


def dot(a, b):
    return jnp.dot(a, b, preferred_element_type=F32)


def dot_t(a, b):
    return lax.dot_general(a, b, (((0,), (0,)), ((), ())), preferred_element_type=F32)


def side(real, imag):
    return jnp.concatenate([real, imag], axis=1)


def split(value):
    high = value.astype(BF16)
    return high, (value - high.astype(F32)).astype(BF16)


def unpack(ref, rank):
    n = ref.shape[0]
    real = ref[:, 0:rank, :].reshape(n * rank, ref.shape[2])
    imag = ref[:, rank : 2 * rank, :].reshape(n * rank, ref.shape[2])
    return real, imag


def fields(ref, rank):
    return side(*unpack(ref, rank)).astype(F32)


def send(out_ref, value, rank):
    s = out_ref.shape[2]
    for p in range(out_ref.shape[0]):
        rows = value[p * rank : (p + 1) * rank].astype(BF16)
        out_ref[p, 0:rank, :] = rows[:, :s]
        out_ref[p, rank : 2 * rank, :] = rows[:, s:]


def ride(out_ref, rows, rank):
    rows = rows + [jnp.zeros_like(rows[0])] * (RIDE - len(rows))
    block = jnp.concatenate(rows, axis=0).astype(BF16)
    for p in range(out_ref.shape[0]):
        out_ref[p, 2 * rank : 2 * rank + RIDE, :] = block


def ridden(ref, rank):
    total = ref[0, 2 * rank : 2 * rank + RIDE, :].astype(F32)
    for p in range(1, ref.shape[0]):
        total = total + ref[p, 2 * rank : 2 * rank + RIDE, :].astype(F32)
    return total


def inner(a, b):
    both = jnp.sum(a * b, axis=0, keepdims=True)
    s = both.shape[1] // 2
    return both[:, :s] + both[:, s:]


def twice(row):
    return jnp.concatenate([row, row], axis=1)


def ratio(top, bottom):
    safe = bottom > 0
    return jnp.where(safe, top / jnp.where(safe, bottom, 1.0), 0.0)


def apply_gram(hi_ref, lo_ref, real, imag):
    vector = jnp.concatenate([side(real, imag), side(-imag, real)], axis=0)
    return dot(hi_ref[...], vector) + dot(lo_ref[...], vector)


def make_gram(factor_ref, hi_ref, lo_ref, limits):
    real, imag = factor_ref[0], factor_ref[1]
    width = real.shape[1]
    rank = width // len(limits)
    level = lax.broadcasted_iota(jnp.int32, (rank, width), 0)

    def put(value, place):
        for p, limit in enumerate(limits):
            rows = slice(p * rank, (p + 1) * rank)
            high, low = split(jnp.where(level < limit, value[rows], 0.0))
            hi_ref[rows, place : place + width] = high
            lo_ref[rows, place : place + width] = low

    put(dot_t(real, real) + dot_t(imag, imag), 0)
    put(dot_t(real, imag) - dot_t(imag, real), width)


def start_kernel(
    rank, here_ref, mine_ref, ranks_hbm, freq_hbm, data_hbm, left_hbm, right_hbm,
    right_ref, back_ref, sums_ref, out_ref, uhi_ref, ulo_ref, vhi_ref, vlo_ref,
    ranks_ref, freq_ref, data_ref, left_ref, sem
):
    n = out_ref.shape[0]
    s = out_ref.shape[2]
    pairs = [
        (left_hbm, left_ref), (data_hbm, data_ref), (ranks_hbm, ranks_ref),
        (freq_hbm, freq_ref), (right_hbm, right_ref),
    ]
    copies = [
        pltpu.make_async_copy(source, target, sem.at[k])
        for k, (source, target) in enumerate(pairs)
    ]
    for copy in copies:
        copy.start()
    for copy in copies[:4]:
        copy.wait()
    here = here_ref[0]
    row_limits = [ranks_ref[here, p] for p in range(n)]
    column_limits = [ranks_ref[p, here] for p in range(n)]
    damping = 0.1 + 0.9 * freq_ref[0].astype(F32) / 229.0
    sums_ref[...] = jnp.full(sums_ref.shape, damping)
    real, imag = data_ref[0], data_ref[1]
    back = dot_t(left_ref[0], side(real, imag)) + dot_t(left_ref[1], side(imag, -real))
    level = lax.broadcasted_iota(jnp.int32, (rank, 2 * s), 0)
    back = jnp.concatenate(
        [
            jnp.where(level < limit, back[p * rank : (p + 1) * rank], 0.0)
            for p, limit in enumerate(row_limits)
        ],
        axis=0,
    )
    back_ref[...] = back
    send(out_ref, back, rank)
    make_gram(left_ref, uhi_ref, ulo_ref, row_limits)
    copies[4].wait()
    make_gram(right_ref, vhi_ref, vlo_ref, column_limits)


def column0(rank, b0_ref, hi_ref, lo_ref, g0_ref, sums_ref, out_ref):
    real, imag = unpack(b0_ref, rank)
    g0 = apply_gram(hi_ref, lo_ref, real, imag)
    g0_ref[...] = g0
    m00 = inner(side(real, imag).astype(F32), g0)
    sums_ref[0:1, :] = m00
    send(out_ref, g0, rank)
    ride(out_ref, [m00], rank)


def row0(rank, c0_ref, hi_ref, lo_ref, back_ref, sums_ref, out_ref):
    real, imag = unpack(c0_ref, rank)
    next0 = apply_gram(hi_ref, lo_ref, real, imag)
    c0 = side(real, imag).astype(F32)
    n00 = inner(c0, next0)
    sums_ref[0:1, :] = n00
    sums_ref[1:2, :] = inner(back_ref[...], c0)
    sums_ref[2:3, :] = ridden(c0_ref, rank)[0:1]
    send(out_ref, next0, rank)
    ride(out_ref, [n00], rank)


def column1(
    rank, b1_ref, b0_ref, hi_ref, lo_ref, g0_ref, n0_ref, g1_ref, sums_ref, out_ref
):
    real, imag = unpack(b1_ref, rank)
    theta0 = ratio(ridden(b1_ref, rank)[0:1], n0_ref[2:3, :])
    wide = twice(theta0)
    g1 = apply_gram(hi_ref, lo_ref, real, imag) - wide * g0_ref[...]
    b0 = fields(b0_ref, rank)
    b1 = side(real, imag).astype(F32) - wide * b0
    g1_ref[...] = g1
    m11 = inner(b1, g1)
    sums_ref[0:1, :] = m11
    sums_ref[1:2, :] = inner(b0, g1)
    sums_ref[2:3, :] = theta0
    send(out_ref, g1, rank)
    ride(out_ref, [m11], rank)


def row1(rank, c1_ref, c0_ref, hi_ref, lo_ref, back_ref, sums_ref, out_ref):
    real, imag = unpack(c1_ref, rank)
    next1 = apply_gram(hi_ref, lo_ref, real, imag)
    c1 = side(real, imag).astype(F32)
    n11 = inner(c1, next1)
    n01 = inner(fields(c0_ref, rank), next1)
    sums_ref[0:1, :] = n11
    sums_ref[1:2, :] = n01
    sums_ref[2:3, :] = inner(back_ref[...], c1)
    sums_ref[3:4, :] = ridden(c1_ref, rank)[0:1]
    send(out_ref, next1, rank)
    ride(out_ref, [n11, n01], rank)


def column2(
    rank, b2_ref, b0_ref, b1_ref, hi_ref, lo_ref, g0_ref, g1_ref,
    damp_ref, m0_ref, n0_ref, m1_ref, n1_ref, sums_ref, out_ref
):
    real, imag = unpack(b2_ref, rank)
    came = ridden(b2_ref, rank)
    theta1 = ratio(came[0:1], n1_ref[3:4, :])
    phi = ratio(came[1:2], n0_ref[2:3, :])
    wide1, wide0 = twice(theta1), twice(phi)
    g2 = apply_gram(hi_ref, lo_ref, real, imag) - wide1 * g1_ref[...] - wide0 * g0_ref[...]
    send(out_ref, g2, rank)
    b0 = fields(b0_ref, rank)
    b1 = fields(b1_ref, rank) - twice(m1_ref[2:3, :]) * b0
    b2 = side(real, imag).astype(F32) - wide1 * b1 - wide0 * b0
    sums_ref[0:1, :] = inner(b0, g2)
    sums_ref[1:2, :] = inner(b1, g2)
    sums_ref[2:3, :] = inner(b2, g2)
    sums_ref[3:4, :] = theta1
    sums_ref[4:5, :] = phi
    damping = damp_ref[0:1, :]
    known = [
        n0_ref[0:1, :] + damping * m0_ref[0:1, :],
        n1_ref[1:2, :] + damping * m1_ref[1:2, :],
        n1_ref[0:1, :] + damping * m1_ref[0:1, :],
        n0_ref[1:2, :],
        n1_ref[2:3, :],
    ]
    rest = [row - row.astype(BF16).astype(F32) for row in known]
    ride(out_ref, known + rest, rank)


def row2(
    rank, share, here_ref, c2_ref, c0_ref, c1_ref, hi_ref, lo_ref, back_ref,
    damp_ref, m1_ref, m2_ref, out_ref, table_ref
):
    real, imag = unpack(c2_ref, rank)
    next2 = apply_gram(hi_ref, lo_ref, real, imag)
    damping = damp_ref[0:1, :]
    came = ridden(c2_ref, rank)
    table_ref[0:5, :] = came[0:5] + came[5:10]
    table_ref[5:6, :] = m1_ref[2:3, :]
    table_ref[6:8, :] = m2_ref[3:5, :]
    table_ref[8:9, :] = damping
    rows = [
        inner(fields(c0_ref, rank), next2) + damping * m2_ref[0:1, :],
        inner(fields(c1_ref, rank), next2) + damping * m2_ref[1:2, :],
        inner(side(real, imag).astype(F32), next2) + damping * m2_ref[2:3, :],
        inner(back_ref[...], side(real, imag).astype(F32)),
        table_ref[pl.ds(here_ref[0] * share, share), :],
    ]
    more = out_ref.shape[1] - LATE - share
    if more:
        rows.append(jnp.zeros((more, real.shape[1]), F32))
    block = jnp.concatenate(rows, axis=0)
    for p in range(out_ref.shape[0]):
        out_ref[p] = block


def forms(h, u, g, p, position, size, axis):
    def times(v):
        return [sum(h[a][b] * v[b] for b in range(size)) for a in range(size)]

    def along(a, b):
        return jnp.sum(sum(x * y for x, y in zip(a, b)), axis=axis, keepdims=True)

    hg, hp, hx = times(g), times(p), times(position)
    rest = [u[a] - hx[a] for a in range(size)]
    return along(g, hg), along(p, hg), along(p, hp), along(g, rest), along(p, rest)


def descend(h, u, theta0, theta1, phi, damping, axis):
    one = jnp.ones_like(theta0)
    a11 = jnp.sum(h[0][0], axis=axis, keepdims=True)
    b1 = jnp.sum(u[0], axis=axis, keepdims=True)
    alpha = b1 / (1.1 * a11)
    p = [alpha * one]
    x = [alpha * one]
    for size in (2, 3):
        zero = jnp.zeros_like(one)
        x = x + [zero]
        p = p + [zero]
        if size == 2:
            g = [one - (theta0 + damping) * x[0], -x[0]]
        else:
            g = [
                one - (theta0 + damping) * x[0] - phi * x[1],
                -x[0] - (theta1 + damping) * x[1],
                -x[1],
            ]
        a11, a12, a22, b1, b2 = forms(h, u, g, p, x, size, axis)
        first, second = 1.1 * a11, 1.1 * a22
        determinant = first * second - a12 * a12
        alpha = (b1 * second - a12 * b2) / determinant
        beta = (first * b2 - a12 * b1) / determinant
        p = [alpha * g[a] + beta * p[a] for a in range(size)]
        x = [x[a] + p[a] for a in range(size)]
    return x


def finish_kernel(
    rank, nfreq, share, mine_ref, data_hbm, left_hbm, recv_ref, right_ref,
    b0_ref, b1_ref, b2_ref, c0_ref, c1_ref, c2_ref, wave_hbm, res_hbm,
    table_ref, mix_ref, wave_ref, res_ref, data_ref, left_ref, sem
):
    left_copy = pltpu.make_async_copy(left_hbm, left_ref, sem.at[2])
    data_copy = pltpu.make_async_copy(data_hbm, data_ref, sem.at[3])
    left_copy.start()
    data_copy.start()
    ntile = recv_ref.shape[0] // nfreq
    for f in range(nfreq):
        total = recv_ref[f * ntile]
        for t in range(1, ntile):
            total = total + recv_ref[f * ntile + t]
        table_ref[0:LATE, f, :] = total[0:LATE]
        for q in range(EARLY):
            place = LATE + q % share
            table_ref[LATE + q, f : f + 1, :] = recv_ref[f * ntile + q // share, place : place + 1]
    h = [[None] * 3 for _ in range(3)]
    places = [(0, 0, 2), (1, 1, 2), (2, 2, 2), (4, 0, 0), (5, 0, 1), (6, 1, 1)]
    for place, a, b in places:
        h[a][b] = h[b][a] = table_ref[place]
    u = [table_ref[7], table_ref[8], table_ref[3]]
    theta0, theta1, phi, damping = [table_ref[9 + a] for a in range(4)]
    x = descend(h, u, theta0, theta1, phi, damping, 0)
    mix_ref[0] = x[0] - theta0 * x[1] + (theta0 * theta1 - phi) * x[2]
    mix_ref[1] = x[1] - theta1 * x[2]
    mix_ref[2] = x[2]
    mix_ref[3] = x[0]
    mix_ref[4] = x[1]
    mix_ref[5] = x[2]
    row = pl.ds(mine_ref[0], 1)

    def combine(refs, offset):
        total = None
        for k, ref in enumerate(refs):
            scale = mix_ref[offset + k, row, :]
            real, imag = unpack(ref, rank)
            term = (scale * real.astype(F32), scale * imag.astype(F32))
            total = term if total is None else (total[0] + term[0], total[1] + term[1])
        return total

    def plain(factor_ref, real, imag):
        (rh, rl), (ih, il) = split(real), split(imag)
        first, second = factor_ref[0], factor_ref[1]
        return (
            dot(first, side(rh, ih)) + dot(second, side(-ih, rh))
            + dot(first, side(rl, il)) + dot(second, side(-il, rl))
        )

    s = wave_ref.shape[2]
    wave = plain(right_ref, *combine([b0_ref, b1_ref, b2_ref], 0))
    wave_ref[0] = wave[:, :s]
    wave_ref[1] = wave[:, s:]
    wave_copy = pltpu.make_async_copy(wave_ref, wave_hbm, sem.at[0])
    wave_copy.start()
    mixed = combine([c0_ref, c1_ref, c2_ref], 3)
    left_copy.wait()
    data_copy.wait()
    image = plain(left_ref, *mixed)
    res_ref[0] = data_ref[0].astype(F32) - image[:, :s]
    res_ref[1] = data_ref[1].astype(F32) - image[:, s:]
    res_copy = pltpu.make_async_copy(res_ref, res_hbm, sem.at[1])
    res_copy.start()
    wave_copy.wait()
    res_copy.wait()


def lane_limits(limits, rank, width):
    lane = lax.broadcasted_iota(jnp.int32, (1, width), 1)
    limit = jnp.zeros((1, width), jnp.int32)
    for p, value in enumerate(limits):
        limit = jnp.where(lane >= p * rank, value, limit)
    return (lax.rem(lane, rank) < limit).astype(F32)


def packed_gram(real, imag):
    width = real.shape[1]
    both = jnp.concatenate([real, imag], axis=0)
    upper = dot_t(both, both)
    lower = dot_t(real, imag) - dot_t(imag, real)
    row = lax.broadcasted_iota(jnp.int32, (width, width), 0)
    column = lax.broadcasted_iota(jnp.int32, (width, width), 1)
    return jnp.where(row <= column, upper, lower).astype(BF16)


def unpacked_gram(packed):
    width = packed.shape[1]
    here = packed.astype(F32)
    there = here.T
    row = lax.broadcasted_iota(jnp.int32, (width, width), 0)
    column = lax.broadcasted_iota(jnp.int32, (width, width), 1)
    real = jnp.where(row <= column, here, there)
    imag = jnp.where(row > column, here, jnp.where(row < column, -there, 0.0))
    return real.astype(BF16), imag.astype(BF16)


def direct_offsets(half):
    others = [k for k in range(1, half) if k != 2]
    return sorted(others, key=lambda k: (min(k, half - k), k))


def gather_start(
    rank, n, here_ref, mine_ref, ranks_hbm, data_hbm, left_hbm, right_hbm, *refs
):
    ranks_ref, data_ref, left_ref, right_ref, back_ref, sem = refs[-6:]
    half = n // 2
    direct = [0] + direct_offsets(half)
    packets, small = refs[: half - 1], refs[half - 1 : half + 1]
    pairs = [
        (left_hbm, left_ref), (data_hbm, data_ref), (ranks_hbm, ranks_ref),
        (right_hbm, right_ref),
    ]
    copies = [
        pltpu.make_async_copy(source, target, sem.at[k])
        for k, (source, target) in enumerate(pairs)
    ]
    for copy in copies:
        copy.start()
    for copy in copies[:3]:
        copy.wait()
    width = left_ref.shape[2]
    s = data_ref.shape[2]
    q = s // n
    here = here_ref[0]
    keep = lane_limits([ranks_ref[here, p] for p in range(n)], rank, width).astype(BF16)
    real, imag = left_ref[0] * keep, left_ref[1] * keep
    both = side(data_ref[0], data_ref[1])
    first, second = dot_t(both, real), dot_t(both, imag)
    back_ref[0] = (first[:s] + second[s:]).astype(BF16)
    back_ref[1] = (first[s:] - second[:s]).astype(BF16)
    gram = packed_gram(real, imag)
    for packet in packets:
        packet[0:width, :] = gram
    copies[3].wait()
    keep = lane_limits([ranks_ref[p, here] for p in range(n)], rank, width).astype(BF16)
    gram = packed_gram(right_ref[0] * keep, right_ref[1] * keep)
    z, x = lax.div(here, 2), lax.rem(here, 2)
    for packet in packets:
        packet[width + 4 * q :, :] = gram
    for k in range(half):
        base = 2 * lax.rem(z + k, half)
        for block, target in enumerate([base + 1 - x, base + x]):
            rows = pl.ds(pl.multiple_of(target * q, q), q)
            if k == 2:
                out, place = small[block], 0
            else:
                out, place = packets[direct.index(k)], width + 2 * q * block
            out[place : place + q, :] = back_ref[0, rows, :]
            out[place + q : place + 2 * q, :] = back_ref[1, rows, :]


def swap_tiles(rank, source, target):
    n, rows, width = source.shape
    per = 128 // rank
    lane = lax.div(lax.broadcasted_iota(jnp.int32, (rows, 128), 1), rank)
    for g in range(n // per):
        for h in range(width // 128):
            ins = [source[per * g + a, :, 128 * h : 128 * h + 128] for a in range(per)]
            for b in range(per):
                out = None
                for a in range(per):
                    shift = (a - b) * rank % 128
                    piece = pltpu.roll(ins[a], shift, 1) if shift else ins[a]
                    out = piece if out is None else jnp.where(lane == a, piece, out)
                target[per * h + b, :, 128 * g : 128 * g + 128] = out


def apply_tiles(gram_ref, source, target):
    n, rows, _ = source.shape
    q = rows // 2
    for j in range(n):
        high, low = split(source[j])
        vector = jnp.concatenate([high, low], axis=0)
        real, imag = dot(vector, gram_ref[0, j]), dot(vector, gram_ref[1, j])
        real = real[:rows] + real[rows:]
        imag = imag[:rows] + imag[rows:]
        target[j, 0:q, :] = real[:q] + imag[q:]
        target[j, q:rows, :] = real[q:] - imag[:q]


def inner_tiles(first, second):
    n, rows, _ = first.shape
    total = first[0] * second[0]
    for j in range(1, n):
        total = total + first[j] * second[j]
    total = jnp.sum(total, axis=1, keepdims=True)
    return total[: rows // 2] + total[rows // 2 :]


def take_off(target, terms):
    scales = [jnp.concatenate([scale, scale], axis=0) for scale, _ in terms]
    for j in range(target.shape[0]):
        value = target[j]
        for scale, (_, other) in zip(scales, terms):
            value = value - scale * other[j]
        target[j] = value


def chain_kernel(
    rank, n, here_ref, freq_ref, *refs
):
    half = n // 2
    order = [0] + direct_offsets(half) + [2]
    tiles = [refs[:half], refs[half:n]]
    small = refs[n : n + 2]
    b_ref, c_ref, stats_ref, left_ref, right_ref, one_ref, two_ref = refs[n + 2 :]
    width = refs[0].shape[1]
    q = stats_ref.shape[0]
    here = here_ref[0]
    z, x = lax.div(here, 2), lax.rem(here, 2)
    for k in range(half):
        base = 2 * lax.rem(z + half - k, half)
        for other in range(2):
            ref = tiles[other][order.index(k)]
            at = pl.ds(base + (1 - x if other else x), 1)
            grams = (ref[0:width, :], ref[width + 4 * q :, :])
            for packed, gram_ref in zip(grams, (left_ref, right_ref)):
                real, imag = unpacked_gram(packed)
                gram_ref[0, at] = real[None]
                gram_ref[1, at] = imag[None]
            start = width + (0 if other else 2 * q)
            if k == 2:
                block = small[1 - other][...]
            else:
                block = ref[start : start + 2 * q, :]
            one_ref[at] = block.astype(F32)[None]
    b0, b1, b2 = b_ref.at[0], b_ref.at[1], b_ref.at[2]
    c0, c1, c2 = c_ref.at[0], c_ref.at[1], c_ref.at[2]
    swap_tiles(rank, one_ref, b0)
    apply_tiles(right_ref, b0, two_ref)
    m00 = inner_tiles(b0, two_ref)
    swap_tiles(rank, two_ref, c0)
    apply_tiles(left_ref, c0, one_ref)
    n00 = inner_tiles(c0, one_ref)
    theta0 = ratio(n00, m00)
    swap_tiles(rank, one_ref, b1)
    take_off(b1, [(theta0, b0)])
    apply_tiles(right_ref, b1, two_ref)
    m11 = inner_tiles(b1, two_ref)
    m01 = inner_tiles(b0, two_ref)
    swap_tiles(rank, two_ref, c1)
    apply_tiles(left_ref, c1, one_ref)
    n11 = inner_tiles(c1, one_ref)
    n01 = inner_tiles(c0, one_ref)
    theta1 = ratio(n11, m11)
    phi = ratio(n01, m00)
    swap_tiles(rank, one_ref, b2)
    take_off(b2, [(theta1, b1), (phi, b0)])
    apply_tiles(right_ref, b2, two_ref)
    m02 = inner_tiles(b0, two_ref)
    m12 = inner_tiles(b1, two_ref)
    m22 = inner_tiles(b2, two_ref)
    swap_tiles(rank, two_ref, c2)
    apply_tiles(left_ref, c2, one_ref)
    n02 = inner_tiles(c0, one_ref)
    n12 = inner_tiles(c1, one_ref)
    n22 = inner_tiles(c2, one_ref)
    damping = 0.1 + 0.9 * freq_ref[0].astype(F32) / 229.0
    values = [
        n00 + damping * m00, n01 + damping * m01, n02 + damping * m02,
        n11 + damping * m11, n12 + damping * m12, n22 + damping * m22,
        m00, m01, m02, theta0, theta1, phi,
    ]
    lane = lax.broadcasted_iota(jnp.int32, stats_ref.shape, 1)
    block = jnp.full(stats_ref.shape, damping)
    for place, value in enumerate(values):
        block = jnp.where(lane == place, value, block)
    stats_ref[...] = block


def mix_kernel(rank, stats_refs, b_ref, c_ref, out_ref):
    blocks = [ref[...] for ref in stats_refs]
    lane = lax.broadcasted_iota(jnp.int32, blocks[0].shape, 1)
    where_f = [lane == f for f in range(len(blocks))]

    def pick(place):
        value = jnp.zeros_like(blocks[0])
        for f, block in enumerate(blocks):
            shift = (f - place) % 128
            value = jnp.where(where_f[f], pltpu.roll(block, shift, 1) if shift else block, value)
        return value

    h = [[None] * 3 for _ in range(3)]
    for place, (a, b) in enumerate([(0, 0), (0, 1), (0, 2), (1, 1), (1, 2), (2, 2)]):
        h[a][b] = h[b][a] = pick(place)
    u = [pick(6), pick(7), pick(8)]
    theta0, theta1, phi, damping = pick(9), pick(10), pick(11), pick(12)
    x = descend(h, u, theta0, theta1, phi, damping, 1)
    n, rows, _ = b_ref.shape[1:]
    scales = []
    for value in x:
        own = jnp.sum(jnp.where(lane == 0, value, 0.0), axis=1, keepdims=True)
        scales.append(jnp.concatenate([own, own], axis=0))
    for j in range(n):
        for place, ref in enumerate((b_ref, c_ref)):
            value = scales[0] * ref[0, j] + scales[1] * ref[1, j] + scales[2] * ref[2, j]
            out_ref[j, place * rows : (place + 1) * rows, :] = value.astype(BF16)


def home_mix(rank, nfreq, data_hbm, left_hbm, right_hbm, *refs):
    stats_refs = refs[:nfreq]
    b_ref, c_ref, out_ref, data_ref, left_ref, right_ref, sem = refs[nfreq:]
    pairs = [(right_hbm, right_ref), (left_hbm, left_ref), (data_hbm, data_ref)]
    copies = [
        pltpu.make_async_copy(source, target, sem.at[k])
        for k, (source, target) in enumerate(pairs)
    ]
    for copy in copies:
        copy.start()
    mix_kernel(rank, stats_refs, b_ref, c_ref, out_ref)
    for copy in copies:
        copy.wait()


def dot_nt(a, b):
    return lax.dot_general(a, b, (((1,), (1,)), ((), ())), preferred_element_type=F32)


def home_kernel(
    rank, recv_ref, data_ref, left_ref, right_ref, wave_hbm, res_hbm, wave_ref, res_ref, sem
):
    n, rows, width = recv_ref.shape
    q = rows // 4
    s = n * q

    def plain(factor_ref, place):
        real = recv_ref[:, place * q : (place + 1) * q, :].reshape(s, width)
        imag = recv_ref[:, (place + 1) * q : (place + 2) * q, :].reshape(s, width)
        both = jnp.concatenate([real, imag], axis=0)
        first, second = dot_nt(factor_ref[0], both), dot_nt(factor_ref[1], both)
        return first[:, :s] - second[:, s:], first[:, s:] + second[:, :s]

    wave_ref[0], wave_ref[1] = plain(right_ref, 0)
    wave_copy = pltpu.make_async_copy(wave_ref, wave_hbm, sem.at[0])
    wave_copy.start()
    real, imag = plain(left_ref, 2)
    res_ref[0] = data_ref[0].astype(F32) - real
    res_ref[1] = data_ref[1].astype(F32) - imag
    res_copy = pltpu.make_async_copy(res_ref, res_hbm, sem.at[1])
    res_copy.start()
    wave_copy.wait()
    res_copy.wait()


def by_source(data, left, right, ranks, freq_index, ntile, nfreq, here, mine):
    width = left.shape[2]
    rank = width // ntile
    s = data.shape[2]
    q = s // ntile
    half = ntile // 2
    room = (16 << 20) + 64 * width * width

    def like(value):
        return jax.ShapeDtypeStruct(value.shape, value.dtype)

    def call(kernel, specs, args, outs, scratch=(), target=VMEM):
        return pl.pallas_call(
            kernel,
            out_shape=outs,
            in_specs=specs,
            out_specs=[target] * len(outs),
            scratch_shapes=scratch,
            compiler_params=pltpu.CompilerParams(vmem_limit_bytes=room),
        )(*args)

    def along(shift, flip=0):
        return [
            (2 * z + x, 2 * ((z + shift) % half) + (x ^ flip))
            for z in range(half) for x in range(2)
        ]

    across = [(t, t ^ 1) for t in range(ntile)]
    sizes = [2 * width + 4 * q] * (half - 1) + [2 * q, 2 * q]
    direct = direct_offsets(half)
    packets = call(
        functools.partial(gather_start, rank, ntile), [SMEM] * 2 + [HBM] * 4,
        (here, mine, ranks, data, left, right),
        [jax.ShapeDtypeStruct((size, width), BF16) for size in sizes],
        [
            pltpu.SMEM(ranks.shape, jnp.int32),
            pltpu.VMEM(data.shape, BF16),
            pltpu.VMEM(left.shape, BF16),
            pltpu.VMEM(right.shape, BF16),
            pltpu.VMEM((2, s, width), BF16),
            pltpu.SemaphoreType.DMA((4,)),
        ],
    )
    same = [packets[0]] + [
        lax.ppermute(packet, "tcol", along(k)) for packet, k in zip(packets[1:], direct)
    ]
    small = [lax.ppermute(packets[half - block], "tcol", along(2, block)) for block in (1, 0)]
    first = lax.ppermute(packets[0], "tcol", across)
    same[1], first, *small = lax.optimization_barrier((same[1], first, *small))
    same.append(lax.ppermute(same[1], "tcol", along(1)))
    other = [first] + [lax.ppermute(value, "tcol", across) for value in same[1:]]
    vectors = jax.ShapeDtypeStruct((3, ntile, 2 * q, width), F32)
    grams = pltpu.VMEM((2, ntile, width, width), BF16)
    vector = pltpu.VMEM((ntile, 2 * q, width), F32)
    b, c, stats = call(
        functools.partial(chain_kernel, rank, ntile), [SMEM] * 2 + [VMEM] * (ntile + 2),
        (here, freq_index, *same, *other, *small),
        (vectors, vectors, jax.ShapeDtypeStruct((q, 128), F32)),
        [grams, grams, vector, vector],
    )
    gathered = stats[None]
    step = 1
    while step < nfreq:
        pairs = [(f, f ^ step) for f in range(nfreq)]
        gathered = jnp.concatenate([gathered, lax.ppermute(gathered, "freq", pairs)], axis=0)
        step *= 2
    out, data_in, left_in, right_in = call(
        functools.partial(home_mix, rank, nfreq), [HBM] * 3 + [VMEM] * (nfreq + 2),
        (data, left, right, *[gathered[f] for f in range(nfreq)], b, c),
        (
            jax.ShapeDtypeStruct((ntile, 4 * q, width), BF16),
            like(data), like(left), like(right),
        ),
        [pltpu.SemaphoreType.DMA((3,))],
    )
    back = lax.all_to_all(out, "tcol", 0, 0, tiled=True)
    shape = jax.ShapeDtypeStruct(data.shape, F32)
    return call(
        functools.partial(home_kernel, rank), [VMEM] * 4, (back, data_in, left_in, right_in),
        (shape, shape),
        [
            pltpu.VMEM(shape.shape, F32),
            pltpu.VMEM(shape.shape, F32),
            pltpu.SemaphoreType.DMA((2,)),
        ],
        HBM,
    )


def body(data, left_factor, right_factor, ranks, freq_index):
    ntile = lax.axis_size("tcol")
    nfreq = lax.axis_size("freq")
    here = lax.axis_index("tcol").reshape(1)
    mine = lax.axis_index("freq").reshape(1)
    data, left, right, ranks = data[0], left_factor[0], right_factor[0], ranks[0]
    data, left, right, ranks = [
        pltpu.with_memory_space_constraint(value, pltpu.HBM)
        for value in (data, left, right, ranks)
    ]
    width = left.shape[2]
    rank = width // ntile
    s = data.shape[2]
    fits = ntile % 2 == 0 and ntile >= 6 and s % (16 * ntile) == 0 and width % 128 == 0 and 128 % rank == 0
    if fits and nfreq & (nfreq - 1) == 0 and ntile * width * width <= 1 << 20:
        wave, res = by_source(data, left, right, ranks, freq_index, ntile, nfreq, here, mine)
        return wave[None], res[None]
    share = -(-EARLY // ntile)
    height = -(-(LATE + share) // 8) * 8
    field = jax.ShapeDtypeStruct((width, 2 * s), F32)
    sums = jax.ShapeDtypeStruct((8, s), F32)
    bare = jax.ShapeDtypeStruct((ntile, 2 * rank, s), BF16)
    message = jax.ShapeDtypeStruct((ntile, 2 * rank + RIDE, s), BF16)
    gram = jax.ShapeDtypeStruct((width, 2 * width), BF16)
    room = (8 << 20) + 24 * width * width

    def like(value):
        return jax.ShapeDtypeStruct(value.shape, value.dtype)

    def call(kernel, specs, args, outs, scratch=(), target=VMEM):
        return pl.pallas_call(
            functools.partial(kernel, rank),
            out_shape=outs,
            in_specs=specs,
            out_specs=[target] * len(outs),
            scratch_shapes=scratch,
            compiler_params=pltpu.CompilerParams(vmem_limit_bytes=room),
        )(*args)

    def step(kernel, args, outs):
        return call(kernel, [VMEM] * len(args), args, outs)

    def exchange(value):
        return lax.all_to_all(value, "tcol", 0, 0, tiled=True)

    vright, back, damp, out, uhi, ulo, vhi, vlo = call(
        start_kernel, [SMEM] * 2 + [HBM] * 5, (here, mine, ranks, freq_index, data, left, right),
        (like(right), field, sums, bare, gram, gram, gram, gram),
        [
            pltpu.SMEM(ranks.shape, jnp.int32),
            pltpu.SMEM(freq_index.shape, jnp.int32),
            pltpu.VMEM(data.shape, BF16),
            pltpu.VMEM(left.shape, BF16),
            pltpu.SemaphoreType.DMA((5,)),
        ],
    )
    b0 = exchange(out)
    g0, m0, out = step(column0, (b0, vhi, vlo), (field, sums, message))
    c0 = exchange(out)
    n0, out = step(row0, (c0, uhi, ulo, back), (sums, message))
    b1 = exchange(out)
    g1, m1, out = step(column1, (b1, b0, vhi, vlo, g0, n0), (field, sums, message))
    c1 = exchange(out)
    n1, out = step(row1, (c1, c0, uhi, ulo, back), (sums, message))
    b2 = exchange(out)
    m2, out = step(
        column2, (b2, b0, b1, vhi, vlo, g0, g1, damp, m0, n0, m1, n1), (sums, message)
    )
    c2 = exchange(out)
    args = (here, c2, c0, c1, uhi, ulo, back, damp, m1, m2)
    (out,) = call(
        lambda rank, *refs: row2(rank, share, *refs), [SMEM] + [VMEM] * 9, args,
        (jax.ShapeDtypeStruct((nfreq * ntile, height, s), F32),),
        [pltpu.VMEM((max(16, ntile * share), s), F32)],
    )
    everyone = lax.all_to_all(out, ("freq", "tcol"), 0, 0, tiled=True)
    shape = jax.ShapeDtypeStruct(data.shape, F32)
    wave, res = call(
        lambda rank, *refs: finish_kernel(rank, nfreq, share, *refs),
        [SMEM, HBM, HBM] + [VMEM] * 8,
        (mine, data, left, everyone, vright, b0, b1, b2, c0, c1, c2), (shape, shape),
        [
            pltpu.VMEM((LATE + EARLY, nfreq, s), F32),
            pltpu.VMEM((6, nfreq, s), F32),
            pltpu.VMEM(shape.shape, F32),
            pltpu.VMEM(shape.shape, F32),
            pltpu.VMEM(data.shape, BF16),
            pltpu.VMEM(left.shape, BF16),
            pltpu.SemaphoreType.DMA((4,)),
        ],
        HBM,
    )
    return wave[None], res[None]


def solution(mesh):
    in_specs = (
        P("freq", None, "tcol", None),
        P("freq", None, "tcol", None),
        P("freq", None, "tcol", None),
        P("freq", None, None),
        P("freq"),
    )
    out_specs = (P("freq", None, "tcol", None), P("freq", None, "tcol", None))
    return jax.shard_map(body, mesh=mesh, in_specs=in_specs, out_specs=out_specs, check_vma=False)
```

```python
import functools

import jax
import jax.numpy as jnp
from jax import lax
from jax.experimental import pallas as pl
from jax.experimental.pallas import tpu as pltpu
from jax.sharding import PartitionSpec as P


RIDE = 16
LATE = 4
EARLY = 9
VMEM = pl.BlockSpec(memory_space=pltpu.VMEM)
SMEM = pl.BlockSpec(memory_space=pltpu.SMEM)
HBM = pl.BlockSpec(memory_space=pltpu.HBM)
F32 = jnp.float32
BF16 = jnp.bfloat16


def dot(a, b):
    return jnp.dot(a, b, preferred_element_type=F32)


def dot_t(a, b):
    return lax.dot_general(a, b, (((0,), (0,)), ((), ())), preferred_element_type=F32)


def side(real, imag):
    return jnp.concatenate([real, imag], axis=1)


def split(value):
    high = value.astype(BF16)
    return high, (value - high.astype(F32)).astype(BF16)


def unpack(ref, rank):
    n = ref.shape[0]
    real = ref[:, 0:rank, :].reshape(n * rank, ref.shape[2])
    imag = ref[:, rank : 2 * rank, :].reshape(n * rank, ref.shape[2])
    return real, imag


def fields(ref, rank):
    return side(*unpack(ref, rank)).astype(F32)


def send(out_ref, value, rank):
    s = out_ref.shape[2]
    for p in range(out_ref.shape[0]):
        rows = value[p * rank : (p + 1) * rank].astype(BF16)
        out_ref[p, 0:rank, :] = rows[:, :s]
        out_ref[p, rank : 2 * rank, :] = rows[:, s:]


def ride(out_ref, rows, rank):
    rows = rows + [jnp.zeros_like(rows[0])] * (RIDE - len(rows))
    block = jnp.concatenate(rows, axis=0).astype(BF16)
    for p in range(out_ref.shape[0]):
        out_ref[p, 2 * rank : 2 * rank + RIDE, :] = block


def ridden(ref, rank):
    total = ref[0, 2 * rank : 2 * rank + RIDE, :].astype(F32)
    for p in range(1, ref.shape[0]):
        total = total + ref[p, 2 * rank : 2 * rank + RIDE, :].astype(F32)
    return total


def inner(a, b):
    both = jnp.sum(a * b, axis=0, keepdims=True)
    s = both.shape[1] // 2
    return both[:, :s] + both[:, s:]


def twice(row):
    return jnp.concatenate([row, row], axis=1)


def ratio(top, bottom):
    safe = bottom > 0
    return jnp.where(safe, top / jnp.where(safe, bottom, 1.0), 0.0)


def apply_gram(hi_ref, lo_ref, real, imag):
    vector = jnp.concatenate([side(real, imag), side(-imag, real)], axis=0)
    return dot(hi_ref[...], vector) + dot(lo_ref[...], vector)


def make_gram(factor_ref, hi_ref, lo_ref, limits):
    real, imag = factor_ref[0], factor_ref[1]
    width = real.shape[1]
    rank = width // len(limits)
    level = lax.broadcasted_iota(jnp.int32, (rank, width), 0)

    def put(value, place):
        for p, limit in enumerate(limits):
            rows = slice(p * rank, (p + 1) * rank)
            high, low = split(jnp.where(level < limit, value[rows], 0.0))
            hi_ref[rows, place : place + width] = high
            lo_ref[rows, place : place + width] = low

    put(dot_t(real, real) + dot_t(imag, imag), 0)
    put(dot_t(real, imag) - dot_t(imag, real), width)


def start_kernel(
    rank, here_ref, mine_ref, ranks_hbm, freq_hbm, data_hbm, left_hbm, right_hbm,
    right_ref, back_ref, sums_ref, out_ref, uhi_ref, ulo_ref, vhi_ref, vlo_ref,
    ranks_ref, freq_ref, data_ref, left_ref, sem
):
    n = out_ref.shape[0]
    s = out_ref.shape[2]
    pairs = [
        (left_hbm, left_ref), (data_hbm, data_ref), (ranks_hbm, ranks_ref),
        (freq_hbm, freq_ref), (right_hbm, right_ref),
    ]
    copies = [
        pltpu.make_async_copy(source, target, sem.at[k])
        for k, (source, target) in enumerate(pairs)
    ]
    for copy in copies:
        copy.start()
    for copy in copies[:4]:
        copy.wait()
    here = here_ref[0]
    row_limits = [ranks_ref[here, p] for p in range(n)]
    column_limits = [ranks_ref[p, here] for p in range(n)]
    damping = 0.1 + 0.9 * freq_ref[0].astype(F32) / 229.0
    sums_ref[...] = jnp.full(sums_ref.shape, damping)
    real, imag = data_ref[0], data_ref[1]
    back = dot_t(left_ref[0], side(real, imag)) + dot_t(left_ref[1], side(imag, -real))
    level = lax.broadcasted_iota(jnp.int32, (rank, 2 * s), 0)
    back = jnp.concatenate(
        [
            jnp.where(level < limit, back[p * rank : (p + 1) * rank], 0.0)
            for p, limit in enumerate(row_limits)
        ],
        axis=0,
    )
    back_ref[...] = back
    send(out_ref, back, rank)
    make_gram(left_ref, uhi_ref, ulo_ref, row_limits)
    copies[4].wait()
    make_gram(right_ref, vhi_ref, vlo_ref, column_limits)


def column0(rank, b0_ref, hi_ref, lo_ref, g0_ref, sums_ref, out_ref):
    real, imag = unpack(b0_ref, rank)
    g0 = apply_gram(hi_ref, lo_ref, real, imag)
    g0_ref[...] = g0
    m00 = inner(side(real, imag).astype(F32), g0)
    sums_ref[0:1, :] = m00
    send(out_ref, g0, rank)
    ride(out_ref, [m00], rank)


def row0(rank, c0_ref, hi_ref, lo_ref, back_ref, sums_ref, out_ref):
    real, imag = unpack(c0_ref, rank)
    next0 = apply_gram(hi_ref, lo_ref, real, imag)
    c0 = side(real, imag).astype(F32)
    n00 = inner(c0, next0)
    sums_ref[0:1, :] = n00
    sums_ref[1:2, :] = inner(back_ref[...], c0)
    sums_ref[2:3, :] = ridden(c0_ref, rank)[0:1]
    send(out_ref, next0, rank)
    ride(out_ref, [n00], rank)


def column1(
    rank, b1_ref, b0_ref, hi_ref, lo_ref, g0_ref, n0_ref, g1_ref, sums_ref, out_ref
):
    real, imag = unpack(b1_ref, rank)
    theta0 = ratio(ridden(b1_ref, rank)[0:1], n0_ref[2:3, :])
    wide = twice(theta0)
    g1 = apply_gram(hi_ref, lo_ref, real, imag) - wide * g0_ref[...]
    b0 = fields(b0_ref, rank)
    b1 = side(real, imag).astype(F32) - wide * b0
    g1_ref[...] = g1
    m11 = inner(b1, g1)
    sums_ref[0:1, :] = m11
    sums_ref[1:2, :] = inner(b0, g1)
    sums_ref[2:3, :] = theta0
    send(out_ref, g1, rank)
    ride(out_ref, [m11], rank)


def row1(rank, c1_ref, c0_ref, hi_ref, lo_ref, back_ref, sums_ref, out_ref):
    real, imag = unpack(c1_ref, rank)
    next1 = apply_gram(hi_ref, lo_ref, real, imag)
    c1 = side(real, imag).astype(F32)
    n11 = inner(c1, next1)
    n01 = inner(fields(c0_ref, rank), next1)
    sums_ref[0:1, :] = n11
    sums_ref[1:2, :] = n01
    sums_ref[2:3, :] = inner(back_ref[...], c1)
    sums_ref[3:4, :] = ridden(c1_ref, rank)[0:1]
    send(out_ref, next1, rank)
    ride(out_ref, [n11, n01], rank)


def column2(
    rank, b2_ref, b0_ref, b1_ref, hi_ref, lo_ref, g0_ref, g1_ref,
    damp_ref, m0_ref, n0_ref, m1_ref, n1_ref, sums_ref, out_ref
):
    real, imag = unpack(b2_ref, rank)
    came = ridden(b2_ref, rank)
    theta1 = ratio(came[0:1], n1_ref[3:4, :])
    phi = ratio(came[1:2], n0_ref[2:3, :])
    wide1, wide0 = twice(theta1), twice(phi)
    g2 = apply_gram(hi_ref, lo_ref, real, imag) - wide1 * g1_ref[...] - wide0 * g0_ref[...]
    send(out_ref, g2, rank)
    b0 = fields(b0_ref, rank)
    b1 = fields(b1_ref, rank) - twice(m1_ref[2:3, :]) * b0
    b2 = side(real, imag).astype(F32) - wide1 * b1 - wide0 * b0
    sums_ref[0:1, :] = inner(b0, g2)
    sums_ref[1:2, :] = inner(b1, g2)
    sums_ref[2:3, :] = inner(b2, g2)
    sums_ref[3:4, :] = theta1
    sums_ref[4:5, :] = phi
    damping = damp_ref[0:1, :]
    known = [
        n0_ref[0:1, :] + damping * m0_ref[0:1, :],
        n1_ref[1:2, :] + damping * m1_ref[1:2, :],
        n1_ref[0:1, :] + damping * m1_ref[0:1, :],
        n0_ref[1:2, :],
        n1_ref[2:3, :],
    ]
    rest = [row - row.astype(BF16).astype(F32) for row in known]
    ride(out_ref, known + rest, rank)


def row2(
    rank, share, here_ref, c2_ref, c0_ref, c1_ref, hi_ref, lo_ref, back_ref,
    damp_ref, m1_ref, m2_ref, out_ref, table_ref
):
    real, imag = unpack(c2_ref, rank)
    next2 = apply_gram(hi_ref, lo_ref, real, imag)
    damping = damp_ref[0:1, :]
    came = ridden(c2_ref, rank)
    table_ref[0:5, :] = came[0:5] + came[5:10]
    table_ref[5:6, :] = m1_ref[2:3, :]
    table_ref[6:8, :] = m2_ref[3:5, :]
    table_ref[8:9, :] = damping
    rows = [
        inner(fields(c0_ref, rank), next2) + damping * m2_ref[0:1, :],
        inner(fields(c1_ref, rank), next2) + damping * m2_ref[1:2, :],
        inner(side(real, imag).astype(F32), next2) + damping * m2_ref[2:3, :],
        inner(back_ref[...], side(real, imag).astype(F32)),
        table_ref[pl.ds(here_ref[0] * share, share), :],
    ]
    more = out_ref.shape[1] - LATE - share
    if more:
        rows.append(jnp.zeros((more, real.shape[1]), F32))
    block = jnp.concatenate(rows, axis=0)
    for p in range(out_ref.shape[0]):
        out_ref[p] = block


def forms(h, u, g, p, position, size, axis):
    def times(v):
        return [sum(h[a][b] * v[b] for b in range(size)) for a in range(size)]

    def along(a, b):
        return jnp.sum(sum(x * y for x, y in zip(a, b)), axis=axis, keepdims=True)

    hg, hp, hx = times(g), times(p), times(position)
    rest = [u[a] - hx[a] for a in range(size)]
    return along(g, hg), along(p, hg), along(p, hp), along(g, rest), along(p, rest)


def descend(h, u, theta0, theta1, phi, damping, axis):
    one = jnp.ones_like(theta0)
    a11 = jnp.sum(h[0][0], axis=axis, keepdims=True)
    b1 = jnp.sum(u[0], axis=axis, keepdims=True)
    alpha = b1 / (1.1 * a11)
    p = [alpha * one]
    x = [alpha * one]
    for size in (2, 3):
        zero = jnp.zeros_like(one)
        x = x + [zero]
        p = p + [zero]
        if size == 2:
            g = [one - (theta0 + damping) * x[0], -x[0]]
        else:
            g = [
                one - (theta0 + damping) * x[0] - phi * x[1],
                -x[0] - (theta1 + damping) * x[1],
                -x[1],
            ]
        a11, a12, a22, b1, b2 = forms(h, u, g, p, x, size, axis)
        first, second = 1.1 * a11, 1.1 * a22
        determinant = first * second - a12 * a12
        alpha = (b1 * second - a12 * b2) / determinant
        beta = (first * b2 - a12 * b1) / determinant
        p = [alpha * g[a] + beta * p[a] for a in range(size)]
        x = [x[a] + p[a] for a in range(size)]
    return x


def finish_kernel(
    rank, nfreq, share, mine_ref, data_hbm, left_hbm, recv_ref, right_ref,
    b0_ref, b1_ref, b2_ref, c0_ref, c1_ref, c2_ref, wave_hbm, res_hbm,
    table_ref, mix_ref, wave_ref, res_ref, data_ref, left_ref, sem
):
    left_copy = pltpu.make_async_copy(left_hbm, left_ref, sem.at[2])
    data_copy = pltpu.make_async_copy(data_hbm, data_ref, sem.at[3])
    left_copy.start()
    data_copy.start()
    ntile = recv_ref.shape[0] // nfreq
    for f in range(nfreq):
        total = recv_ref[f * ntile]
        for t in range(1, ntile):
            total = total + recv_ref[f * ntile + t]
        table_ref[0:LATE, f, :] = total[0:LATE]
        for q in range(EARLY):
            place = LATE + q % share
            table_ref[LATE + q, f : f + 1, :] = recv_ref[f * ntile + q // share, place : place + 1]
    h = [[None] * 3 for _ in range(3)]
    places = [(0, 0, 2), (1, 1, 2), (2, 2, 2), (4, 0, 0), (5, 0, 1), (6, 1, 1)]
    for place, a, b in places:
        h[a][b] = h[b][a] = table_ref[place]
    u = [table_ref[7], table_ref[8], table_ref[3]]
    theta0, theta1, phi, damping = [table_ref[9 + a] for a in range(4)]
    x = descend(h, u, theta0, theta1, phi, damping, 0)
    mix_ref[0] = x[0] - theta0 * x[1] + (theta0 * theta1 - phi) * x[2]
    mix_ref[1] = x[1] - theta1 * x[2]
    mix_ref[2] = x[2]
    mix_ref[3] = x[0]
    mix_ref[4] = x[1]
    mix_ref[5] = x[2]
    row = pl.ds(mine_ref[0], 1)

    def combine(refs, offset):
        total = None
        for k, ref in enumerate(refs):
            scale = mix_ref[offset + k, row, :]
            real, imag = unpack(ref, rank)
            term = (scale * real.astype(F32), scale * imag.astype(F32))
            total = term if total is None else (total[0] + term[0], total[1] + term[1])
        return total

    def plain(factor_ref, real, imag):
        (rh, rl), (ih, il) = split(real), split(imag)
        first, second = factor_ref[0], factor_ref[1]
        return (
            dot(first, side(rh, ih)) + dot(second, side(-ih, rh))
            + dot(first, side(rl, il)) + dot(second, side(-il, rl))
        )

    s = wave_ref.shape[2]
    wave = plain(right_ref, *combine([b0_ref, b1_ref, b2_ref], 0))
    wave_ref[0] = wave[:, :s]
    wave_ref[1] = wave[:, s:]
    wave_copy = pltpu.make_async_copy(wave_ref, wave_hbm, sem.at[0])
    wave_copy.start()
    mixed = combine([c0_ref, c1_ref, c2_ref], 3)
    left_copy.wait()
    data_copy.wait()
    image = plain(left_ref, *mixed)
    res_ref[0] = data_ref[0].astype(F32) - image[:, :s]
    res_ref[1] = data_ref[1].astype(F32) - image[:, s:]
    res_copy = pltpu.make_async_copy(res_ref, res_hbm, sem.at[1])
    res_copy.start()
    wave_copy.wait()
    res_copy.wait()


def lane_limits(limits, rank, width):
    lane = lax.broadcasted_iota(jnp.int32, (1, width), 1)
    limit = jnp.zeros((1, width), jnp.int32)
    for p, value in enumerate(limits):
        limit = jnp.where(lane >= p * rank, value, limit)
    return (lax.rem(lane, rank) < limit).astype(F32)


def packed_gram(real, imag):
    width = real.shape[1]
    both = jnp.concatenate([real, imag], axis=0)
    upper = dot_t(both, both)
    lower = dot_t(real, imag) - dot_t(imag, real)
    row = lax.broadcasted_iota(jnp.int32, (width, width), 0)
    column = lax.broadcasted_iota(jnp.int32, (width, width), 1)
    return jnp.where(row <= column, upper, lower).astype(BF16)


def unpacked_gram(packed):
    width = packed.shape[1]
    here = packed.astype(F32)
    there = here.T
    row = lax.broadcasted_iota(jnp.int32, (width, width), 0)
    column = lax.broadcasted_iota(jnp.int32, (width, width), 1)
    real = jnp.where(row <= column, here, there)
    imag = jnp.where(row > column, here, jnp.where(row < column, -there, 0.0))
    return real.astype(BF16), imag.astype(BF16)


def direct_offsets(half):
    others = [k for k in range(1, half) if k != 2]
    return sorted(others, key=lambda k: (min(k, half - k), k))


def start_left(rank, n, here_ref, mine_ref, ranks_hbm, data_hbm, left_hbm, *refs):
    ranks_ref, data_ref, left_ref, back_ref, sem = refs[-5:]
    half = n // 2
    direct = [0] + direct_offsets(half)
    packets, small, own = refs[: half - 1], refs[half - 1 : half + 1], refs[half + 1]
    pairs = [(left_hbm, left_ref), (data_hbm, data_ref), (ranks_hbm, ranks_ref)]
    copies = [
        pltpu.make_async_copy(source, target, sem.at[k])
        for k, (source, target) in enumerate(pairs)
    ]
    for copy in copies:
        copy.start()
    for copy in copies:
        copy.wait()
    width = left_ref.shape[2]
    s = data_ref.shape[2]
    q = s // n
    here = here_ref[0]
    keep = lane_limits([ranks_ref[here, p] for p in range(n)], rank, width).astype(BF16)
    real, imag = left_ref[0] * keep, left_ref[1] * keep
    both = side(data_ref[0], data_ref[1])
    first, second = dot_t(both, real), dot_t(both, imag)
    back_ref[0] = (first[:s] + second[s:]).astype(BF16)
    back_ref[1] = (first[s:] - second[:s]).astype(BF16)
    gram = packed_gram(real, imag)
    for packet in packets:
        packet[0:width, :] = gram
    z, x = lax.div(here, 2), lax.rem(here, 2)
    for k in range(half):
        base = 2 * lax.rem(z + k, half)
        for block, target in enumerate([base + 1 - x, base + x]):
            rows = pl.ds(pl.multiple_of(target * q, q), q)
            if k == 2:
                out, place = small[block], 0
            elif k == 0 and block == 1:
                out, place = own, 0
            else:
                out, place = packets[direct.index(k)], width + 2 * q * block
            out[place : place + q, :] = back_ref[0, rows, :]
            out[place + q : place + 2 * q, :] = back_ref[1, rows, :]


def start_right(rank, n, here_ref, ranks_hbm, right_hbm, out_ref, ranks_ref, right_ref, sem):
    copies = [
        pltpu.make_async_copy(right_hbm, right_ref, sem.at[0]),
        pltpu.make_async_copy(ranks_hbm, ranks_ref, sem.at[1]),
    ]
    for copy in copies:
        copy.start()
    for copy in copies:
        copy.wait()
    here = here_ref[0]
    width = right_ref.shape[2]
    keep = lane_limits([ranks_ref[p, here] for p in range(n)], rank, width).astype(BF16)
    out_ref[...] = packed_gram(right_ref[0] * keep, right_ref[1] * keep)


def swap_tiles(rank, source, target):
    n, rows, width = source.shape
    per = 128 // rank
    lane = lax.div(lax.broadcasted_iota(jnp.int32, (rows, 128), 1), rank)
    for g in range(n // per):
        for h in range(width // 128):
            ins = [source[per * g + a, :, 128 * h : 128 * h + 128] for a in range(per)]
            for b in range(per):
                out = None
                for a in range(per):
                    shift = (a - b) * rank % 128
                    piece = pltpu.roll(ins[a], shift, 1) if shift else ins[a]
                    out = piece if out is None else jnp.where(lane == a, piece, out)
                target[per * h + b, :, 128 * g : 128 * g + 128] = out


def apply_tiles(gram_ref, source, target):
    n, rows, _ = source.shape
    q = rows // 2
    for j in range(n):
        high, low = split(source[j])
        vector = jnp.concatenate([high, low], axis=0)
        real, imag = dot(vector, gram_ref[0, j]), dot(vector, gram_ref[1, j])
        real = real[:rows] + real[rows:]
        imag = imag[:rows] + imag[rows:]
        target[j, 0:q, :] = real[:q] + imag[q:]
        target[j, q:rows, :] = real[q:] - imag[:q]


def inner_tiles(first, second):
    n, rows, _ = first.shape
    total = first[0] * second[0]
    for j in range(1, n):
        total = total + first[j] * second[j]
    total = jnp.sum(total, axis=1, keepdims=True)
    return total[: rows // 2] + total[rows // 2 :]


def take_off(target, terms):
    scales = [jnp.concatenate([scale, scale], axis=0) for scale, _ in terms]
    for j in range(target.shape[0]):
        value = target[j]
        for scale, (_, other) in zip(scales, terms):
            value = value - scale * other[j]
        target[j] = value


def chain_kernel(
    rank, n, here_ref, freq_ref, *refs
):
    half = n // 2
    order = [0] + direct_offsets(half) + [2]
    lefts = [refs[:half], refs[half:n]]
    rights = [refs[n : n + half], refs[n + half : 2 * n]]
    small, own = refs[2 * n : 2 * n + 2], refs[2 * n + 2]
    b_ref, c_ref, stats_ref, left_ref, right_ref, one_ref, two_ref = refs[2 * n + 3 :]
    width = refs[0].shape[1]
    q = stats_ref.shape[0]
    here = here_ref[0]
    z, x = lax.div(here, 2), lax.rem(here, 2)
    for k in range(half):
        base = 2 * lax.rem(z + half - k, half)
        for other in range(2):
            ref = lefts[other][order.index(k)]
            at = pl.ds(base + (1 - x if other else x), 1)
            grams = (ref[0:width, :], rights[other][order.index(k)][...])
            for packed, gram_ref in zip(grams, (left_ref, right_ref)):
                real, imag = unpacked_gram(packed)
                gram_ref[0, at] = real[None]
                gram_ref[1, at] = imag[None]
            start = width + (0 if other else 2 * q)
            if k == 2:
                block = small[1 - other][...]
            elif k == 0 and not other:
                block = own[...]
            else:
                block = ref[start : start + 2 * q, :]
            one_ref[at] = block.astype(F32)[None]
    b0, b1, b2 = b_ref.at[0], b_ref.at[1], b_ref.at[2]
    c0, c1, c2 = c_ref.at[0], c_ref.at[1], c_ref.at[2]
    swap_tiles(rank, one_ref, b0)
    apply_tiles(right_ref, b0, two_ref)
    m00 = inner_tiles(b0, two_ref)
    swap_tiles(rank, two_ref, c0)
    apply_tiles(left_ref, c0, one_ref)
    n00 = inner_tiles(c0, one_ref)
    theta0 = ratio(n00, m00)
    swap_tiles(rank, one_ref, b1)
    take_off(b1, [(theta0, b0)])
    apply_tiles(right_ref, b1, two_ref)
    m11 = inner_tiles(b1, two_ref)
    m01 = inner_tiles(b0, two_ref)
    swap_tiles(rank, two_ref, c1)
    apply_tiles(left_ref, c1, one_ref)
    n11 = inner_tiles(c1, one_ref)
    n01 = inner_tiles(c0, one_ref)
    theta1 = ratio(n11, m11)
    phi = ratio(n01, m00)
    swap_tiles(rank, one_ref, b2)
    take_off(b2, [(theta1, b1), (phi, b0)])
    apply_tiles(right_ref, b2, two_ref)
    m02 = inner_tiles(b0, two_ref)
    m12 = inner_tiles(b1, two_ref)
    m22 = inner_tiles(b2, two_ref)
    swap_tiles(rank, two_ref, c2)
    apply_tiles(left_ref, c2, one_ref)
    n02 = inner_tiles(c0, one_ref)
    n12 = inner_tiles(c1, one_ref)
    n22 = inner_tiles(c2, one_ref)
    damping = 0.1 + 0.9 * freq_ref[0].astype(F32) / 229.0
    values = [
        n00 + damping * m00, n01 + damping * m01, n02 + damping * m02,
        n11 + damping * m11, n12 + damping * m12, n22 + damping * m22,
        m00, m01, m02, theta0, theta1, phi,
    ]
    lane = lax.broadcasted_iota(jnp.int32, stats_ref.shape, 1)
    block = jnp.full(stats_ref.shape, damping)
    for place, value in enumerate(values):
        block = jnp.where(lane == place, value, block)
    stats_ref[...] = block


def mix_kernel(stats_refs, b_ref, c_ref, out_ref):
    blocks = [ref[...] for ref in stats_refs]
    lane = lax.broadcasted_iota(jnp.int32, blocks[0].shape, 1)
    where_f = [lane == f for f in range(len(blocks))]

    def pick(place):
        value = jnp.zeros_like(blocks[0])
        for f, block in enumerate(blocks):
            shift = (f - place) % 128
            value = jnp.where(where_f[f], pltpu.roll(block, shift, 1) if shift else block, value)
        return value

    h = [[None] * 3 for _ in range(3)]
    for place, (a, b) in enumerate([(0, 0), (0, 1), (0, 2), (1, 1), (1, 2), (2, 2)]):
        h[a][b] = h[b][a] = pick(place)
    u = [pick(6), pick(7), pick(8)]
    theta0, theta1, phi, damping = pick(9), pick(10), pick(11), pick(12)
    x = descend(h, u, theta0, theta1, phi, damping, 1)
    n, rows, _ = b_ref.shape[1:]
    scales = []
    for value in x:
        own = jnp.sum(jnp.where(lane == 0, value, 0.0), axis=1, keepdims=True)
        scales.append(jnp.concatenate([own, own], axis=0))
    for j in range(n):
        for place, ref in enumerate((b_ref, c_ref)):
            value = scales[0] * ref[0, j] + scales[1] * ref[1, j] + scales[2] * ref[2, j]
            out_ref[j, place * rows : (place + 1) * rows, :] = value.astype(BF16)


def home_mix(nfreq, data_hbm, left_hbm, right_hbm, *refs):
    stats_refs = refs[:nfreq]
    b_ref, c_ref, out_ref, data_ref, left_ref, right_ref, sem = refs[nfreq:]
    pairs = [(right_hbm, right_ref), (left_hbm, left_ref), (data_hbm, data_ref)]
    copies = [
        pltpu.make_async_copy(source, target, sem.at[k])
        for k, (source, target) in enumerate(pairs)
    ]
    for copy in copies:
        copy.start()
    mix_kernel(stats_refs, b_ref, c_ref, out_ref)
    for copy in copies:
        copy.wait()


def dot_nt(a, b):
    return lax.dot_general(a, b, (((1,), (1,)), ((), ())), preferred_element_type=F32)


def home_kernel(
    recv_ref, data_ref, left_ref, right_ref, wave_hbm, res_hbm, wave_ref, res_ref, sem
):
    n, rows, width = recv_ref.shape
    q = rows // 4
    s = n * q

    def plain(factor_ref, place):
        real = recv_ref[:, place * q : (place + 1) * q, :].reshape(s, width)
        imag = recv_ref[:, (place + 1) * q : (place + 2) * q, :].reshape(s, width)
        both = jnp.concatenate([real, imag], axis=0)
        first, second = dot_nt(factor_ref[0], both), dot_nt(factor_ref[1], both)
        return first[:, :s] - second[:, s:], first[:, s:] + second[:, :s]

    wave_ref[0], wave_ref[1] = plain(right_ref, 0)
    wave_copy = pltpu.make_async_copy(wave_ref, wave_hbm, sem.at[0])
    wave_copy.start()
    real, imag = plain(left_ref, 2)
    res_ref[0] = data_ref[0].astype(F32) - real
    res_ref[1] = data_ref[1].astype(F32) - imag
    res_copy = pltpu.make_async_copy(res_ref, res_hbm, sem.at[1])
    res_copy.start()
    wave_copy.wait()
    res_copy.wait()


def by_source(data, left, right, ranks, freq_index, ntile, nfreq, here, mine):
    width = left.shape[2]
    rank = width // ntile
    s = data.shape[2]
    q = s // ntile
    half = ntile // 2
    room = (16 << 20) + 64 * width * width

    def like(value):
        return jax.ShapeDtypeStruct(value.shape, value.dtype)

    def call(kernel, specs, args, outs, scratch=(), target=VMEM):
        return pl.pallas_call(
            kernel,
            out_shape=outs,
            in_specs=specs,
            out_specs=[target] * len(outs),
            scratch_shapes=scratch,
            compiler_params=pltpu.CompilerParams(vmem_limit_bytes=room),
        )(*args)

    def along(shift, flip=0):
        return [
            (2 * z + x, 2 * ((z + shift) % half) + (x ^ flip))
            for z in range(half) for x in range(2)
        ]

    across = [(t, t ^ 1) for t in range(ntile)]
    sizes = [width + 2 * q] + [width + 4 * q] * (half - 2) + [2 * q] * 3
    direct = direct_offsets(half)
    parts = call(
        functools.partial(start_left, rank, ntile), [SMEM] * 2 + [HBM] * 3,
        (here, mine, ranks, data, left),
        [jax.ShapeDtypeStruct((size, width), BF16) for size in sizes],
        [
            pltpu.SMEM(ranks.shape, jnp.int32),
            pltpu.VMEM(data.shape, BF16),
            pltpu.VMEM(left.shape, BF16),
            pltpu.VMEM((2, s, width), BF16),
            pltpu.SemaphoreType.DMA((3,)),
        ],
    )
    (gram,) = call(
        functools.partial(start_right, rank, ntile), [SMEM] + [HBM] * 2, (here, ranks, right),
        [jax.ShapeDtypeStruct((width, width), BF16)],
        [
            pltpu.SMEM(ranks.shape, jnp.int32),
            pltpu.VMEM(right.shape, BF16),
            pltpu.SemaphoreType.DMA((2,)),
        ],
    )

    def hop(value, pairs):
        return lax.ppermute(value, "tcol", pairs)

    lefts, rights = [parts[0]], [gram]
    cross = [hop(parts[0], across), hop(gram, across)]
    for place, k in enumerate(direct):
        first, second = parts[1 + place], gram
        if place:
            first, _ = lax.optimization_barrier((first, lefts[-1]))
            second, _ = lax.optimization_barrier((second, rights[-1]))
        lefts.append(hop(first, along(k)))
        rights.append(hop(second, along(k)))
    small = [hop(parts[half - block], along(2, block)) for block in (1, 0)]
    first, _ = lax.optimization_barrier((lefts[1][:width], lefts[-1]))
    second, _ = lax.optimization_barrier((rights[1], rights[-1]))
    lefts.append(hop(first, along(1)))
    rights.append(hop(second, along(1)))
    other_lefts, other_rights = cross[:1], cross[1:]
    for place in range(1, half):
        other_lefts.append(hop(lefts[place], across))
        other_rights.append(hop(rights[place], across))
    packets = (*lefts, *other_lefts, *rights, *other_rights, *small, parts[half + 1])
    vectors = jax.ShapeDtypeStruct((3, ntile, 2 * q, width), F32)
    grams = pltpu.VMEM((2, ntile, width, width), BF16)
    vector = pltpu.VMEM((ntile, 2 * q, width), F32)
    b, c, stats = call(
        functools.partial(chain_kernel, rank, ntile), [SMEM] * 2 + [VMEM] * len(packets),
        (here, freq_index, *packets),
        (vectors, vectors, jax.ShapeDtypeStruct((q, 128), F32)),
        [grams, grams, vector, vector],
    )
    gathered = [stats] + [
        lax.ppermute(stats, "freq", [(f, f ^ step) for f in range(nfreq)])
        for step in range(1, nfreq)
    ]
    out, data_in, left_in, right_in = call(
        functools.partial(home_mix, nfreq), [HBM] * 3 + [VMEM] * (nfreq + 2),
        (data, left, right, *gathered, b, c),
        (
            jax.ShapeDtypeStruct((ntile, 4 * q, width), BF16),
            like(data), like(left), like(right),
        ),
        [pltpu.SemaphoreType.DMA((3,))],
    )
    back = lax.all_to_all(out, "tcol", 0, 0, tiled=True)
    shape = jax.ShapeDtypeStruct(data.shape, F32)
    return call(
        home_kernel, [VMEM] * 4, (back, data_in, left_in, right_in),
        (shape, shape),
        [
            pltpu.VMEM(shape.shape, F32),
            pltpu.VMEM(shape.shape, F32),
            pltpu.SemaphoreType.DMA((2,)),
        ],
        HBM,
    )


def body(data, left_factor, right_factor, ranks, freq_index):
    ntile = lax.axis_size("tcol")
    nfreq = lax.axis_size("freq")
    here = lax.axis_index("tcol").reshape(1)
    mine = lax.axis_index("freq").reshape(1)
    data, left, right, ranks = data[0], left_factor[0], right_factor[0], ranks[0]
    data, left, right, ranks = [
        pltpu.with_memory_space_constraint(value, pltpu.HBM)
        for value in (data, left, right, ranks)
    ]
    width = left.shape[2]
    rank = width // ntile
    s = data.shape[2]
    fits = ntile % 2 == 0 and ntile >= 6 and s % (16 * ntile) == 0 and width % 128 == 0 and 128 % rank == 0
    if fits and nfreq & (nfreq - 1) == 0 and ntile * width * width <= 1 << 20:
        wave, res = by_source(data, left, right, ranks, freq_index, ntile, nfreq, here, mine)
        return wave[None], res[None]
    share = -(-EARLY // ntile)
    height = -(-(LATE + share) // 8) * 8
    field = jax.ShapeDtypeStruct((width, 2 * s), F32)
    sums = jax.ShapeDtypeStruct((8, s), F32)
    bare = jax.ShapeDtypeStruct((ntile, 2 * rank, s), BF16)
    message = jax.ShapeDtypeStruct((ntile, 2 * rank + RIDE, s), BF16)
    gram = jax.ShapeDtypeStruct((width, 2 * width), BF16)
    room = (8 << 20) + 24 * width * width

    def like(value):
        return jax.ShapeDtypeStruct(value.shape, value.dtype)

    def call(kernel, specs, args, outs, scratch=(), target=VMEM):
        return pl.pallas_call(
            functools.partial(kernel, rank),
            out_shape=outs,
            in_specs=specs,
            out_specs=[target] * len(outs),
            scratch_shapes=scratch,
            compiler_params=pltpu.CompilerParams(vmem_limit_bytes=room),
        )(*args)

    def step(kernel, args, outs):
        return call(kernel, [VMEM] * len(args), args, outs)

    def exchange(value):
        return lax.all_to_all(value, "tcol", 0, 0, tiled=True)

    vright, back, damp, out, uhi, ulo, vhi, vlo = call(
        start_kernel, [SMEM] * 2 + [HBM] * 5, (here, mine, ranks, freq_index, data, left, right),
        (like(right), field, sums, bare, gram, gram, gram, gram),
        [
            pltpu.SMEM(ranks.shape, jnp.int32),
            pltpu.SMEM(freq_index.shape, jnp.int32),
            pltpu.VMEM(data.shape, BF16),
            pltpu.VMEM(left.shape, BF16),
            pltpu.SemaphoreType.DMA((5,)),
        ],
    )
    b0 = exchange(out)
    g0, m0, out = step(column0, (b0, vhi, vlo), (field, sums, message))
    c0 = exchange(out)
    n0, out = step(row0, (c0, uhi, ulo, back), (sums, message))
    b1 = exchange(out)
    g1, m1, out = step(column1, (b1, b0, vhi, vlo, g0, n0), (field, sums, message))
    c1 = exchange(out)
    n1, out = step(row1, (c1, c0, uhi, ulo, back), (sums, message))
    b2 = exchange(out)
    m2, out = step(
        column2, (b2, b0, b1, vhi, vlo, g0, g1, damp, m0, n0, m1, n1), (sums, message)
    )
    c2 = exchange(out)
    args = (here, c2, c0, c1, uhi, ulo, back, damp, m1, m2)
    (out,) = call(
        lambda rank, *refs: row2(rank, share, *refs), [SMEM] + [VMEM] * 9, args,
        (jax.ShapeDtypeStruct((nfreq * ntile, height, s), F32),),
        [pltpu.VMEM((max(16, ntile * share), s), F32)],
    )
    everyone = lax.all_to_all(out, ("freq", "tcol"), 0, 0, tiled=True)
    shape = jax.ShapeDtypeStruct(data.shape, F32)
    wave, res = call(
        lambda rank, *refs: finish_kernel(rank, nfreq, share, *refs),
        [SMEM, HBM, HBM] + [VMEM] * 8,
        (mine, data, left, everyone, vright, b0, b1, b2, c0, c1, c2), (shape, shape),
        [
            pltpu.VMEM((LATE + EARLY, nfreq, s), F32),
            pltpu.VMEM((6, nfreq, s), F32),
            pltpu.VMEM(shape.shape, F32),
            pltpu.VMEM(shape.shape, F32),
            pltpu.VMEM(data.shape, BF16),
            pltpu.VMEM(left.shape, BF16),
            pltpu.SemaphoreType.DMA((4,)),
        ],
        HBM,
    )
    return wave[None], res[None]


def solution(mesh):
    in_specs = (
        P("freq", None, "tcol", None),
        P("freq", None, "tcol", None),
        P("freq", None, "tcol", None),
        P("freq", None, None),
        P("freq"),
    )
    out_specs = (P("freq", None, "tcol", None), P("freq", None, "tcol", None))
    return jax.shard_map(body, mesh=mesh, in_specs=in_specs, out_specs=out_specs, check_vma=False)
```

```python
import functools

import jax
import jax.numpy as jnp
from jax import lax
from jax.experimental import pallas as pl
from jax.experimental.pallas import tpu as pltpu
from jax.sharding import PartitionSpec as P


RIDE = 16
LATE = 4
EARLY = 9
VMEM = pl.BlockSpec(memory_space=pltpu.VMEM)
SMEM = pl.BlockSpec(memory_space=pltpu.SMEM)
HBM = pl.BlockSpec(memory_space=pltpu.HBM)
F32 = jnp.float32
BF16 = jnp.bfloat16


def dot(a, b):
    return jnp.dot(a, b, preferred_element_type=F32)


def dot_t(a, b):
    return lax.dot_general(a, b, (((0,), (0,)), ((), ())), preferred_element_type=F32)


def side(real, imag):
    return jnp.concatenate([real, imag], axis=1)


def split(value):
    high = value.astype(BF16)
    return high, (value - high.astype(F32)).astype(BF16)


def unpack(ref, rank):
    n = ref.shape[0]
    real = ref[:, 0:rank, :].reshape(n * rank, ref.shape[2])
    imag = ref[:, rank : 2 * rank, :].reshape(n * rank, ref.shape[2])
    return real, imag


def fields(ref, rank):
    return side(*unpack(ref, rank)).astype(F32)


def send(out_ref, value, rank):
    s = out_ref.shape[2]
    for p in range(out_ref.shape[0]):
        rows = value[p * rank : (p + 1) * rank].astype(BF16)
        out_ref[p, 0:rank, :] = rows[:, :s]
        out_ref[p, rank : 2 * rank, :] = rows[:, s:]


def ride(out_ref, rows, rank):
    rows = rows + [jnp.zeros_like(rows[0])] * (RIDE - len(rows))
    block = jnp.concatenate(rows, axis=0).astype(BF16)
    for p in range(out_ref.shape[0]):
        out_ref[p, 2 * rank : 2 * rank + RIDE, :] = block


def ridden(ref, rank):
    total = ref[0, 2 * rank : 2 * rank + RIDE, :].astype(F32)
    for p in range(1, ref.shape[0]):
        total = total + ref[p, 2 * rank : 2 * rank + RIDE, :].astype(F32)
    return total


def inner(a, b):
    both = jnp.sum(a * b, axis=0, keepdims=True)
    s = both.shape[1] // 2
    return both[:, :s] + both[:, s:]


def twice(row):
    return jnp.concatenate([row, row], axis=1)


def ratio(top, bottom):
    safe = bottom > 0
    return jnp.where(safe, top / jnp.where(safe, bottom, 1.0), 0.0)


def apply_gram(hi_ref, lo_ref, real, imag):
    vector = jnp.concatenate([side(real, imag), side(-imag, real)], axis=0)
    return dot(hi_ref[...], vector) + dot(lo_ref[...], vector)


def make_gram(factor_ref, hi_ref, lo_ref, limits):
    real, imag = factor_ref[0], factor_ref[1]
    width = real.shape[1]
    rank = width // len(limits)
    level = lax.broadcasted_iota(jnp.int32, (rank, width), 0)

    def put(value, place):
        for p, limit in enumerate(limits):
            rows = slice(p * rank, (p + 1) * rank)
            high, low = split(jnp.where(level < limit, value[rows], 0.0))
            hi_ref[rows, place : place + width] = high
            lo_ref[rows, place : place + width] = low

    put(dot_t(real, real) + dot_t(imag, imag), 0)
    put(dot_t(real, imag) - dot_t(imag, real), width)


def start_kernel(
    rank, here_ref, mine_ref, ranks_hbm, freq_hbm, data_hbm, left_hbm, right_hbm,
    right_ref, back_ref, sums_ref, out_ref, uhi_ref, ulo_ref, vhi_ref, vlo_ref,
    ranks_ref, freq_ref, data_ref, left_ref, sem
):
    n = out_ref.shape[0]
    s = out_ref.shape[2]
    pairs = [
        (left_hbm, left_ref), (data_hbm, data_ref), (ranks_hbm, ranks_ref),
        (freq_hbm, freq_ref), (right_hbm, right_ref),
    ]
    copies = [
        pltpu.make_async_copy(source, target, sem.at[k])
        for k, (source, target) in enumerate(pairs)
    ]
    for copy in copies:
        copy.start()
    for copy in copies[:4]:
        copy.wait()
    here = here_ref[0]
    row_limits = [ranks_ref[here, p] for p in range(n)]
    column_limits = [ranks_ref[p, here] for p in range(n)]
    damping = 0.1 + 0.9 * freq_ref[0].astype(F32) / 229.0
    sums_ref[...] = jnp.full(sums_ref.shape, damping)
    real, imag = data_ref[0], data_ref[1]
    back = dot_t(left_ref[0], side(real, imag)) + dot_t(left_ref[1], side(imag, -real))
    level = lax.broadcasted_iota(jnp.int32, (rank, 2 * s), 0)
    back = jnp.concatenate(
        [
            jnp.where(level < limit, back[p * rank : (p + 1) * rank], 0.0)
            for p, limit in enumerate(row_limits)
        ],
        axis=0,
    )
    back_ref[...] = back
    send(out_ref, back, rank)
    make_gram(left_ref, uhi_ref, ulo_ref, row_limits)
    copies[4].wait()
    make_gram(right_ref, vhi_ref, vlo_ref, column_limits)


def column0(rank, b0_ref, hi_ref, lo_ref, g0_ref, sums_ref, out_ref):
    real, imag = unpack(b0_ref, rank)
    g0 = apply_gram(hi_ref, lo_ref, real, imag)
    g0_ref[...] = g0
    m00 = inner(side(real, imag).astype(F32), g0)
    sums_ref[0:1, :] = m00
    send(out_ref, g0, rank)
    ride(out_ref, [m00], rank)


def row0(rank, c0_ref, hi_ref, lo_ref, back_ref, sums_ref, out_ref):
    real, imag = unpack(c0_ref, rank)
    next0 = apply_gram(hi_ref, lo_ref, real, imag)
    c0 = side(real, imag).astype(F32)
    n00 = inner(c0, next0)
    sums_ref[0:1, :] = n00
    sums_ref[1:2, :] = inner(back_ref[...], c0)
    sums_ref[2:3, :] = ridden(c0_ref, rank)[0:1]
    send(out_ref, next0, rank)
    ride(out_ref, [n00], rank)


def column1(
    rank, b1_ref, b0_ref, hi_ref, lo_ref, g0_ref, n0_ref, g1_ref, sums_ref, out_ref
):
    real, imag = unpack(b1_ref, rank)
    theta0 = ratio(ridden(b1_ref, rank)[0:1], n0_ref[2:3, :])
    wide = twice(theta0)
    g1 = apply_gram(hi_ref, lo_ref, real, imag) - wide * g0_ref[...]
    b0 = fields(b0_ref, rank)
    b1 = side(real, imag).astype(F32) - wide * b0
    g1_ref[...] = g1
    m11 = inner(b1, g1)
    sums_ref[0:1, :] = m11
    sums_ref[1:2, :] = inner(b0, g1)
    sums_ref[2:3, :] = theta0
    send(out_ref, g1, rank)
    ride(out_ref, [m11], rank)


def row1(rank, c1_ref, c0_ref, hi_ref, lo_ref, back_ref, sums_ref, out_ref):
    real, imag = unpack(c1_ref, rank)
    next1 = apply_gram(hi_ref, lo_ref, real, imag)
    c1 = side(real, imag).astype(F32)
    n11 = inner(c1, next1)
    n01 = inner(fields(c0_ref, rank), next1)
    sums_ref[0:1, :] = n11
    sums_ref[1:2, :] = n01
    sums_ref[2:3, :] = inner(back_ref[...], c1)
    sums_ref[3:4, :] = ridden(c1_ref, rank)[0:1]
    send(out_ref, next1, rank)
    ride(out_ref, [n11, n01], rank)


def column2(
    rank, b2_ref, b0_ref, b1_ref, hi_ref, lo_ref, g0_ref, g1_ref,
    damp_ref, m0_ref, n0_ref, m1_ref, n1_ref, sums_ref, out_ref
):
    real, imag = unpack(b2_ref, rank)
    came = ridden(b2_ref, rank)
    theta1 = ratio(came[0:1], n1_ref[3:4, :])
    phi = ratio(came[1:2], n0_ref[2:3, :])
    wide1, wide0 = twice(theta1), twice(phi)
    g2 = apply_gram(hi_ref, lo_ref, real, imag) - wide1 * g1_ref[...] - wide0 * g0_ref[...]
    send(out_ref, g2, rank)
    b0 = fields(b0_ref, rank)
    b1 = fields(b1_ref, rank) - twice(m1_ref[2:3, :]) * b0
    b2 = side(real, imag).astype(F32) - wide1 * b1 - wide0 * b0
    sums_ref[0:1, :] = inner(b0, g2)
    sums_ref[1:2, :] = inner(b1, g2)
    sums_ref[2:3, :] = inner(b2, g2)
    sums_ref[3:4, :] = theta1
    sums_ref[4:5, :] = phi
    damping = damp_ref[0:1, :]
    known = [
        n0_ref[0:1, :] + damping * m0_ref[0:1, :],
        n1_ref[1:2, :] + damping * m1_ref[1:2, :],
        n1_ref[0:1, :] + damping * m1_ref[0:1, :],
        n0_ref[1:2, :],
        n1_ref[2:3, :],
    ]
    rest = [row - row.astype(BF16).astype(F32) for row in known]
    ride(out_ref, known + rest, rank)


def row2(
    rank, share, here_ref, c2_ref, c0_ref, c1_ref, hi_ref, lo_ref, back_ref,
    damp_ref, m1_ref, m2_ref, out_ref, table_ref
):
    real, imag = unpack(c2_ref, rank)
    next2 = apply_gram(hi_ref, lo_ref, real, imag)
    damping = damp_ref[0:1, :]
    came = ridden(c2_ref, rank)
    table_ref[0:5, :] = came[0:5] + came[5:10]
    table_ref[5:6, :] = m1_ref[2:3, :]
    table_ref[6:8, :] = m2_ref[3:5, :]
    table_ref[8:9, :] = damping
    rows = [
        inner(fields(c0_ref, rank), next2) + damping * m2_ref[0:1, :],
        inner(fields(c1_ref, rank), next2) + damping * m2_ref[1:2, :],
        inner(side(real, imag).astype(F32), next2) + damping * m2_ref[2:3, :],
        inner(back_ref[...], side(real, imag).astype(F32)),
        table_ref[pl.ds(here_ref[0] * share, share), :],
    ]
    more = out_ref.shape[1] - LATE - share
    if more:
        rows.append(jnp.zeros((more, real.shape[1]), F32))
    block = jnp.concatenate(rows, axis=0)
    for p in range(out_ref.shape[0]):
        out_ref[p] = block


def forms(h, u, g, p, position, size, axis):
    def times(v):
        return [sum(h[a][b] * v[b] for b in range(size)) for a in range(size)]

    def along(a, b):
        return jnp.sum(sum(x * y for x, y in zip(a, b)), axis=axis, keepdims=True)

    hg, hp, hx = times(g), times(p), times(position)
    rest = [u[a] - hx[a] for a in range(size)]
    return along(g, hg), along(p, hg), along(p, hp), along(g, rest), along(p, rest)


def descend(h, u, theta0, theta1, phi, damping, axis):
    one = jnp.ones_like(theta0)
    a11 = jnp.sum(h[0][0], axis=axis, keepdims=True)
    b1 = jnp.sum(u[0], axis=axis, keepdims=True)
    alpha = b1 / (1.1 * a11)
    p = [alpha * one]
    x = [alpha * one]
    for size in (2, 3):
        zero = jnp.zeros_like(one)
        x = x + [zero]
        p = p + [zero]
        if size == 2:
            g = [one - (theta0 + damping) * x[0], -x[0]]
        else:
            g = [
                one - (theta0 + damping) * x[0] - phi * x[1],
                -x[0] - (theta1 + damping) * x[1],
                -x[1],
            ]
        a11, a12, a22, b1, b2 = forms(h, u, g, p, x, size, axis)
        first, second = 1.1 * a11, 1.1 * a22
        determinant = first * second - a12 * a12
        alpha = (b1 * second - a12 * b2) / determinant
        beta = (first * b2 - a12 * b1) / determinant
        p = [alpha * g[a] + beta * p[a] for a in range(size)]
        x = [x[a] + p[a] for a in range(size)]
    return x


def finish_kernel(
    rank, nfreq, share, mine_ref, data_hbm, left_hbm, recv_ref, right_ref,
    b0_ref, b1_ref, b2_ref, c0_ref, c1_ref, c2_ref, wave_hbm, res_hbm,
    table_ref, mix_ref, wave_ref, res_ref, data_ref, left_ref, sem
):
    left_copy = pltpu.make_async_copy(left_hbm, left_ref, sem.at[2])
    data_copy = pltpu.make_async_copy(data_hbm, data_ref, sem.at[3])
    left_copy.start()
    data_copy.start()
    ntile = recv_ref.shape[0] // nfreq
    for f in range(nfreq):
        total = recv_ref[f * ntile]
        for t in range(1, ntile):
            total = total + recv_ref[f * ntile + t]
        table_ref[0:LATE, f, :] = total[0:LATE]
        for q in range(EARLY):
            place = LATE + q % share
            table_ref[LATE + q, f : f + 1, :] = recv_ref[f * ntile + q // share, place : place + 1]
    h = [[None] * 3 for _ in range(3)]
    places = [(0, 0, 2), (1, 1, 2), (2, 2, 2), (4, 0, 0), (5, 0, 1), (6, 1, 1)]
    for place, a, b in places:
        h[a][b] = h[b][a] = table_ref[place]
    u = [table_ref[7], table_ref[8], table_ref[3]]
    theta0, theta1, phi, damping = [table_ref[9 + a] for a in range(4)]
    x = descend(h, u, theta0, theta1, phi, damping, 0)
    mix_ref[0] = x[0] - theta0 * x[1] + (theta0 * theta1 - phi) * x[2]
    mix_ref[1] = x[1] - theta1 * x[2]
    mix_ref[2] = x[2]
    mix_ref[3] = x[0]
    mix_ref[4] = x[1]
    mix_ref[5] = x[2]
    row = pl.ds(mine_ref[0], 1)

    def combine(refs, offset):
        total = None
        for k, ref in enumerate(refs):
            scale = mix_ref[offset + k, row, :]
            real, imag = unpack(ref, rank)
            term = (scale * real.astype(F32), scale * imag.astype(F32))
            total = term if total is None else (total[0] + term[0], total[1] + term[1])
        return total

    def plain(factor_ref, real, imag):
        (rh, rl), (ih, il) = split(real), split(imag)
        first, second = factor_ref[0], factor_ref[1]
        return (
            dot(first, side(rh, ih)) + dot(second, side(-ih, rh))
            + dot(first, side(rl, il)) + dot(second, side(-il, rl))
        )

    s = wave_ref.shape[2]
    wave = plain(right_ref, *combine([b0_ref, b1_ref, b2_ref], 0))
    wave_ref[0] = wave[:, :s]
    wave_ref[1] = wave[:, s:]
    wave_copy = pltpu.make_async_copy(wave_ref, wave_hbm, sem.at[0])
    wave_copy.start()
    mixed = combine([c0_ref, c1_ref, c2_ref], 3)
    left_copy.wait()
    data_copy.wait()
    image = plain(left_ref, *mixed)
    res_ref[0] = data_ref[0].astype(F32) - image[:, :s]
    res_ref[1] = data_ref[1].astype(F32) - image[:, s:]
    res_copy = pltpu.make_async_copy(res_ref, res_hbm, sem.at[1])
    res_copy.start()
    wave_copy.wait()
    res_copy.wait()


def lane_limits(limits, rank, width):
    lane = lax.broadcasted_iota(jnp.int32, (1, width), 1)
    limit = jnp.zeros((1, width), jnp.int32)
    for p, value in enumerate(limits):
        limit = jnp.where(lane >= p * rank, value, limit)
    return (lax.rem(lane, rank) < limit).astype(F32)


def packed_gram(real, imag):
    width = real.shape[1]
    both = jnp.concatenate([real, imag], axis=0)
    upper = dot_t(both, both)
    lower = dot_t(real, imag) - dot_t(imag, real)
    row = lax.broadcasted_iota(jnp.int32, (width, width), 0)
    column = lax.broadcasted_iota(jnp.int32, (width, width), 1)
    return jnp.where(row <= column, upper, lower).astype(BF16)


def unpacked_gram(packed):
    width = packed.shape[1]
    here = packed.astype(F32)
    there = here.T
    row = lax.broadcasted_iota(jnp.int32, (width, width), 0)
    column = lax.broadcasted_iota(jnp.int32, (width, width), 1)
    real = jnp.where(row <= column, here, there)
    imag = jnp.where(row > column, here, jnp.where(row < column, -there, 0.0))
    return real.astype(BF16), imag.astype(BF16)


def direct_offsets(half):
    others = [k for k in range(1, half) if k != 2]
    return sorted(others, key=lambda k: (min(k, half - k), k))


def start_left(rank, n, here_ref, mine_ref, ranks_hbm, data_hbm, left_hbm, right_hbm, *refs):
    keep_ref, right_ref, ranks_ref, data_ref, left_ref, back_ref, sem = refs[-7:]
    half = n // 2
    direct = [0] + direct_offsets(half)
    packets, own = refs[: half - 1], refs[half - 1]
    pairs = [
        (left_hbm, left_ref), (data_hbm, data_ref), (ranks_hbm, ranks_ref),
        (right_hbm, right_ref),
    ]
    copies = [
        pltpu.make_async_copy(source, target, sem.at[k])
        for k, (source, target) in enumerate(pairs)
    ]
    for copy in copies:
        copy.start()
    for copy in copies[:3]:
        copy.wait()
    width = left_ref.shape[2]
    s = data_ref.shape[2]
    q = s // n
    here = here_ref[0]
    keep = lane_limits([ranks_ref[here, p] for p in range(n)], rank, width).astype(BF16)
    real, imag = left_ref[0] * keep, left_ref[1] * keep
    both = side(data_ref[0], data_ref[1])
    first, second = dot_t(both, real), dot_t(both, imag)
    back_ref[0] = (first[:s] + second[s:]).astype(BF16)
    back_ref[1] = (first[s:] - second[:s]).astype(BF16)
    gram = packed_gram(real, imag)
    for k, packet in zip(direct, packets):
        place = 4 * q if k == 1 else 0
        packet[place : place + width, :] = gram
    z, x = lax.div(here, 2), lax.rem(here, 2)
    for k in range(half):
        base = 2 * lax.rem(z + k, half)
        for block, target in enumerate([base + 1 - x, base + x]):
            rows = pl.ds(pl.multiple_of(target * q, q), q)
            if k == 2:
                out, place = packets[direct.index(1)], 2 * q * block
            elif k == 0 and block == 1:
                out, place = own, 0
            else:
                out, place = packets[direct.index(k)], width + 2 * q * block
                place += 4 * q if k == 1 else 0
            out[place : place + q, :] = back_ref[0, rows, :]
            out[place + q : place + 2 * q, :] = back_ref[1, rows, :]
    keep = lane_limits([ranks_ref[p, here] for p in range(n)], rank, width)
    keep_ref[...] = jnp.broadcast_to(keep, keep_ref.shape)
    copies[3].wait()


def start_right(right_ref, keep_ref, out_ref):
    keep = keep_ref[0:1, :].astype(BF16)
    out_ref[...] = packed_gram(right_ref[0] * keep, right_ref[1] * keep)


def swap_tiles(rank, source, target):
    n, rows, width = source.shape
    per = 128 // rank
    lane = lax.div(lax.broadcasted_iota(jnp.int32, (rows, 128), 1), rank)
    for g in range(n // per):
        for h in range(width // 128):
            ins = [source[per * g + a, :, 128 * h : 128 * h + 128] for a in range(per)]
            for b in range(per):
                out = None
                for a in range(per):
                    shift = (a - b) * rank % 128
                    piece = pltpu.roll(ins[a], shift, 1) if shift else ins[a]
                    out = piece if out is None else jnp.where(lane == a, piece, out)
                target[per * h + b, :, 128 * g : 128 * g + 128] = out


def apply_tiles(gram_ref, source, target):
    n, rows, _ = source.shape
    q = rows // 2
    for j in range(n):
        high, low = split(source[j])
        vector = jnp.concatenate([high, low], axis=0)
        real, imag = dot(vector, gram_ref[0, j]), dot(vector, gram_ref[1, j])
        real = real[:rows] + real[rows:]
        imag = imag[:rows] + imag[rows:]
        target[j, 0:q, :] = real[:q] + imag[q:]
        target[j, q:rows, :] = real[q:] - imag[:q]


def inner_tiles(first, second):
    n, rows, _ = first.shape
    total = first[0] * second[0]
    for j in range(1, n):
        total = total + first[j] * second[j]
    total = jnp.sum(total, axis=1, keepdims=True)
    return total[: rows // 2] + total[rows // 2 :]


def take_off(target, terms):
    scales = [jnp.concatenate([scale, scale], axis=0) for scale, _ in terms]
    for j in range(target.shape[0]):
        value = target[j]
        for scale, (_, other) in zip(scales, terms):
            value = value - scale * other[j]
        target[j] = value


def chain_kernel(
    rank, n, here_ref, freq_ref, *refs
):
    half = n // 2
    order = [0] + direct_offsets(half) + [2]
    lefts = [refs[:half], refs[half:n]]
    rights = [refs[n : n + half], refs[n + half : 2 * n]]
    own = refs[2 * n]
    b_ref, c_ref, stats_ref, left_ref, right_ref, one_ref, two_ref = refs[2 * n + 1 :]
    width = refs[0].shape[1]
    q = stats_ref.shape[0]
    here = here_ref[0]
    z, x = lax.div(here, 2), lax.rem(here, 2)
    for k in range(half):
        base = 2 * lax.rem(z + half - k, half)
        for other in range(2):
            ref = lefts[other][order.index(k)]
            at = pl.ds(base + (1 - x if other else x), 1)
            top = 4 * q if k == 2 or (k == 1 and not other) else 0
            grams = (ref[top : top + width, :], rights[other][order.index(k)][...])
            for packed, gram_ref in zip(grams, (left_ref, right_ref)):
                real, imag = unpacked_gram(packed)
                gram_ref[0, at] = real[None]
                gram_ref[1, at] = imag[None]
            start = (0 if k == 2 else top + width) + (0 if other else 2 * q)
            if k == 0 and not other:
                block = own[...]
            else:
                block = ref[start : start + 2 * q, :]
            one_ref[at] = block.astype(F32)[None]
    b0, b1, b2 = b_ref.at[0], b_ref.at[1], b_ref.at[2]
    c0, c1, c2 = c_ref.at[0], c_ref.at[1], c_ref.at[2]
    swap_tiles(rank, one_ref, b0)
    apply_tiles(right_ref, b0, two_ref)
    m00 = inner_tiles(b0, two_ref)
    swap_tiles(rank, two_ref, c0)
    apply_tiles(left_ref, c0, one_ref)
    n00 = inner_tiles(c0, one_ref)
    theta0 = ratio(n00, m00)
    swap_tiles(rank, one_ref, b1)
    take_off(b1, [(theta0, b0)])
    apply_tiles(right_ref, b1, two_ref)
    m11 = inner_tiles(b1, two_ref)
    m01 = inner_tiles(b0, two_ref)
    swap_tiles(rank, two_ref, c1)
    apply_tiles(left_ref, c1, one_ref)
    n11 = inner_tiles(c1, one_ref)
    n01 = inner_tiles(c0, one_ref)
    theta1 = ratio(n11, m11)
    phi = ratio(n01, m00)
    swap_tiles(rank, one_ref, b2)
    take_off(b2, [(theta1, b1), (phi, b0)])
    apply_tiles(right_ref, b2, two_ref)
    m02 = inner_tiles(b0, two_ref)
    m12 = inner_tiles(b1, two_ref)
    m22 = inner_tiles(b2, two_ref)
    swap_tiles(rank, two_ref, c2)
    apply_tiles(left_ref, c2, one_ref)
    n02 = inner_tiles(c0, one_ref)
    n12 = inner_tiles(c1, one_ref)
    n22 = inner_tiles(c2, one_ref)
    damping = 0.1 + 0.9 * freq_ref[0].astype(F32) / 229.0
    values = [
        n00 + damping * m00, n01 + damping * m01, n02 + damping * m02,
        n11 + damping * m11, n12 + damping * m12, n22 + damping * m22,
        m00, m01, m02, theta0, theta1, phi,
    ]
    lane = lax.broadcasted_iota(jnp.int32, stats_ref.shape, 1)
    block = jnp.full(stats_ref.shape, damping)
    for place, value in enumerate(values):
        block = jnp.where(lane == place, value, block)
    stats_ref[...] = block


def mix_kernel(stats_refs, b_ref, c_ref, out_ref):
    blocks = [ref[...] for ref in stats_refs]
    lane = lax.broadcasted_iota(jnp.int32, blocks[0].shape, 1)
    where_f = [lane == f for f in range(len(blocks))]

    def pick(place):
        value = jnp.zeros_like(blocks[0])
        for f, block in enumerate(blocks):
            shift = (f - place) % 128
            value = jnp.where(where_f[f], pltpu.roll(block, shift, 1) if shift else block, value)
        return value

    h = [[None] * 3 for _ in range(3)]
    for place, (a, b) in enumerate([(0, 0), (0, 1), (0, 2), (1, 1), (1, 2), (2, 2)]):
        h[a][b] = h[b][a] = pick(place)
    u = [pick(6), pick(7), pick(8)]
    theta0, theta1, phi, damping = pick(9), pick(10), pick(11), pick(12)
    x = descend(h, u, theta0, theta1, phi, damping, 1)
    n, rows, _ = b_ref.shape[1:]
    scales = []
    for value in x:
        own = jnp.sum(jnp.where(lane == 0, value, 0.0), axis=1, keepdims=True)
        scales.append(jnp.concatenate([own, own], axis=0))
    for j in range(n):
        for place, ref in enumerate((b_ref, c_ref)):
            value = scales[0] * ref[0, j] + scales[1] * ref[1, j] + scales[2] * ref[2, j]
            out_ref[j, place * rows : (place + 1) * rows, :] = value.astype(BF16)


def home_mix(nfreq, data_hbm, left_hbm, right_hbm, *refs):
    stats_refs = refs[:nfreq]
    b_ref, c_ref, out_ref, data_ref, left_ref, right_ref, sem = refs[nfreq:]
    pairs = [(right_hbm, right_ref), (left_hbm, left_ref), (data_hbm, data_ref)]
    copies = [
        pltpu.make_async_copy(source, target, sem.at[k])
        for k, (source, target) in enumerate(pairs)
    ]
    for copy in copies:
        copy.start()
    mix_kernel(stats_refs, b_ref, c_ref, out_ref)
    for copy in copies:
        copy.wait()


def dot_nt(a, b):
    return lax.dot_general(a, b, (((1,), (1,)), ((), ())), preferred_element_type=F32)


def home_kernel(
    recv_ref, data_ref, left_ref, right_ref, wave_hbm, res_hbm, wave_ref, res_ref, sem
):
    n, rows, width = recv_ref.shape
    q = rows // 4
    s = n * q

    def plain(factor_ref, place):
        real = recv_ref[:, place * q : (place + 1) * q, :].reshape(s, width)
        imag = recv_ref[:, (place + 1) * q : (place + 2) * q, :].reshape(s, width)
        both = jnp.concatenate([real, imag], axis=0)
        first, second = dot_nt(factor_ref[0], both), dot_nt(factor_ref[1], both)
        return first[:, :s] - second[:, s:], first[:, s:] + second[:, :s]

    wave_ref[0], wave_ref[1] = plain(right_ref, 0)
    wave_copy = pltpu.make_async_copy(wave_ref, wave_hbm, sem.at[0])
    wave_copy.start()
    real, imag = plain(left_ref, 2)
    res_ref[0] = data_ref[0].astype(F32) - real
    res_ref[1] = data_ref[1].astype(F32) - imag
    res_copy = pltpu.make_async_copy(res_ref, res_hbm, sem.at[1])
    res_copy.start()
    wave_copy.wait()
    res_copy.wait()


def by_source(data, left, right, ranks, freq_index, ntile, nfreq, here, mine):
    width = left.shape[2]
    rank = width // ntile
    s = data.shape[2]
    q = s // ntile
    half = ntile // 2
    room = (16 << 20) + 64 * width * width

    def like(value):
        return jax.ShapeDtypeStruct(value.shape, value.dtype)

    def call(kernel, specs, args, outs, scratch=(), target=VMEM):
        return pl.pallas_call(
            kernel,
            out_shape=outs,
            in_specs=specs,
            out_specs=[target] * len(outs),
            scratch_shapes=scratch,
            compiler_params=pltpu.CompilerParams(vmem_limit_bytes=room),
        )(*args)

    def along(shift):
        return [
            (2 * z + x, 2 * ((z + shift) % half) + x) for z in range(half) for x in range(2)
        ]

    across = [(t, t ^ 1) for t in range(ntile)]
    direct = direct_offsets(half)
    sizes = [width + (8 if k == 1 else 4) * q for k in direct]
    sizes = [width + 2 * q] + sizes + [2 * q]
    parts = call(
        functools.partial(start_left, rank, ntile), [SMEM] * 2 + [HBM] * 4,
        (here, mine, ranks, data, left, right),
        [jax.ShapeDtypeStruct((size, width), BF16) for size in sizes]
        + [jax.ShapeDtypeStruct((8, width), F32), like(right)],
        [
            pltpu.SMEM(ranks.shape, jnp.int32),
            pltpu.VMEM(data.shape, BF16),
            pltpu.VMEM(left.shape, BF16),
            pltpu.VMEM((2, s, width), BF16),
            pltpu.SemaphoreType.DMA((4,)),
        ],
    )
    (gram,) = call(
        start_right, [VMEM] * 2, (parts[-1], parts[-2]),
        [jax.ShapeDtypeStruct((width, width), BF16)],
    )

    def hop(value, pairs):
        return lax.ppermute(value, "tcol", pairs)

    lefts, rights = [parts[0]], [gram]
    cross = [hop(parts[0], across), hop(gram, across)]
    for place, k in enumerate(direct):
        first, second = parts[1 + place], gram
        if place:
            first, _ = lax.optimization_barrier((first, lefts[-1]))
            second, _ = lax.optimization_barrier((second, rights[-1]))
        lefts.append(hop(first, along(k)))
        rights.append(hop(second, along(k)))
    first, _ = lax.optimization_barrier((lefts[1], lefts[-1]))
    first = first[: width + 4 * q]
    second, _ = lax.optimization_barrier((rights[1], rights[-1]))
    lefts.append(hop(first, along(1)))
    rights.append(hop(second, along(1)))
    other_lefts, other_rights = cross[:1], cross[1:]
    for place in range(1, half):
        value = lefts[1][4 * q :] if place == 1 else lefts[place]
        other_lefts.append(hop(value, across))
        other_rights.append(hop(rights[place], across))
    packets = (*lefts, *other_lefts, *rights, *other_rights, parts[half - 1])
    vectors = jax.ShapeDtypeStruct((3, ntile, 2 * q, width), F32)
    grams = pltpu.VMEM((2, ntile, width, width), BF16)
    vector = pltpu.VMEM((ntile, 2 * q, width), F32)
    b, c, stats = call(
        functools.partial(chain_kernel, rank, ntile), [SMEM] * 2 + [VMEM] * len(packets),
        (here, freq_index, *packets),
        (vectors, vectors, jax.ShapeDtypeStruct((q, 128), F32)),
        [grams, grams, vector, vector],
    )
    gathered = [stats] + [
        lax.ppermute(stats, "freq", [(f, f ^ step) for f in range(nfreq)])
        for step in range(1, nfreq)
    ]
    out, data_in, left_in, right_in = call(
        functools.partial(home_mix, nfreq), [HBM] * 3 + [VMEM] * (nfreq + 2),
        (data, left, right, *gathered, b, c),
        (
            jax.ShapeDtypeStruct((ntile, 4 * q, width), BF16),
            like(data), like(left), like(right),
        ),
        [pltpu.SemaphoreType.DMA((3,))],
    )
    back = lax.all_to_all(out, "tcol", 0, 0, tiled=True)
    shape = jax.ShapeDtypeStruct(data.shape, F32)
    return call(
        home_kernel, [VMEM] * 4, (back, data_in, left_in, right_in),
        (shape, shape),
        [
            pltpu.VMEM(shape.shape, F32),
            pltpu.VMEM(shape.shape, F32),
            pltpu.SemaphoreType.DMA((2,)),
        ],
        HBM,
    )


def body(data, left_factor, right_factor, ranks, freq_index):
    ntile = lax.axis_size("tcol")
    nfreq = lax.axis_size("freq")
    here = lax.axis_index("tcol").reshape(1)
    mine = lax.axis_index("freq").reshape(1)
    data, left, right, ranks = data[0], left_factor[0], right_factor[0], ranks[0]
    data, left, right, ranks = [
        pltpu.with_memory_space_constraint(value, pltpu.HBM)
        for value in (data, left, right, ranks)
    ]
    width = left.shape[2]
    rank = width // ntile
    s = data.shape[2]
    fits = ntile % 2 == 0 and ntile >= 6 and s % (16 * ntile) == 0 and width % 128 == 0 and 128 % rank == 0
    if fits and nfreq & (nfreq - 1) == 0 and ntile * width * width <= 1 << 20:
        wave, res = by_source(data, left, right, ranks, freq_index, ntile, nfreq, here, mine)
        return wave[None], res[None]
    share = -(-EARLY // ntile)
    height = -(-(LATE + share) // 8) * 8
    field = jax.ShapeDtypeStruct((width, 2 * s), F32)
    sums = jax.ShapeDtypeStruct((8, s), F32)
    bare = jax.ShapeDtypeStruct((ntile, 2 * rank, s), BF16)
    message = jax.ShapeDtypeStruct((ntile, 2 * rank + RIDE, s), BF16)
    gram = jax.ShapeDtypeStruct((width, 2 * width), BF16)
    room = (8 << 20) + 24 * width * width

    def like(value):
        return jax.ShapeDtypeStruct(value.shape, value.dtype)

    def call(kernel, specs, args, outs, scratch=(), target=VMEM):
        return pl.pallas_call(
            functools.partial(kernel, rank),
            out_shape=outs,
            in_specs=specs,
            out_specs=[target] * len(outs),
            scratch_shapes=scratch,
            compiler_params=pltpu.CompilerParams(vmem_limit_bytes=room),
        )(*args)

    def step(kernel, args, outs):
        return call(kernel, [VMEM] * len(args), args, outs)

    def exchange(value):
        return lax.all_to_all(value, "tcol", 0, 0, tiled=True)

    vright, back, damp, out, uhi, ulo, vhi, vlo = call(
        start_kernel, [SMEM] * 2 + [HBM] * 5, (here, mine, ranks, freq_index, data, left, right),
        (like(right), field, sums, bare, gram, gram, gram, gram),
        [
            pltpu.SMEM(ranks.shape, jnp.int32),
            pltpu.SMEM(freq_index.shape, jnp.int32),
            pltpu.VMEM(data.shape, BF16),
            pltpu.VMEM(left.shape, BF16),
            pltpu.SemaphoreType.DMA((5,)),
        ],
    )
    b0 = exchange(out)
    g0, m0, out = step(column0, (b0, vhi, vlo), (field, sums, message))
    c0 = exchange(out)
    n0, out = step(row0, (c0, uhi, ulo, back), (sums, message))
    b1 = exchange(out)
    g1, m1, out = step(column1, (b1, b0, vhi, vlo, g0, n0), (field, sums, message))
    c1 = exchange(out)
    n1, out = step(row1, (c1, c0, uhi, ulo, back), (sums, message))
    b2 = exchange(out)
    m2, out = step(
        column2, (b2, b0, b1, vhi, vlo, g0, g1, damp, m0, n0, m1, n1), (sums, message)
    )
    c2 = exchange(out)
    args = (here, c2, c0, c1, uhi, ulo, back, damp, m1, m2)
    (out,) = call(
        lambda rank, *refs: row2(rank, share, *refs), [SMEM] + [VMEM] * 9, args,
        (jax.ShapeDtypeStruct((nfreq * ntile, height, s), F32),),
        [pltpu.VMEM((max(16, ntile * share), s), F32)],
    )
    everyone = lax.all_to_all(out, ("freq", "tcol"), 0, 0, tiled=True)
    shape = jax.ShapeDtypeStruct(data.shape, F32)
    wave, res = call(
        lambda rank, *refs: finish_kernel(rank, nfreq, share, *refs),
        [SMEM, HBM, HBM] + [VMEM] * 8,
        (mine, data, left, everyone, vright, b0, b1, b2, c0, c1, c2), (shape, shape),
        [
            pltpu.VMEM((LATE + EARLY, nfreq, s), F32),
            pltpu.VMEM((6, nfreq, s), F32),
            pltpu.VMEM(shape.shape, F32),
            pltpu.VMEM(shape.shape, F32),
            pltpu.VMEM(data.shape, BF16),
            pltpu.VMEM(left.shape, BF16),
            pltpu.SemaphoreType.DMA((4,)),
        ],
        HBM,
    )
    return wave[None], res[None]


def solution(mesh):
    in_specs = (
        P("freq", None, "tcol", None),
        P("freq", None, "tcol", None),
        P("freq", None, "tcol", None),
        P("freq", None, None),
        P("freq"),
    )
    out_specs = (P("freq", None, "tcol", None), P("freq", None, "tcol", None))
    return jax.shard_map(body, mesh=mesh, in_specs=in_specs, out_specs=out_specs, check_vma=False)
```

```python
import functools

import jax
import jax.numpy as jnp
from jax import lax
from jax.experimental import pallas as pl
from jax.experimental.pallas import tpu as pltpu
from jax.sharding import PartitionSpec as P


RIDE = 16
LATE = 4
EARLY = 9
VMEM = pl.BlockSpec(memory_space=pltpu.VMEM)
SMEM = pl.BlockSpec(memory_space=pltpu.SMEM)
HBM = pl.BlockSpec(memory_space=pltpu.HBM)
F32 = jnp.float32
BF16 = jnp.bfloat16


def dot(a, b):
    return jnp.dot(a, b, preferred_element_type=F32)


def dot_t(a, b):
    return lax.dot_general(a, b, (((0,), (0,)), ((), ())), preferred_element_type=F32)


def side(real, imag):
    return jnp.concatenate([real, imag], axis=1)


def split(value):
    high = value.astype(BF16)
    return high, (value - high.astype(F32)).astype(BF16)


def unpack(ref, rank):
    n = ref.shape[0]
    real = ref[:, 0:rank, :].reshape(n * rank, ref.shape[2])
    imag = ref[:, rank : 2 * rank, :].reshape(n * rank, ref.shape[2])
    return real, imag


def fields(ref, rank):
    return side(*unpack(ref, rank)).astype(F32)


def send(out_ref, value, rank):
    s = out_ref.shape[2]
    for p in range(out_ref.shape[0]):
        rows = value[p * rank : (p + 1) * rank].astype(BF16)
        out_ref[p, 0:rank, :] = rows[:, :s]
        out_ref[p, rank : 2 * rank, :] = rows[:, s:]


def ride(out_ref, rows, rank):
    rows = rows + [jnp.zeros_like(rows[0])] * (RIDE - len(rows))
    block = jnp.concatenate(rows, axis=0).astype(BF16)
    for p in range(out_ref.shape[0]):
        out_ref[p, 2 * rank : 2 * rank + RIDE, :] = block


def ridden(ref, rank):
    total = ref[0, 2 * rank : 2 * rank + RIDE, :].astype(F32)
    for p in range(1, ref.shape[0]):
        total = total + ref[p, 2 * rank : 2 * rank + RIDE, :].astype(F32)
    return total


def inner(a, b):
    both = jnp.sum(a * b, axis=0, keepdims=True)
    s = both.shape[1] // 2
    return both[:, :s] + both[:, s:]


def twice(row):
    return jnp.concatenate([row, row], axis=1)


def ratio(top, bottom):
    safe = bottom > 0
    return jnp.where(safe, top / jnp.where(safe, bottom, 1.0), 0.0)


def apply_gram(hi_ref, lo_ref, real, imag):
    vector = jnp.concatenate([side(real, imag), side(-imag, real)], axis=0)
    return dot(hi_ref[...], vector) + dot(lo_ref[...], vector)


def make_gram(factor_ref, hi_ref, lo_ref, limits):
    real, imag = factor_ref[0], factor_ref[1]
    width = real.shape[1]
    rank = width // len(limits)
    level = lax.broadcasted_iota(jnp.int32, (rank, width), 0)

    def put(value, place):
        for p, limit in enumerate(limits):
            rows = slice(p * rank, (p + 1) * rank)
            high, low = split(jnp.where(level < limit, value[rows], 0.0))
            hi_ref[rows, place : place + width] = high
            lo_ref[rows, place : place + width] = low

    put(dot_t(real, real) + dot_t(imag, imag), 0)
    put(dot_t(real, imag) - dot_t(imag, real), width)


def start_kernel(
    rank, here_ref, mine_ref, ranks_hbm, freq_hbm, data_hbm, left_hbm, right_hbm,
    right_ref, back_ref, sums_ref, out_ref, uhi_ref, ulo_ref, vhi_ref, vlo_ref,
    ranks_ref, freq_ref, data_ref, left_ref, sem
):
    n = out_ref.shape[0]
    s = out_ref.shape[2]
    pairs = [
        (left_hbm, left_ref), (data_hbm, data_ref), (ranks_hbm, ranks_ref),
        (freq_hbm, freq_ref), (right_hbm, right_ref),
    ]
    copies = [
        pltpu.make_async_copy(source, target, sem.at[k])
        for k, (source, target) in enumerate(pairs)
    ]
    for copy in copies:
        copy.start()
    for copy in copies[:4]:
        copy.wait()
    here = here_ref[0]
    row_limits = [ranks_ref[here, p] for p in range(n)]
    column_limits = [ranks_ref[p, here] for p in range(n)]
    damping = 0.1 + 0.9 * freq_ref[0].astype(F32) / 229.0
    sums_ref[...] = jnp.full(sums_ref.shape, damping)
    real, imag = data_ref[0], data_ref[1]
    back = dot_t(left_ref[0], side(real, imag)) + dot_t(left_ref[1], side(imag, -real))
    level = lax.broadcasted_iota(jnp.int32, (rank, 2 * s), 0)
    back = jnp.concatenate(
        [
            jnp.where(level < limit, back[p * rank : (p + 1) * rank], 0.0)
            for p, limit in enumerate(row_limits)
        ],
        axis=0,
    )
    back_ref[...] = back
    send(out_ref, back, rank)
    make_gram(left_ref, uhi_ref, ulo_ref, row_limits)
    copies[4].wait()
    make_gram(right_ref, vhi_ref, vlo_ref, column_limits)


def column0(rank, b0_ref, hi_ref, lo_ref, g0_ref, sums_ref, out_ref):
    real, imag = unpack(b0_ref, rank)
    g0 = apply_gram(hi_ref, lo_ref, real, imag)
    g0_ref[...] = g0
    m00 = inner(side(real, imag).astype(F32), g0)
    sums_ref[0:1, :] = m00
    send(out_ref, g0, rank)
    ride(out_ref, [m00], rank)


def row0(rank, c0_ref, hi_ref, lo_ref, back_ref, sums_ref, out_ref):
    real, imag = unpack(c0_ref, rank)
    next0 = apply_gram(hi_ref, lo_ref, real, imag)
    c0 = side(real, imag).astype(F32)
    n00 = inner(c0, next0)
    sums_ref[0:1, :] = n00
    sums_ref[1:2, :] = inner(back_ref[...], c0)
    sums_ref[2:3, :] = ridden(c0_ref, rank)[0:1]
    send(out_ref, next0, rank)
    ride(out_ref, [n00], rank)


def column1(
    rank, b1_ref, b0_ref, hi_ref, lo_ref, g0_ref, n0_ref, g1_ref, sums_ref, out_ref
):
    real, imag = unpack(b1_ref, rank)
    theta0 = ratio(ridden(b1_ref, rank)[0:1], n0_ref[2:3, :])
    wide = twice(theta0)
    g1 = apply_gram(hi_ref, lo_ref, real, imag) - wide * g0_ref[...]
    b0 = fields(b0_ref, rank)
    b1 = side(real, imag).astype(F32) - wide * b0
    g1_ref[...] = g1
    m11 = inner(b1, g1)
    sums_ref[0:1, :] = m11
    sums_ref[1:2, :] = inner(b0, g1)
    sums_ref[2:3, :] = theta0
    send(out_ref, g1, rank)
    ride(out_ref, [m11], rank)


def row1(rank, c1_ref, c0_ref, hi_ref, lo_ref, back_ref, sums_ref, out_ref):
    real, imag = unpack(c1_ref, rank)
    next1 = apply_gram(hi_ref, lo_ref, real, imag)
    c1 = side(real, imag).astype(F32)
    n11 = inner(c1, next1)
    n01 = inner(fields(c0_ref, rank), next1)
    sums_ref[0:1, :] = n11
    sums_ref[1:2, :] = n01
    sums_ref[2:3, :] = inner(back_ref[...], c1)
    sums_ref[3:4, :] = ridden(c1_ref, rank)[0:1]
    send(out_ref, next1, rank)
    ride(out_ref, [n11, n01], rank)


def column2(
    rank, b2_ref, b0_ref, b1_ref, hi_ref, lo_ref, g0_ref, g1_ref,
    damp_ref, m0_ref, n0_ref, m1_ref, n1_ref, sums_ref, out_ref
):
    real, imag = unpack(b2_ref, rank)
    came = ridden(b2_ref, rank)
    theta1 = ratio(came[0:1], n1_ref[3:4, :])
    phi = ratio(came[1:2], n0_ref[2:3, :])
    wide1, wide0 = twice(theta1), twice(phi)
    g2 = apply_gram(hi_ref, lo_ref, real, imag) - wide1 * g1_ref[...] - wide0 * g0_ref[...]
    send(out_ref, g2, rank)
    b0 = fields(b0_ref, rank)
    b1 = fields(b1_ref, rank) - twice(m1_ref[2:3, :]) * b0
    b2 = side(real, imag).astype(F32) - wide1 * b1 - wide0 * b0
    sums_ref[0:1, :] = inner(b0, g2)
    sums_ref[1:2, :] = inner(b1, g2)
    sums_ref[2:3, :] = inner(b2, g2)
    sums_ref[3:4, :] = theta1
    sums_ref[4:5, :] = phi
    damping = damp_ref[0:1, :]
    known = [
        n0_ref[0:1, :] + damping * m0_ref[0:1, :],
        n1_ref[1:2, :] + damping * m1_ref[1:2, :],
        n1_ref[0:1, :] + damping * m1_ref[0:1, :],
        n0_ref[1:2, :],
        n1_ref[2:3, :],
    ]
    rest = [row - row.astype(BF16).astype(F32) for row in known]
    ride(out_ref, known + rest, rank)


def row2(
    rank, share, here_ref, c2_ref, c0_ref, c1_ref, hi_ref, lo_ref, back_ref,
    damp_ref, m1_ref, m2_ref, out_ref, table_ref
):
    real, imag = unpack(c2_ref, rank)
    next2 = apply_gram(hi_ref, lo_ref, real, imag)
    damping = damp_ref[0:1, :]
    came = ridden(c2_ref, rank)
    table_ref[0:5, :] = came[0:5] + came[5:10]
    table_ref[5:6, :] = m1_ref[2:3, :]
    table_ref[6:8, :] = m2_ref[3:5, :]
    table_ref[8:9, :] = damping
    rows = [
        inner(fields(c0_ref, rank), next2) + damping * m2_ref[0:1, :],
        inner(fields(c1_ref, rank), next2) + damping * m2_ref[1:2, :],
        inner(side(real, imag).astype(F32), next2) + damping * m2_ref[2:3, :],
        inner(back_ref[...], side(real, imag).astype(F32)),
        table_ref[pl.ds(here_ref[0] * share, share), :],
    ]
    more = out_ref.shape[1] - LATE - share
    if more:
        rows.append(jnp.zeros((more, real.shape[1]), F32))
    block = jnp.concatenate(rows, axis=0)
    for p in range(out_ref.shape[0]):
        out_ref[p] = block


def forms(h, u, g, p, position, size, axis):
    def times(v):
        return [sum(h[a][b] * v[b] for b in range(size)) for a in range(size)]

    def along(a, b):
        return jnp.sum(sum(x * y for x, y in zip(a, b)), axis=axis, keepdims=True)

    hg, hp, hx = times(g), times(p), times(position)
    rest = [u[a] - hx[a] for a in range(size)]
    return along(g, hg), along(p, hg), along(p, hp), along(g, rest), along(p, rest)


def descend(h, u, theta0, theta1, phi, damping, axis):
    one = jnp.ones_like(theta0)
    a11 = jnp.sum(h[0][0], axis=axis, keepdims=True)
    b1 = jnp.sum(u[0], axis=axis, keepdims=True)
    alpha = b1 / (1.1 * a11)
    p = [alpha * one]
    x = [alpha * one]
    for size in (2, 3):
        zero = jnp.zeros_like(one)
        x = x + [zero]
        p = p + [zero]
        if size == 2:
            g = [one - (theta0 + damping) * x[0], -x[0]]
        else:
            g = [
                one - (theta0 + damping) * x[0] - phi * x[1],
                -x[0] - (theta1 + damping) * x[1],
                -x[1],
            ]
        a11, a12, a22, b1, b2 = forms(h, u, g, p, x, size, axis)
        first, second = 1.1 * a11, 1.1 * a22
        determinant = first * second - a12 * a12
        alpha = (b1 * second - a12 * b2) / determinant
        beta = (first * b2 - a12 * b1) / determinant
        p = [alpha * g[a] + beta * p[a] for a in range(size)]
        x = [x[a] + p[a] for a in range(size)]
    return x


def finish_kernel(
    rank, nfreq, share, mine_ref, data_hbm, left_hbm, recv_ref, right_ref,
    b0_ref, b1_ref, b2_ref, c0_ref, c1_ref, c2_ref, wave_hbm, res_hbm,
    table_ref, mix_ref, wave_ref, res_ref, data_ref, left_ref, sem
):
    left_copy = pltpu.make_async_copy(left_hbm, left_ref, sem.at[2])
    data_copy = pltpu.make_async_copy(data_hbm, data_ref, sem.at[3])
    left_copy.start()
    data_copy.start()
    ntile = recv_ref.shape[0] // nfreq
    for f in range(nfreq):
        total = recv_ref[f * ntile]
        for t in range(1, ntile):
            total = total + recv_ref[f * ntile + t]
        table_ref[0:LATE, f, :] = total[0:LATE]
        for q in range(EARLY):
            place = LATE + q % share
            table_ref[LATE + q, f : f + 1, :] = recv_ref[f * ntile + q // share, place : place + 1]
    h = [[None] * 3 for _ in range(3)]
    places = [(0, 0, 2), (1, 1, 2), (2, 2, 2), (4, 0, 0), (5, 0, 1), (6, 1, 1)]
    for place, a, b in places:
        h[a][b] = h[b][a] = table_ref[place]
    u = [table_ref[7], table_ref[8], table_ref[3]]
    theta0, theta1, phi, damping = [table_ref[9 + a] for a in range(4)]
    x = descend(h, u, theta0, theta1, phi, damping, 0)
    mix_ref[0] = x[0] - theta0 * x[1] + (theta0 * theta1 - phi) * x[2]
    mix_ref[1] = x[1] - theta1 * x[2]
    mix_ref[2] = x[2]
    mix_ref[3] = x[0]
    mix_ref[4] = x[1]
    mix_ref[5] = x[2]
    row = pl.ds(mine_ref[0], 1)

    def combine(refs, offset):
        total = None
        for k, ref in enumerate(refs):
            scale = mix_ref[offset + k, row, :]
            real, imag = unpack(ref, rank)
            term = (scale * real.astype(F32), scale * imag.astype(F32))
            total = term if total is None else (total[0] + term[0], total[1] + term[1])
        return total

    def plain(factor_ref, real, imag):
        (rh, rl), (ih, il) = split(real), split(imag)
        first, second = factor_ref[0], factor_ref[1]
        return (
            dot(first, side(rh, ih)) + dot(second, side(-ih, rh))
            + dot(first, side(rl, il)) + dot(second, side(-il, rl))
        )

    s = wave_ref.shape[2]
    wave = plain(right_ref, *combine([b0_ref, b1_ref, b2_ref], 0))
    wave_ref[0] = wave[:, :s]
    wave_ref[1] = wave[:, s:]
    wave_copy = pltpu.make_async_copy(wave_ref, wave_hbm, sem.at[0])
    wave_copy.start()
    mixed = combine([c0_ref, c1_ref, c2_ref], 3)
    left_copy.wait()
    data_copy.wait()
    image = plain(left_ref, *mixed)
    res_ref[0] = data_ref[0].astype(F32) - image[:, :s]
    res_ref[1] = data_ref[1].astype(F32) - image[:, s:]
    res_copy = pltpu.make_async_copy(res_ref, res_hbm, sem.at[1])
    res_copy.start()
    wave_copy.wait()
    res_copy.wait()


def lane_limits(limits, rank, width):
    lane = lax.broadcasted_iota(jnp.int32, (1, width), 1)
    limit = jnp.zeros((1, width), jnp.int32)
    for p, value in enumerate(limits):
        limit = jnp.where(lane >= p * rank, value, limit)
    return (lax.rem(lane, rank) < limit).astype(F32)


def packed_gram(real, imag):
    width = real.shape[1]
    both = jnp.concatenate([real, imag], axis=0)
    upper = dot_t(both, both)
    lower = dot_t(real, imag) - dot_t(imag, real)
    row = lax.broadcasted_iota(jnp.int32, (width, width), 0)
    column = lax.broadcasted_iota(jnp.int32, (width, width), 1)
    return jnp.where(row <= column, upper, lower).astype(BF16)


def unpacked_gram(packed):
    width = packed.shape[1]
    here = packed.astype(F32)
    there = here.T
    row = lax.broadcasted_iota(jnp.int32, (width, width), 0)
    column = lax.broadcasted_iota(jnp.int32, (width, width), 1)
    real = jnp.where(row <= column, here, there)
    imag = jnp.where(row > column, here, jnp.where(row < column, -there, 0.0))
    return real.astype(BF16), imag.astype(BF16)


def direct_offsets(half):
    others = [k for k in range(1, half) if k != 2]
    return sorted(others, key=lambda k: (min(k, half - k), k))


def start_left(rank, n, here_ref, mine_ref, ranks_hbm, data_hbm, left_hbm, right_hbm, *refs):
    keep_ref, right_ref, ranks_ref, data_ref, left_ref, back_ref, sem = refs[-7:]
    half = n // 2
    direct = [0] + direct_offsets(half)
    packets, small, own = refs[: half - 1], refs[half - 1 : half + 1], refs[half + 1]
    pairs = [
        (left_hbm, left_ref), (data_hbm, data_ref), (ranks_hbm, ranks_ref),
        (right_hbm, right_ref),
    ]
    copies = [
        pltpu.make_async_copy(source, target, sem.at[k])
        for k, (source, target) in enumerate(pairs)
    ]
    for copy in copies:
        copy.start()
    for copy in copies[:3]:
        copy.wait()
    width = left_ref.shape[2]
    s = data_ref.shape[2]
    q = s // n
    here = here_ref[0]
    keep = lane_limits([ranks_ref[here, p] for p in range(n)], rank, width).astype(BF16)
    real, imag = left_ref[0] * keep, left_ref[1] * keep
    both = side(data_ref[0], data_ref[1])
    first, second = dot_t(both, real), dot_t(both, imag)
    back_ref[0] = (first[:s] + second[s:]).astype(BF16)
    back_ref[1] = (first[s:] - second[:s]).astype(BF16)
    gram = packed_gram(real, imag)
    for packet in packets:
        packet[0:width, :] = gram
    z, x = lax.div(here, 2), lax.rem(here, 2)
    for k in range(half):
        base = 2 * lax.rem(z + k, half)
        for block, target in enumerate([base + 1 - x, base + x]):
            rows = pl.ds(pl.multiple_of(target * q, q), q)
            if k == 2:
                out, place = small[block], 0
            elif k == 0 and block == 1:
                out, place = own, 0
            else:
                out, place = packets[direct.index(k)], width + 2 * q * block
            out[place : place + q, :] = back_ref[0, rows, :]
            out[place + q : place + 2 * q, :] = back_ref[1, rows, :]
    keep = lane_limits([ranks_ref[p, here] for p in range(n)], rank, width)
    keep_ref[...] = jnp.broadcast_to(keep, keep_ref.shape)
    copies[3].wait()


def start_right(right_ref, keep_ref, out_ref):
    keep = keep_ref[0:1, :].astype(BF16)
    out_ref[...] = packed_gram(right_ref[0] * keep, right_ref[1] * keep)


def swap_tiles(rank, source, target):
    n, rows, width = source.shape
    per = 128 // rank
    lane = lax.div(lax.broadcasted_iota(jnp.int32, (rows, 128), 1), rank)
    for g in range(n // per):
        for h in range(width // 128):
            ins = [source[per * g + a, :, 128 * h : 128 * h + 128] for a in range(per)]
            for b in range(per):
                out = None
                for a in range(per):
                    shift = (a - b) * rank % 128
                    piece = pltpu.roll(ins[a], shift, 1) if shift else ins[a]
                    out = piece if out is None else jnp.where(lane == a, piece, out)
                target[per * h + b, :, 128 * g : 128 * g + 128] = out


def apply_tiles(gram_ref, source, target):
    n, rows, _ = source.shape
    q = rows // 2
    for j in range(n):
        high, low = split(source[j])
        vector = jnp.concatenate([high, low], axis=0)
        real, imag = dot(vector, gram_ref[0, j]), dot(vector, gram_ref[1, j])
        real = real[:rows] + real[rows:]
        imag = imag[:rows] + imag[rows:]
        target[j, 0:q, :] = real[:q] + imag[q:]
        target[j, q:rows, :] = real[q:] - imag[:q]


def inner_tiles(first, second):
    n, rows, _ = first.shape
    total = first[0] * second[0]
    for j in range(1, n):
        total = total + first[j] * second[j]
    total = jnp.sum(total, axis=1, keepdims=True)
    return total[: rows // 2] + total[rows // 2 :]


def take_off(target, terms):
    scales = [jnp.concatenate([scale, scale], axis=0) for scale, _ in terms]
    for j in range(target.shape[0]):
        value = target[j]
        for scale, (_, other) in zip(scales, terms):
            value = value - scale * other[j]
        target[j] = value


def chain_kernel(
    rank, n, here_ref, freq_ref, *refs
):
    half = n // 2
    order = [0] + direct_offsets(half) + [2]
    lefts = [refs[:half], refs[half:n]]
    rights = [refs[n : n + half], refs[n + half : 2 * n]]
    small, own = refs[2 * n : 2 * n + 2], refs[2 * n + 2]
    b_ref, c_ref, stats_ref, left_ref, right_ref, one_ref, two_ref = refs[2 * n + 3 :]
    width = refs[0].shape[1]
    q = stats_ref.shape[0]
    here = here_ref[0]
    z, x = lax.div(here, 2), lax.rem(here, 2)
    for k in range(half):
        base = 2 * lax.rem(z + half - k, half)
        for other in range(2):
            ref = lefts[other][order.index(k)]
            at = pl.ds(base + (1 - x if other else x), 1)
            grams = (ref[0:width, :], rights[other][order.index(k)][...])
            for packed, gram_ref in zip(grams, (left_ref, right_ref)):
                real, imag = unpacked_gram(packed)
                gram_ref[0, at] = real[None]
                gram_ref[1, at] = imag[None]
            start = width + (0 if other else 2 * q)
            if k == 2:
                block = small[1 - other][...]
            elif k == 0 and not other:
                block = own[...]
            else:
                block = ref[start : start + 2 * q, :]
            one_ref[at] = block.astype(F32)[None]
    b0, b1, b2 = b_ref.at[0], b_ref.at[1], b_ref.at[2]
    c0, c1, c2 = c_ref.at[0], c_ref.at[1], c_ref.at[2]
    swap_tiles(rank, one_ref, b0)
    apply_tiles(right_ref, b0, two_ref)
    m00 = inner_tiles(b0, two_ref)
    swap_tiles(rank, two_ref, c0)
    apply_tiles(left_ref, c0, one_ref)
    n00 = inner_tiles(c0, one_ref)
    theta0 = ratio(n00, m00)
    swap_tiles(rank, one_ref, b1)
    take_off(b1, [(theta0, b0)])
    apply_tiles(right_ref, b1, two_ref)
    m11 = inner_tiles(b1, two_ref)
    m01 = inner_tiles(b0, two_ref)
    swap_tiles(rank, two_ref, c1)
    apply_tiles(left_ref, c1, one_ref)
    n11 = inner_tiles(c1, one_ref)
    n01 = inner_tiles(c0, one_ref)
    theta1 = ratio(n11, m11)
    phi = ratio(n01, m00)
    swap_tiles(rank, one_ref, b2)
    take_off(b2, [(theta1, b1), (phi, b0)])
    apply_tiles(right_ref, b2, two_ref)
    m02 = inner_tiles(b0, two_ref)
    m12 = inner_tiles(b1, two_ref)
    m22 = inner_tiles(b2, two_ref)
    swap_tiles(rank, two_ref, c2)
    apply_tiles(left_ref, c2, one_ref)
    n02 = inner_tiles(c0, one_ref)
    n12 = inner_tiles(c1, one_ref)
    n22 = inner_tiles(c2, one_ref)
    damping = 0.1 + 0.9 * freq_ref[0].astype(F32) / 229.0
    values = [
        n00 + damping * m00, n01 + damping * m01, n02 + damping * m02,
        n11 + damping * m11, n12 + damping * m12, n22 + damping * m22,
        m00, m01, m02, theta0, theta1, phi,
    ]
    lane = lax.broadcasted_iota(jnp.int32, stats_ref.shape, 1)
    block = jnp.full(stats_ref.shape, damping)
    for place, value in enumerate(values):
        block = jnp.where(lane == place, value, block)
    stats_ref[...] = block


def mix_kernel(stats_refs, b_ref, c_ref, out_ref):
    blocks = [ref[...] for ref in stats_refs]
    lane = lax.broadcasted_iota(jnp.int32, blocks[0].shape, 1)
    where_f = [lane == f for f in range(len(blocks))]

    def pick(place):
        value = jnp.zeros_like(blocks[0])
        for f, block in enumerate(blocks):
            shift = (f - place) % 128
            value = jnp.where(where_f[f], pltpu.roll(block, shift, 1) if shift else block, value)
        return value

    h = [[None] * 3 for _ in range(3)]
    for place, (a, b) in enumerate([(0, 0), (0, 1), (0, 2), (1, 1), (1, 2), (2, 2)]):
        h[a][b] = h[b][a] = pick(place)
    u = [pick(6), pick(7), pick(8)]
    theta0, theta1, phi, damping = pick(9), pick(10), pick(11), pick(12)
    x = descend(h, u, theta0, theta1, phi, damping, 1)
    n, rows, _ = b_ref.shape[1:]
    scales = []
    for value in x:
        own = jnp.sum(jnp.where(lane == 0, value, 0.0), axis=1, keepdims=True)
        scales.append(jnp.concatenate([own, own], axis=0))
    for j in range(n):
        for place, ref in enumerate((b_ref, c_ref)):
            value = scales[0] * ref[0, j] + scales[1] * ref[1, j] + scales[2] * ref[2, j]
            out_ref[j, place * rows : (place + 1) * rows, :] = value.astype(BF16)


def home_mix(nfreq, data_hbm, left_hbm, right_hbm, *refs):
    stats_refs = refs[:nfreq]
    b_ref, c_ref, out_ref, data_ref, left_ref, right_ref, sem = refs[nfreq:]
    pairs = [(right_hbm, right_ref), (left_hbm, left_ref), (data_hbm, data_ref)]
    copies = [
        pltpu.make_async_copy(source, target, sem.at[k])
        for k, (source, target) in enumerate(pairs)
    ]
    for copy in copies:
        copy.start()
    mix_kernel(stats_refs, b_ref, c_ref, out_ref)
    for copy in copies:
        copy.wait()


def dot_nt(a, b):
    return lax.dot_general(a, b, (((1,), (1,)), ((), ())), preferred_element_type=F32)


def home_kernel(
    recv_ref, data_ref, left_ref, right_ref, wave_hbm, res_hbm, wave_ref, res_ref, sem
):
    n, rows, width = recv_ref.shape
    q = rows // 4
    s = n * q

    def plain(factor_ref, place):
        real = recv_ref[:, place * q : (place + 1) * q, :].reshape(s, width)
        imag = recv_ref[:, (place + 1) * q : (place + 2) * q, :].reshape(s, width)
        both = jnp.concatenate([real, imag], axis=0)
        first, second = dot_nt(factor_ref[0], both), dot_nt(factor_ref[1], both)
        return first[:, :s] - second[:, s:], first[:, s:] + second[:, :s]

    wave_ref[0], wave_ref[1] = plain(right_ref, 0)
    wave_copy = pltpu.make_async_copy(wave_ref, wave_hbm, sem.at[0])
    wave_copy.start()
    real, imag = plain(left_ref, 2)
    res_ref[0] = data_ref[0].astype(F32) - real
    res_ref[1] = data_ref[1].astype(F32) - imag
    res_copy = pltpu.make_async_copy(res_ref, res_hbm, sem.at[1])
    res_copy.start()
    wave_copy.wait()
    res_copy.wait()


def by_source(data, left, right, ranks, freq_index, ntile, nfreq, here, mine):
    width = left.shape[2]
    rank = width // ntile
    s = data.shape[2]
    q = s // ntile
    half = ntile // 2
    room = (16 << 20) + 64 * width * width

    def like(value):
        return jax.ShapeDtypeStruct(value.shape, value.dtype)

    def call(kernel, specs, args, outs, scratch=(), target=VMEM):
        return pl.pallas_call(
            kernel,
            out_shape=outs,
            in_specs=specs,
            out_specs=[target] * len(outs),
            scratch_shapes=scratch,
            compiler_params=pltpu.CompilerParams(vmem_limit_bytes=room),
        )(*args)

    def along(shift, flip=0):
        return [
            (2 * z + x, 2 * ((z + shift) % half) + (x ^ flip))
            for z in range(half) for x in range(2)
        ]

    across = [(t, t ^ 1) for t in range(ntile)]
    sizes = [width + 2 * q] + [width + 4 * q] * (half - 2) + [2 * q] * 3
    direct = direct_offsets(half)
    parts = call(
        functools.partial(start_left, rank, ntile), [SMEM] * 2 + [HBM] * 4,
        (here, mine, ranks, data, left, right),
        [jax.ShapeDtypeStruct((size, width), BF16) for size in sizes]
        + [jax.ShapeDtypeStruct((8, width), F32), like(right)],
        [
            pltpu.SMEM(ranks.shape, jnp.int32),
            pltpu.VMEM(data.shape, BF16),
            pltpu.VMEM(left.shape, BF16),
            pltpu.VMEM((2, s, width), BF16),
            pltpu.SemaphoreType.DMA((4,)),
        ],
    )
    (gram,) = call(
        start_right, [VMEM] * 2, (parts[-1], parts[-2]),
        [jax.ShapeDtypeStruct((width, width), BF16)],
    )

    def hop(value, pairs):
        return lax.ppermute(value, "tcol", pairs)

    lefts, rights = [parts[0]], [gram]
    cross = [hop(parts[0], across), hop(gram, across)]
    for place, k in enumerate(direct):
        first, second = parts[1 + place], gram
        if place:
            first, _ = lax.optimization_barrier((first, lefts[-1]))
            second, _ = lax.optimization_barrier((second, rights[-1]))
        lefts.append(hop(first, along(k)))
        rights.append(hop(second, along(k)))
    small = [hop(parts[half - block], along(2, block)) for block in (1, 0)]
    first, _ = lax.optimization_barrier((lefts[1][:width], lefts[-1]))
    second, _ = lax.optimization_barrier((rights[1], rights[-1]))
    lefts.append(hop(first, along(1)))
    rights.append(hop(second, along(1)))
    other_lefts, other_rights = cross[:1], cross[1:]
    for place in range(1, half):
        other_lefts.append(hop(lefts[place], across))
        other_rights.append(hop(rights[place], across))
    packets = (*lefts, *other_lefts, *rights, *other_rights, *small, parts[half + 1])
    vectors = jax.ShapeDtypeStruct((3, ntile, 2 * q, width), F32)
    grams = pltpu.VMEM((2, ntile, width, width), BF16)
    vector = pltpu.VMEM((ntile, 2 * q, width), F32)
    b, c, stats = call(
        functools.partial(chain_kernel, rank, ntile), [SMEM] * 2 + [VMEM] * len(packets),
        (here, freq_index, *packets),
        (vectors, vectors, jax.ShapeDtypeStruct((q, 128), F32)),
        [grams, grams, vector, vector],
    )
    gathered = [stats] + [
        lax.ppermute(stats, "freq", [(f, f ^ step) for f in range(nfreq)])
        for step in range(1, nfreq)
    ]
    out, data_in, left_in, right_in = call(
        functools.partial(home_mix, nfreq), [HBM] * 3 + [VMEM] * (nfreq + 2),
        (data, left, right, *gathered, b, c),
        (
            jax.ShapeDtypeStruct((ntile, 4 * q, width), BF16),
            like(data), like(left), like(right),
        ),
        [pltpu.SemaphoreType.DMA((3,))],
    )
    back = lax.all_to_all(out, "tcol", 0, 0, tiled=True)
    shape = jax.ShapeDtypeStruct(data.shape, F32)
    return call(
        home_kernel, [VMEM] * 4, (back, data_in, left_in, right_in),
        (shape, shape),
        [
            pltpu.VMEM(shape.shape, F32),
            pltpu.VMEM(shape.shape, F32),
            pltpu.SemaphoreType.DMA((2,)),
        ],
        HBM,
    )


def body(data, left_factor, right_factor, ranks, freq_index):
    ntile = lax.axis_size("tcol")
    nfreq = lax.axis_size("freq")
    here = lax.axis_index("tcol").reshape(1)
    mine = lax.axis_index("freq").reshape(1)
    data, left, right, ranks = data[0], left_factor[0], right_factor[0], ranks[0]
    data, left, right, ranks = [
        pltpu.with_memory_space_constraint(value, pltpu.HBM)
        for value in (data, left, right, ranks)
    ]
    width = left.shape[2]
    rank = width // ntile
    s = data.shape[2]
    fits = ntile % 2 == 0 and ntile >= 6 and s % (16 * ntile) == 0 and width % 128 == 0 and 128 % rank == 0
    if fits and nfreq & (nfreq - 1) == 0 and ntile * width * width <= 1 << 20:
        wave, res = by_source(data, left, right, ranks, freq_index, ntile, nfreq, here, mine)
        return wave[None], res[None]
    share = -(-EARLY // ntile)
    height = -(-(LATE + share) // 8) * 8
    field = jax.ShapeDtypeStruct((width, 2 * s), F32)
    sums = jax.ShapeDtypeStruct((8, s), F32)
    bare = jax.ShapeDtypeStruct((ntile, 2 * rank, s), BF16)
    message = jax.ShapeDtypeStruct((ntile, 2 * rank + RIDE, s), BF16)
    gram = jax.ShapeDtypeStruct((width, 2 * width), BF16)
    room = (8 << 20) + 24 * width * width

    def like(value):
        return jax.ShapeDtypeStruct(value.shape, value.dtype)

    def call(kernel, specs, args, outs, scratch=(), target=VMEM):
        return pl.pallas_call(
            functools.partial(kernel, rank),
            out_shape=outs,
            in_specs=specs,
            out_specs=[target] * len(outs),
            scratch_shapes=scratch,
            compiler_params=pltpu.CompilerParams(vmem_limit_bytes=room),
        )(*args)

    def step(kernel, args, outs):
        return call(kernel, [VMEM] * len(args), args, outs)

    def exchange(value):
        return lax.all_to_all(value, "tcol", 0, 0, tiled=True)

    vright, back, damp, out, uhi, ulo, vhi, vlo = call(
        start_kernel, [SMEM] * 2 + [HBM] * 5, (here, mine, ranks, freq_index, data, left, right),
        (like(right), field, sums, bare, gram, gram, gram, gram),
        [
            pltpu.SMEM(ranks.shape, jnp.int32),
            pltpu.SMEM(freq_index.shape, jnp.int32),
            pltpu.VMEM(data.shape, BF16),
            pltpu.VMEM(left.shape, BF16),
            pltpu.SemaphoreType.DMA((5,)),
        ],
    )
    b0 = exchange(out)
    g0, m0, out = step(column0, (b0, vhi, vlo), (field, sums, message))
    c0 = exchange(out)
    n0, out = step(row0, (c0, uhi, ulo, back), (sums, message))
    b1 = exchange(out)
    g1, m1, out = step(column1, (b1, b0, vhi, vlo, g0, n0), (field, sums, message))
    c1 = exchange(out)
    n1, out = step(row1, (c1, c0, uhi, ulo, back), (sums, message))
    b2 = exchange(out)
    m2, out = step(
        column2, (b2, b0, b1, vhi, vlo, g0, g1, damp, m0, n0, m1, n1), (sums, message)
    )
    c2 = exchange(out)
    args = (here, c2, c0, c1, uhi, ulo, back, damp, m1, m2)
    (out,) = call(
        lambda rank, *refs: row2(rank, share, *refs), [SMEM] + [VMEM] * 9, args,
        (jax.ShapeDtypeStruct((nfreq * ntile, height, s), F32),),
        [pltpu.VMEM((max(16, ntile * share), s), F32)],
    )
    everyone = lax.all_to_all(out, ("freq", "tcol"), 0, 0, tiled=True)
    shape = jax.ShapeDtypeStruct(data.shape, F32)
    wave, res = call(
        lambda rank, *refs: finish_kernel(rank, nfreq, share, *refs),
        [SMEM, HBM, HBM] + [VMEM] * 8,
        (mine, data, left, everyone, vright, b0, b1, b2, c0, c1, c2), (shape, shape),
        [
            pltpu.VMEM((LATE + EARLY, nfreq, s), F32),
            pltpu.VMEM((6, nfreq, s), F32),
            pltpu.VMEM(shape.shape, F32),
            pltpu.VMEM(shape.shape, F32),
            pltpu.VMEM(data.shape, BF16),
            pltpu.VMEM(left.shape, BF16),
            pltpu.SemaphoreType.DMA((4,)),
        ],
        HBM,
    )
    return wave[None], res[None]


def solution(mesh):
    in_specs = (
        P("freq", None, "tcol", None),
        P("freq", None, "tcol", None),
        P("freq", None, "tcol", None),
        P("freq", None, None),
        P("freq"),
    )
    out_specs = (P("freq", None, "tcol", None), P("freq", None, "tcol", None))
    return jax.shard_map(body, mesh=mesh, in_specs=in_specs, out_specs=out_specs, check_vma=False)
```

```python
import functools

import jax
import jax.numpy as jnp
from jax import lax
from jax.experimental import pallas as pl
from jax.experimental.pallas import tpu as pltpu
from jax.sharding import PartitionSpec as P


RIDE = 16
LATE = 4
EARLY = 9
VMEM = pl.BlockSpec(memory_space=pltpu.VMEM)
SMEM = pl.BlockSpec(memory_space=pltpu.SMEM)
HBM = pl.BlockSpec(memory_space=pltpu.HBM)
F32 = jnp.float32
BF16 = jnp.bfloat16


def dot(a, b):
    return jnp.dot(a, b, preferred_element_type=F32)


def dot_t(a, b):
    return lax.dot_general(a, b, (((0,), (0,)), ((), ())), preferred_element_type=F32)


def side(real, imag):
    return jnp.concatenate([real, imag], axis=1)


def split(value):
    high = value.astype(BF16)
    return high, (value - high.astype(F32)).astype(BF16)


def unpack(ref, rank):
    n = ref.shape[0]
    real = ref[:, 0:rank, :].reshape(n * rank, ref.shape[2])
    imag = ref[:, rank : 2 * rank, :].reshape(n * rank, ref.shape[2])
    return real, imag


def fields(ref, rank):
    return side(*unpack(ref, rank)).astype(F32)


def send(out_ref, value, rank):
    s = out_ref.shape[2]
    for p in range(out_ref.shape[0]):
        rows = value[p * rank : (p + 1) * rank].astype(BF16)
        out_ref[p, 0:rank, :] = rows[:, :s]
        out_ref[p, rank : 2 * rank, :] = rows[:, s:]


def ride(out_ref, rows, rank):
    rows = rows + [jnp.zeros_like(rows[0])] * (RIDE - len(rows))
    block = jnp.concatenate(rows, axis=0).astype(BF16)
    for p in range(out_ref.shape[0]):
        out_ref[p, 2 * rank : 2 * rank + RIDE, :] = block


def ridden(ref, rank):
    total = ref[0, 2 * rank : 2 * rank + RIDE, :].astype(F32)
    for p in range(1, ref.shape[0]):
        total = total + ref[p, 2 * rank : 2 * rank + RIDE, :].astype(F32)
    return total


def inner(a, b):
    both = jnp.sum(a * b, axis=0, keepdims=True)
    s = both.shape[1] // 2
    return both[:, :s] + both[:, s:]


def twice(row):
    return jnp.concatenate([row, row], axis=1)


def ratio(top, bottom):
    safe = bottom > 0
    return jnp.where(safe, top / jnp.where(safe, bottom, 1.0), 0.0)


def apply_gram(hi_ref, lo_ref, real, imag):
    vector = jnp.concatenate([side(real, imag), side(-imag, real)], axis=0)
    return dot(hi_ref[...], vector) + dot(lo_ref[...], vector)


def make_gram(factor_ref, hi_ref, lo_ref, limits):
    real, imag = factor_ref[0], factor_ref[1]
    width = real.shape[1]
    rank = width // len(limits)
    level = lax.broadcasted_iota(jnp.int32, (rank, width), 0)

    def put(value, place):
        for p, limit in enumerate(limits):
            rows = slice(p * rank, (p + 1) * rank)
            high, low = split(jnp.where(level < limit, value[rows], 0.0))
            hi_ref[rows, place : place + width] = high
            lo_ref[rows, place : place + width] = low

    put(dot_t(real, real) + dot_t(imag, imag), 0)
    put(dot_t(real, imag) - dot_t(imag, real), width)


def start_kernel(
    rank, here_ref, mine_ref, ranks_hbm, freq_hbm, data_hbm, left_hbm, right_hbm,
    right_ref, back_ref, sums_ref, out_ref, uhi_ref, ulo_ref, vhi_ref, vlo_ref,
    ranks_ref, freq_ref, data_ref, left_ref, sem
):
    n = out_ref.shape[0]
    s = out_ref.shape[2]
    pairs = [
        (left_hbm, left_ref), (data_hbm, data_ref), (ranks_hbm, ranks_ref),
        (freq_hbm, freq_ref), (right_hbm, right_ref),
    ]
    copies = [
        pltpu.make_async_copy(source, target, sem.at[k])
        for k, (source, target) in enumerate(pairs)
    ]
    for copy in copies:
        copy.start()
    for copy in copies[:4]:
        copy.wait()
    here = here_ref[0]
    row_limits = [ranks_ref[here, p] for p in range(n)]
    column_limits = [ranks_ref[p, here] for p in range(n)]
    damping = 0.1 + 0.9 * freq_ref[0].astype(F32) / 229.0
    sums_ref[...] = jnp.full(sums_ref.shape, damping)
    real, imag = data_ref[0], data_ref[1]
    back = dot_t(left_ref[0], side(real, imag)) + dot_t(left_ref[1], side(imag, -real))
    level = lax.broadcasted_iota(jnp.int32, (rank, 2 * s), 0)
    back = jnp.concatenate(
        [
            jnp.where(level < limit, back[p * rank : (p + 1) * rank], 0.0)
            for p, limit in enumerate(row_limits)
        ],
        axis=0,
    )
    back_ref[...] = back
    send(out_ref, back, rank)
    make_gram(left_ref, uhi_ref, ulo_ref, row_limits)
    copies[4].wait()
    make_gram(right_ref, vhi_ref, vlo_ref, column_limits)


def column0(rank, b0_ref, hi_ref, lo_ref, g0_ref, sums_ref, out_ref):
    real, imag = unpack(b0_ref, rank)
    g0 = apply_gram(hi_ref, lo_ref, real, imag)
    g0_ref[...] = g0
    m00 = inner(side(real, imag).astype(F32), g0)
    sums_ref[0:1, :] = m00
    send(out_ref, g0, rank)
    ride(out_ref, [m00], rank)


def row0(rank, c0_ref, hi_ref, lo_ref, back_ref, sums_ref, out_ref):
    real, imag = unpack(c0_ref, rank)
    next0 = apply_gram(hi_ref, lo_ref, real, imag)
    c0 = side(real, imag).astype(F32)
    n00 = inner(c0, next0)
    sums_ref[0:1, :] = n00
    sums_ref[1:2, :] = inner(back_ref[...], c0)
    sums_ref[2:3, :] = ridden(c0_ref, rank)[0:1]
    send(out_ref, next0, rank)
    ride(out_ref, [n00], rank)


def column1(
    rank, b1_ref, b0_ref, hi_ref, lo_ref, g0_ref, n0_ref, g1_ref, sums_ref, out_ref
):
    real, imag = unpack(b1_ref, rank)
    theta0 = ratio(ridden(b1_ref, rank)[0:1], n0_ref[2:3, :])
    wide = twice(theta0)
    g1 = apply_gram(hi_ref, lo_ref, real, imag) - wide * g0_ref[...]
    b0 = fields(b0_ref, rank)
    b1 = side(real, imag).astype(F32) - wide * b0
    g1_ref[...] = g1
    m11 = inner(b1, g1)
    sums_ref[0:1, :] = m11
    sums_ref[1:2, :] = inner(b0, g1)
    sums_ref[2:3, :] = theta0
    send(out_ref, g1, rank)
    ride(out_ref, [m11], rank)


def row1(rank, c1_ref, c0_ref, hi_ref, lo_ref, back_ref, sums_ref, out_ref):
    real, imag = unpack(c1_ref, rank)
    next1 = apply_gram(hi_ref, lo_ref, real, imag)
    c1 = side(real, imag).astype(F32)
    n11 = inner(c1, next1)
    n01 = inner(fields(c0_ref, rank), next1)
    sums_ref[0:1, :] = n11
    sums_ref[1:2, :] = n01
    sums_ref[2:3, :] = inner(back_ref[...], c1)
    sums_ref[3:4, :] = ridden(c1_ref, rank)[0:1]
    send(out_ref, next1, rank)
    ride(out_ref, [n11, n01], rank)


def column2(
    rank, b2_ref, b0_ref, b1_ref, hi_ref, lo_ref, g0_ref, g1_ref,
    damp_ref, m0_ref, n0_ref, m1_ref, n1_ref, sums_ref, out_ref
):
    real, imag = unpack(b2_ref, rank)
    came = ridden(b2_ref, rank)
    theta1 = ratio(came[0:1], n1_ref[3:4, :])
    phi = ratio(came[1:2], n0_ref[2:3, :])
    wide1, wide0 = twice(theta1), twice(phi)
    g2 = apply_gram(hi_ref, lo_ref, real, imag) - wide1 * g1_ref[...] - wide0 * g0_ref[...]
    send(out_ref, g2, rank)
    b0 = fields(b0_ref, rank)
    b1 = fields(b1_ref, rank) - twice(m1_ref[2:3, :]) * b0
    b2 = side(real, imag).astype(F32) - wide1 * b1 - wide0 * b0
    sums_ref[0:1, :] = inner(b0, g2)
    sums_ref[1:2, :] = inner(b1, g2)
    sums_ref[2:3, :] = inner(b2, g2)
    sums_ref[3:4, :] = theta1
    sums_ref[4:5, :] = phi
    damping = damp_ref[0:1, :]
    known = [
        n0_ref[0:1, :] + damping * m0_ref[0:1, :],
        n1_ref[1:2, :] + damping * m1_ref[1:2, :],
        n1_ref[0:1, :] + damping * m1_ref[0:1, :],
        n0_ref[1:2, :],
        n1_ref[2:3, :],
    ]
    rest = [row - row.astype(BF16).astype(F32) for row in known]
    ride(out_ref, known + rest, rank)


def row2(
    rank, share, here_ref, c2_ref, c0_ref, c1_ref, hi_ref, lo_ref, back_ref,
    damp_ref, m1_ref, m2_ref, out_ref, table_ref
):
    real, imag = unpack(c2_ref, rank)
    next2 = apply_gram(hi_ref, lo_ref, real, imag)
    damping = damp_ref[0:1, :]
    came = ridden(c2_ref, rank)
    table_ref[0:5, :] = came[0:5] + came[5:10]
    table_ref[5:6, :] = m1_ref[2:3, :]
    table_ref[6:8, :] = m2_ref[3:5, :]
    table_ref[8:9, :] = damping
    rows = [
        inner(fields(c0_ref, rank), next2) + damping * m2_ref[0:1, :],
        inner(fields(c1_ref, rank), next2) + damping * m2_ref[1:2, :],
        inner(side(real, imag).astype(F32), next2) + damping * m2_ref[2:3, :],
        inner(back_ref[...], side(real, imag).astype(F32)),
        table_ref[pl.ds(here_ref[0] * share, share), :],
    ]
    more = out_ref.shape[1] - LATE - share
    if more:
        rows.append(jnp.zeros((more, real.shape[1]), F32))
    block = jnp.concatenate(rows, axis=0)
    for p in range(out_ref.shape[0]):
        out_ref[p] = block


def forms(h, u, g, p, position, size, axis):
    def times(v):
        return [sum(h[a][b] * v[b] for b in range(size)) for a in range(size)]

    def along(a, b):
        return jnp.sum(sum(x * y for x, y in zip(a, b)), axis=axis, keepdims=True)

    hg, hp, hx = times(g), times(p), times(position)
    rest = [u[a] - hx[a] for a in range(size)]
    return along(g, hg), along(p, hg), along(p, hp), along(g, rest), along(p, rest)


def descend(h, u, theta0, theta1, phi, damping, axis):
    one = jnp.ones_like(theta0)
    a11 = jnp.sum(h[0][0], axis=axis, keepdims=True)
    b1 = jnp.sum(u[0], axis=axis, keepdims=True)
    alpha = b1 / (1.1 * a11)
    p = [alpha * one]
    x = [alpha * one]
    for size in (2, 3):
        zero = jnp.zeros_like(one)
        x = x + [zero]
        p = p + [zero]
        if size == 2:
            g = [one - (theta0 + damping) * x[0], -x[0]]
        else:
            g = [
                one - (theta0 + damping) * x[0] - phi * x[1],
                -x[0] - (theta1 + damping) * x[1],
                -x[1],
            ]
        a11, a12, a22, b1, b2 = forms(h, u, g, p, x, size, axis)
        first, second = 1.1 * a11, 1.1 * a22
        determinant = first * second - a12 * a12
        alpha = (b1 * second - a12 * b2) / determinant
        beta = (first * b2 - a12 * b1) / determinant
        p = [alpha * g[a] + beta * p[a] for a in range(size)]
        x = [x[a] + p[a] for a in range(size)]
    return x


def finish_kernel(
    rank, nfreq, share, mine_ref, data_hbm, left_hbm, recv_ref, right_ref,
    b0_ref, b1_ref, b2_ref, c0_ref, c1_ref, c2_ref, wave_hbm, res_hbm,
    table_ref, mix_ref, wave_ref, res_ref, data_ref, left_ref, sem
):
    left_copy = pltpu.make_async_copy(left_hbm, left_ref, sem.at[2])
    data_copy = pltpu.make_async_copy(data_hbm, data_ref, sem.at[3])
    left_copy.start()
    data_copy.start()
    ntile = recv_ref.shape[0] // nfreq
    for f in range(nfreq):
        total = recv_ref[f * ntile]
        for t in range(1, ntile):
            total = total + recv_ref[f * ntile + t]
        table_ref[0:LATE, f, :] = total[0:LATE]
        for q in range(EARLY):
            place = LATE + q % share
            table_ref[LATE + q, f : f + 1, :] = recv_ref[f * ntile + q // share, place : place + 1]
    h = [[None] * 3 for _ in range(3)]
    places = [(0, 0, 2), (1, 1, 2), (2, 2, 2), (4, 0, 0), (5, 0, 1), (6, 1, 1)]
    for place, a, b in places:
        h[a][b] = h[b][a] = table_ref[place]
    u = [table_ref[7], table_ref[8], table_ref[3]]
    theta0, theta1, phi, damping = [table_ref[9 + a] for a in range(4)]
    x = descend(h, u, theta0, theta1, phi, damping, 0)
    mix_ref[0] = x[0] - theta0 * x[1] + (theta0 * theta1 - phi) * x[2]
    mix_ref[1] = x[1] - theta1 * x[2]
    mix_ref[2] = x[2]
    mix_ref[3] = x[0]
    mix_ref[4] = x[1]
    mix_ref[5] = x[2]
    row = pl.ds(mine_ref[0], 1)

    def combine(refs, offset):
        total = None
        for k, ref in enumerate(refs):
            scale = mix_ref[offset + k, row, :]
            real, imag = unpack(ref, rank)
            term = (scale * real.astype(F32), scale * imag.astype(F32))
            total = term if total is None else (total[0] + term[0], total[1] + term[1])
        return total

    def plain(factor_ref, real, imag):
        (rh, rl), (ih, il) = split(real), split(imag)
        first, second = factor_ref[0], factor_ref[1]
        return (
            dot(first, side(rh, ih)) + dot(second, side(-ih, rh))
            + dot(first, side(rl, il)) + dot(second, side(-il, rl))
        )

    s = wave_ref.shape[2]
    wave = plain(right_ref, *combine([b0_ref, b1_ref, b2_ref], 0))
    wave_ref[0] = wave[:, :s]
    wave_ref[1] = wave[:, s:]
    wave_copy = pltpu.make_async_copy(wave_ref, wave_hbm, sem.at[0])
    wave_copy.start()
    mixed = combine([c0_ref, c1_ref, c2_ref], 3)
    left_copy.wait()
    data_copy.wait()
    image = plain(left_ref, *mixed)
    res_ref[0] = data_ref[0].astype(F32) - image[:, :s]
    res_ref[1] = data_ref[1].astype(F32) - image[:, s:]
    res_copy = pltpu.make_async_copy(res_ref, res_hbm, sem.at[1])
    res_copy.start()
    wave_copy.wait()
    res_copy.wait()


def lane_limits(limits, rank, width):
    lane = lax.broadcasted_iota(jnp.int32, (1, width), 1)
    limit = jnp.zeros((1, width), jnp.int32)
    for p, value in enumerate(limits):
        limit = jnp.where(lane >= p * rank, value, limit)
    return (lax.rem(lane, rank) < limit).astype(F32)


def packed_gram(real, imag):
    width = real.shape[1]
    both = jnp.concatenate([real, imag], axis=0)
    upper = dot_t(both, both)
    lower = dot_t(real, imag) - dot_t(imag, real)
    row = lax.broadcasted_iota(jnp.int32, (width, width), 0)
    column = lax.broadcasted_iota(jnp.int32, (width, width), 1)
    return jnp.where(row <= column, upper, lower).astype(BF16)


def unpacked_gram(packed):
    width = packed.shape[1]
    here = packed.astype(F32)
    there = here.T
    row = lax.broadcasted_iota(jnp.int32, (width, width), 0)
    column = lax.broadcasted_iota(jnp.int32, (width, width), 1)
    real = jnp.where(row <= column, here, there)
    imag = jnp.where(row > column, here, jnp.where(row < column, -there, 0.0))
    return real.astype(BF16), imag.astype(BF16)


def direct_offsets(half):
    others = [k for k in range(1, half) if k != 2]
    return sorted(others, key=lambda k: (min(k, half - k), k))


def start_left(rank, n, here_ref, mine_ref, ranks_hbm, data_hbm, left_hbm, right_hbm, *refs):
    keep_ref, right_ref, ranks_ref, data_ref, left_ref, back_ref, sem = refs[-7:]
    half = n // 2
    direct = [0] + direct_offsets(half)
    packets, small, own = refs[: half - 1], refs[half - 1 : half + 1], refs[half + 1]
    pairs = [
        (left_hbm, left_ref), (data_hbm, data_ref), (ranks_hbm, ranks_ref),
        (right_hbm, right_ref),
    ]
    copies = [
        pltpu.make_async_copy(source, target, sem.at[k])
        for k, (source, target) in enumerate(pairs)
    ]
    for copy in copies:
        copy.start()
    for copy in copies[:3]:
        copy.wait()
    width = left_ref.shape[2]
    s = data_ref.shape[2]
    q = s // n
    here = here_ref[0]
    keep = lane_limits([ranks_ref[here, p] for p in range(n)], rank, width).astype(BF16)
    real, imag = left_ref[0] * keep, left_ref[1] * keep
    both = side(data_ref[0], data_ref[1])
    first, second = dot_t(both, real), dot_t(both, imag)
    back_ref[0] = (first[:s] + second[s:]).astype(BF16)
    back_ref[1] = (first[s:] - second[:s]).astype(BF16)
    gram = packed_gram(real, imag)
    for packet in packets:
        packet[0:width, :] = gram
    z, x = lax.div(here, 2), lax.rem(here, 2)
    for k in range(half):
        base = 2 * lax.rem(z + k, half)
        for block, target in enumerate([base + 1 - x, base + x]):
            rows = pl.ds(pl.multiple_of(target * q, q), q)
            if k == 2:
                out, place = small[block], 0
            elif k == 0 and block == 1:
                out, place = own, 0
            else:
                out, place = packets[direct.index(k)], width + 2 * q * block
            out[place : place + q, :] = back_ref[0, rows, :]
            out[place + q : place + 2 * q, :] = back_ref[1, rows, :]
    keep = lane_limits([ranks_ref[p, here] for p in range(n)], rank, width)
    keep_ref[...] = jnp.broadcast_to(keep, keep_ref.shape)
    copies[3].wait()


def start_right(right_ref, keep_ref, out_ref):
    keep = keep_ref[0:1, :].astype(BF16)
    out_ref[...] = packed_gram(right_ref[0] * keep, right_ref[1] * keep)


def swap_tiles(rank, source, target):
    n, rows, width = source.shape
    per = 128 // rank
    lane = lax.div(lax.broadcasted_iota(jnp.int32, (rows, 128), 1), rank)
    for g in range(n // per):
        for h in range(width // 128):
            ins = [source[per * g + a, :, 128 * h : 128 * h + 128] for a in range(per)]
            for b in range(per):
                out = None
                for a in range(per):
                    shift = (a - b) * rank % 128
                    piece = pltpu.roll(ins[a], shift, 1) if shift else ins[a]
                    out = piece if out is None else jnp.where(lane == a, piece, out)
                target[per * h + b, :, 128 * g : 128 * g + 128] = out


def apply_tiles(gram_ref, source, target):
    n, rows, _ = source.shape
    q = rows // 2
    for j in range(n):
        high, low = split(source[j])
        vector = jnp.concatenate([high, low], axis=0)
        real, imag = dot(vector, gram_ref[0, j]), dot(vector, gram_ref[1, j])
        real = real[:rows] + real[rows:]
        imag = imag[:rows] + imag[rows:]
        target[j, 0:q, :] = real[:q] + imag[q:]
        target[j, q:rows, :] = real[q:] - imag[:q]


def inner_tiles(first, second):
    n, rows, _ = first.shape
    total = first[0] * second[0]
    for j in range(1, n):
        total = total + first[j] * second[j]
    total = jnp.sum(total, axis=1, keepdims=True)
    return total[: rows // 2] + total[rows // 2 :]


def take_off(target, terms):
    scales = [jnp.concatenate([scale, scale], axis=0) for scale, _ in terms]
    for j in range(target.shape[0]):
        value = target[j]
        for scale, (_, other) in zip(scales, terms):
            value = value - scale * other[j]
        target[j] = value


def chain_kernel(
    rank, n, here_ref, freq_ref, *refs
):
    half = n // 2
    order = [0] + direct_offsets(half) + [2]
    lefts = [refs[:half], refs[half:n]]
    rights = [refs[n : n + half], refs[n + half : 2 * n]]
    small, own = refs[2 * n : 2 * n + 2], refs[2 * n + 2]
    b_ref, c_ref, stats_ref, left_ref, right_ref, one_ref, two_ref = refs[2 * n + 3 :]
    width = refs[0].shape[1]
    q = stats_ref.shape[0]
    here = here_ref[0]
    z, x = lax.div(here, 2), lax.rem(here, 2)
    for k in range(half):
        base = 2 * lax.rem(z + half - k, half)
        for other in range(2):
            ref = lefts[other][order.index(k)]
            at = pl.ds(base + (1 - x if other else x), 1)
            grams = (ref[0:width, :], rights[other][order.index(k)][...])
            for packed, gram_ref in zip(grams, (left_ref, right_ref)):
                real, imag = unpacked_gram(packed)
                gram_ref[0, at] = real[None]
                gram_ref[1, at] = imag[None]
            start = width + (0 if other else 2 * q)
            if k == 2:
                block = small[1 - other][...]
            elif k == 0 and not other:
                block = own[...]
            else:
                block = ref[start : start + 2 * q, :]
            one_ref[at] = block.astype(F32)[None]
    b0, b1, b2 = b_ref.at[0], b_ref.at[1], b_ref.at[2]
    c0, c1, c2 = c_ref.at[0], c_ref.at[1], c_ref.at[2]
    swap_tiles(rank, one_ref, b0)
    apply_tiles(right_ref, b0, two_ref)
    m00 = inner_tiles(b0, two_ref)
    swap_tiles(rank, two_ref, c0)
    apply_tiles(left_ref, c0, one_ref)
    n00 = inner_tiles(c0, one_ref)
    theta0 = ratio(n00, m00)
    swap_tiles(rank, one_ref, b1)
    take_off(b1, [(theta0, b0)])
    apply_tiles(right_ref, b1, two_ref)
    m11 = inner_tiles(b1, two_ref)
    m01 = inner_tiles(b0, two_ref)
    swap_tiles(rank, two_ref, c1)
    apply_tiles(left_ref, c1, one_ref)
    n11 = inner_tiles(c1, one_ref)
    n01 = inner_tiles(c0, one_ref)
    theta1 = ratio(n11, m11)
    phi = ratio(n01, m00)
    swap_tiles(rank, one_ref, b2)
    take_off(b2, [(theta1, b1), (phi, b0)])
    apply_tiles(right_ref, b2, two_ref)
    m02 = inner_tiles(b0, two_ref)
    m12 = inner_tiles(b1, two_ref)
    m22 = inner_tiles(b2, two_ref)
    swap_tiles(rank, two_ref, c2)
    apply_tiles(left_ref, c2, one_ref)
    n02 = inner_tiles(c0, one_ref)
    n12 = inner_tiles(c1, one_ref)
    n22 = inner_tiles(c2, one_ref)
    damping = 0.1 + 0.9 * freq_ref[0].astype(F32) / 229.0
    values = [
        n00 + damping * m00, n01 + damping * m01, n02 + damping * m02,
        n11 + damping * m11, n12 + damping * m12, n22 + damping * m22,
        m00, m01, m02, theta0, theta1, phi,
    ]
    lane = lax.broadcasted_iota(jnp.int32, stats_ref.shape, 1)
    block = jnp.full(stats_ref.shape, damping)
    for place, value in enumerate(values):
        block = jnp.where(lane == place, value, block)
    stats_ref[...] = block


def mix_kernel(stats_refs, b_ref, c_ref, out_ref):
    blocks = [ref[...] for ref in stats_refs]
    lane = lax.broadcasted_iota(jnp.int32, blocks[0].shape, 1)
    where_f = [lane == f for f in range(len(blocks))]

    def pick(place):
        value = jnp.zeros_like(blocks[0])
        for f, block in enumerate(blocks):
            shift = (f - place) % 128
            value = jnp.where(where_f[f], pltpu.roll(block, shift, 1) if shift else block, value)
        return value

    h = [[None] * 3 for _ in range(3)]
    for place, (a, b) in enumerate([(0, 0), (0, 1), (0, 2), (1, 1), (1, 2), (2, 2)]):
        h[a][b] = h[b][a] = pick(place)
    u = [pick(6), pick(7), pick(8)]
    theta0, theta1, phi, damping = pick(9), pick(10), pick(11), pick(12)
    x = descend(h, u, theta0, theta1, phi, damping, 1)
    n, rows, _ = b_ref.shape[1:]
    scales = []
    for value in x:
        own = jnp.sum(jnp.where(lane == 0, value, 0.0), axis=1, keepdims=True)
        scales.append(jnp.concatenate([own, own], axis=0))
    for j in range(n):
        for place, ref in enumerate((b_ref, c_ref)):
            value = scales[0] * ref[0, j] + scales[1] * ref[1, j] + scales[2] * ref[2, j]
            out_ref[j, place * rows : (place + 1) * rows, :] = value.astype(BF16)


def home_mix(nfreq, data_hbm, left_hbm, right_hbm, *refs):
    stats_refs = refs[:nfreq]
    b_ref, c_ref, out_ref, data_ref, left_ref, right_ref, sem = refs[nfreq:]
    pairs = [(right_hbm, right_ref), (left_hbm, left_ref), (data_hbm, data_ref)]
    copies = [
        pltpu.make_async_copy(source, target, sem.at[k])
        for k, (source, target) in enumerate(pairs)
    ]
    for copy in copies:
        copy.start()
    mix_kernel(stats_refs, b_ref, c_ref, out_ref)
    for copy in copies:
        copy.wait()


def dot_nt(a, b):
    return lax.dot_general(a, b, (((1,), (1,)), ((), ())), preferred_element_type=F32)


def home_kernel(
    recv_ref, data_ref, left_ref, right_ref, wave_hbm, res_hbm, wave_ref, res_ref, sem
):
    n, rows, width = recv_ref.shape
    q = rows // 4
    s = n * q

    def plain(factor_ref, place):
        real = recv_ref[:, place * q : (place + 1) * q, :].reshape(s, width)
        imag = recv_ref[:, (place + 1) * q : (place + 2) * q, :].reshape(s, width)
        both = jnp.concatenate([real, imag], axis=0)
        first, second = dot_nt(factor_ref[0], both), dot_nt(factor_ref[1], both)
        return first[:, :s] - second[:, s:], first[:, s:] + second[:, :s]

    wave_ref[0], wave_ref[1] = plain(right_ref, 0)
    wave_copy = pltpu.make_async_copy(wave_ref, wave_hbm, sem.at[0])
    wave_copy.start()
    real, imag = plain(left_ref, 2)
    res_ref[0] = data_ref[0].astype(F32) - real
    res_ref[1] = data_ref[1].astype(F32) - imag
    res_copy = pltpu.make_async_copy(res_ref, res_hbm, sem.at[1])
    res_copy.start()
    wave_copy.wait()
    res_copy.wait()


def by_source(data, left, right, ranks, freq_index, ntile, nfreq, here, mine):
    width = left.shape[2]
    rank = width // ntile
    s = data.shape[2]
    q = s // ntile
    half = ntile // 2
    room = (16 << 20) + 64 * width * width

    def like(value):
        return jax.ShapeDtypeStruct(value.shape, value.dtype)

    def call(kernel, specs, args, outs, scratch=(), target=VMEM):
        return pl.pallas_call(
            kernel,
            out_shape=outs,
            in_specs=specs,
            out_specs=[target] * len(outs),
            scratch_shapes=scratch,
            compiler_params=pltpu.CompilerParams(vmem_limit_bytes=room),
        )(*args)

    def along(shift, flip=0):
        return [
            (2 * z + x, 2 * ((z + shift) % half) + (x ^ flip))
            for z in range(half) for x in range(2)
        ]

    across = [(t, t ^ 1) for t in range(ntile)]
    sizes = [width + 2 * q] + [width + 4 * q] * (half - 2) + [2 * q] * 3
    direct = direct_offsets(half)
    parts = call(
        functools.partial(start_left, rank, ntile), [SMEM] * 2 + [HBM] * 4,
        (here, mine, ranks, data, left, right),
        [jax.ShapeDtypeStruct((size, width), BF16) for size in sizes]
        + [jax.ShapeDtypeStruct((8, width), F32), like(right)],
        [
            pltpu.SMEM(ranks.shape, jnp.int32),
            pltpu.VMEM(data.shape, BF16),
            pltpu.VMEM(left.shape, BF16),
            pltpu.VMEM((2, s, width), BF16),
            pltpu.SemaphoreType.DMA((4,)),
        ],
    )
    (gram,) = call(
        start_right, [VMEM] * 2, (parts[-1], parts[-2]),
        [jax.ShapeDtypeStruct((width, width), BF16)],
    )

    def hop(value, pairs):
        return lax.ppermute(value, "tcol", pairs)

    lefts, rights = [parts[0]], [gram]
    cross = [hop(parts[0], across), hop(gram, across)]
    for place, k in enumerate(direct):
        first, second = parts[1 + place], gram
        if place:
            first, _ = lax.optimization_barrier((first, lefts[-1]))
        lefts.append(hop(first, along(k)))
        rights.append(hop(second, along(k)))
    small = [hop(parts[half - block], along(2, block)) for block in (1, 0)]
    lefts.append(hop(lefts[1][:width], along(1)))
    rights.append(hop(rights[1], along(1)))
    other_lefts, other_rights = cross[:1], cross[1:]
    for place in range(1, half):
        other_lefts.append(hop(lefts[place], across))
        other_rights.append(hop(rights[place], across))
    packets = (*lefts, *other_lefts, *rights, *other_rights, *small, parts[half + 1])
    vectors = jax.ShapeDtypeStruct((3, ntile, 2 * q, width), F32)
    grams = pltpu.VMEM((2, ntile, width, width), BF16)
    vector = pltpu.VMEM((ntile, 2 * q, width), F32)
    b, c, stats = call(
        functools.partial(chain_kernel, rank, ntile), [SMEM] * 2 + [VMEM] * len(packets),
        (here, freq_index, *packets),
        (vectors, vectors, jax.ShapeDtypeStruct((q, 128), F32)),
        [grams, grams, vector, vector],
    )
    gathered = [stats] + [
        lax.ppermute(stats, "freq", [(f, f ^ step) for f in range(nfreq)])
        for step in range(1, nfreq)
    ]
    out, data_in, left_in, right_in = call(
        functools.partial(home_mix, nfreq), [HBM] * 3 + [VMEM] * (nfreq + 2),
        (data, left, right, *gathered, b, c),
        (
            jax.ShapeDtypeStruct((ntile, 4 * q, width), BF16),
            like(data), like(left), like(right),
        ),
        [pltpu.SemaphoreType.DMA((3,))],
    )
    back = lax.all_to_all(out, "tcol", 0, 0, tiled=True)
    shape = jax.ShapeDtypeStruct(data.shape, F32)
    return call(
        home_kernel, [VMEM] * 4, (back, data_in, left_in, right_in),
        (shape, shape),
        [
            pltpu.VMEM(shape.shape, F32),
            pltpu.VMEM(shape.shape, F32),
            pltpu.SemaphoreType.DMA((2,)),
        ],
        HBM,
    )


def body(data, left_factor, right_factor, ranks, freq_index):
    ntile = lax.axis_size("tcol")
    nfreq = lax.axis_size("freq")
    here = lax.axis_index("tcol").reshape(1)
    mine = lax.axis_index("freq").reshape(1)
    data, left, right, ranks = data[0], left_factor[0], right_factor[0], ranks[0]
    data, left, right, ranks = [
        pltpu.with_memory_space_constraint(value, pltpu.HBM)
        for value in (data, left, right, ranks)
    ]
    width = left.shape[2]
    rank = width // ntile
    s = data.shape[2]
    fits = ntile % 2 == 0 and ntile >= 6 and s % (16 * ntile) == 0 and width % 128 == 0 and 128 % rank == 0
    if fits and nfreq & (nfreq - 1) == 0 and ntile * width * width <= 1 << 20:
        wave, res = by_source(data, left, right, ranks, freq_index, ntile, nfreq, here, mine)
        return wave[None], res[None]
    share = -(-EARLY // ntile)
    height = -(-(LATE + share) // 8) * 8
    field = jax.ShapeDtypeStruct((width, 2 * s), F32)
    sums = jax.ShapeDtypeStruct((8, s), F32)
    bare = jax.ShapeDtypeStruct((ntile, 2 * rank, s), BF16)
    message = jax.ShapeDtypeStruct((ntile, 2 * rank + RIDE, s), BF16)
    gram = jax.ShapeDtypeStruct((width, 2 * width), BF16)
    room = (8 << 20) + 24 * width * width

    def like(value):
        return jax.ShapeDtypeStruct(value.shape, value.dtype)

    def call(kernel, specs, args, outs, scratch=(), target=VMEM):
        return pl.pallas_call(
            functools.partial(kernel, rank),
            out_shape=outs,
            in_specs=specs,
            out_specs=[target] * len(outs),
            scratch_shapes=scratch,
            compiler_params=pltpu.CompilerParams(vmem_limit_bytes=room),
        )(*args)

    def step(kernel, args, outs):
        return call(kernel, [VMEM] * len(args), args, outs)

    def exchange(value):
        return lax.all_to_all(value, "tcol", 0, 0, tiled=True)

    vright, back, damp, out, uhi, ulo, vhi, vlo = call(
        start_kernel, [SMEM] * 2 + [HBM] * 5, (here, mine, ranks, freq_index, data, left, right),
        (like(right), field, sums, bare, gram, gram, gram, gram),
        [
            pltpu.SMEM(ranks.shape, jnp.int32),
            pltpu.SMEM(freq_index.shape, jnp.int32),
            pltpu.VMEM(data.shape, BF16),
            pltpu.VMEM(left.shape, BF16),
            pltpu.SemaphoreType.DMA((5,)),
        ],
    )
    b0 = exchange(out)
    g0, m0, out = step(column0, (b0, vhi, vlo), (field, sums, message))
    c0 = exchange(out)
    n0, out = step(row0, (c0, uhi, ulo, back), (sums, message))
    b1 = exchange(out)
    g1, m1, out = step(column1, (b1, b0, vhi, vlo, g0, n0), (field, sums, message))
    c1 = exchange(out)
    n1, out = step(row1, (c1, c0, uhi, ulo, back), (sums, message))
    b2 = exchange(out)
    m2, out = step(
        column2, (b2, b0, b1, vhi, vlo, g0, g1, damp, m0, n0, m1, n1), (sums, message)
    )
    c2 = exchange(out)
    args = (here, c2, c0, c1, uhi, ulo, back, damp, m1, m2)
    (out,) = call(
        lambda rank, *refs: row2(rank, share, *refs), [SMEM] + [VMEM] * 9, args,
        (jax.ShapeDtypeStruct((nfreq * ntile, height, s), F32),),
        [pltpu.VMEM((max(16, ntile * share), s), F32)],
    )
    everyone = lax.all_to_all(out, ("freq", "tcol"), 0, 0, tiled=True)
    shape = jax.ShapeDtypeStruct(data.shape, F32)
    wave, res = call(
        lambda rank, *refs: finish_kernel(rank, nfreq, share, *refs),
        [SMEM, HBM, HBM] + [VMEM] * 8,
        (mine, data, left, everyone, vright, b0, b1, b2, c0, c1, c2), (shape, shape),
        [
            pltpu.VMEM((LATE + EARLY, nfreq, s), F32),
            pltpu.VMEM((6, nfreq, s), F32),
            pltpu.VMEM(shape.shape, F32),
            pltpu.VMEM(shape.shape, F32),
            pltpu.VMEM(data.shape, BF16),
            pltpu.VMEM(left.shape, BF16),
            pltpu.SemaphoreType.DMA((4,)),
        ],
        HBM,
    )
    return wave[None], res[None]


def solution(mesh):
    in_specs = (
        P("freq", None, "tcol", None),
        P("freq", None, "tcol", None),
        P("freq", None, "tcol", None),
        P("freq", None, None),
        P("freq"),
    )
    out_specs = (P("freq", None, "tcol", None), P("freq", None, "tcol", None))
    return jax.shard_map(body, mesh=mesh, in_specs=in_specs, out_specs=out_specs, check_vma=False)
```
